128 devices in a mesh: lev: 4 (over z_hi, core), win: 32 (over x, z_lo, y).
Axes of the slice: x: 4, y: 4, z: 4 (z_hi: 2, z_lo: 2; z = z_hi * 2 + z_lo), core: 2. Of those that a mesh axis runs over, the one named last changes fastest.
Arguments:
- fields: bfloat16 [12, 36864, 512], P('lev', 'win'), may hold values from -6 to 6
- patch_order: int32 [36864], replicated, may hold values from 0 to 36863, as said below
- shift_offsets: int32 [2], replicated, may hold values from 1 to 11
- latent_query: bfloat16 [3, 512], replicated, may hold values from -72 to 72
- enc_kv: bfloat16 [512, 1024], replicated, may hold values from -0.25 to 0.25
- enc_out: bfloat16 [512, 512], replicated, may hold values from -0.25 to 0.25
- qkv_a: bfloat16 [512, 1536], replicated, may hold values from -1 to 10
- proj_a: bfloat16 [512, 512], replicated, may hold values from -0.25 to 0.25
- merge_w: bfloat16 [2048, 1024], replicated, may hold values from -0.125 to 0.125
- qkv_b: bfloat16 [1024, 3072], replicated, may hold values from -1 to 10
- proj_b: bfloat16 [1024, 1024], replicated, may hold values from -0.1875 to 0.1875
- expand_w: bfloat16 [1024, 2048], replicated, may hold values from -0.1875 to 0.1875
- qkv_c: bfloat16 [512, 1536], replicated, may hold values from -1 to 10
- proj_c: bfloat16 [512, 512], replicated, may hold values from -0.25 to 0.25
Outputs:
- result: bfloat16 [48, 768, 3, 512], P('lev', 'win')
The draws below stay inside these ranges and needn't reach their ends.
Inputs may be any that keep to these rules, and one draw needn't show every extreme that they name: `patch_order`: A permutation of the 36864 grid patches over the stored slots; the 1152 slots of each index of win hold exactly 9 patches of every pair of latitude band (12 rows) and longitude shard (24 columns), in no particular order.
All inputs are finite; a program needn't handle non-finite values.
Results may differ from the reference program's by a relative error of at most 0.015.
Values may be sent and summed in bfloat16 or wider, within the bound.
A program may use at most 256 MiB of HBM per device.

```python
import math
import jax
import jax.numpy as jnp
from jax import lax

D = 512
HEADS = 16
LATENT = 3
LEV_DEV = 3
WLAT = 6
WLON = 12
PLAT = 12
PLON = 24
LEVELS = 12
GLAT = 48
GLON = 768
PATCHES = 36864
PSH = 1152
N_LEV = 4
N_WIN = 32


def draw_patch_order(key, part):
    per_pair = PLAT * PLON
    shard_count = PATCHES // PSH
    band_count = PSH // per_pair
    kpair = per_pair // shard_count
    groups = band_count * shard_count
    first_key, second_key = jax.random.split(jax.random.fold_in(key, 7))

    def permute_pair(inner):
        return jax.random.permutation(inner, per_pair).astype(jnp.int32)

    def permute_shard(inner):
        return jax.random.permutation(inner, PSH).astype(jnp.int32)
    ranks = jax.vmap(permute_pair)(jax.random.split(first_key, groups))
    shuffle = jax.vmap(permute_shard)(jax.random.split(second_key, shard_count))
    group_ids = jnp.arange(groups, dtype=jnp.int32)[:, None]
    source = ranks // kpair
    local = group_ids * kpair + ranks % kpair
    slot = source * PSH + shuffle[source, local]
    within = jnp.arange(per_pair, dtype=jnp.int32)[None, :]
    band = group_ids // shard_count
    shard = group_ids % shard_count
    grid_id = (band * PLAT + within // PLON) * GLON + shard * PLON + within % PLON
    return jnp.zeros((PATCHES,), jnp.int32).at[slot.reshape(-1)].set(grid_id.reshape(-1))


def draw_latent_query(key, part):
    base = jax.random.normal(jax.random.fold_in(key, 11), (LATENT, D), jnp.float32)
    return jnp.clip(base, -6.0, 6.0).astype(jnp.bfloat16)


def window_projection(key, width):
    limit = 6.0 / width ** 0.5
    base = jnp.clip(jax.random.normal(key, (width, 3 * width), jnp.float32) / width ** 0.5, -limit, limit)
    return base.astype(jnp.bfloat16)


def draw_qkv_a(key, part):
    return window_projection(jax.random.fold_in(key, 21), D)


def draw_qkv_b(key, part):
    return window_projection(jax.random.fold_in(key, 22), 2 * D)


def draw_qkv_c(key, part):
    return window_projection(jax.random.fold_in(key, 23), D)


def block_scale(rng, extent, shards, low, high):
    def one(dim, shards_of):
        draws = jax.random.uniform(jax.random.fold_in(jax.random.fold_in(rng, 6), dim), (shards_of,), jnp.float32, low / len(shards), high / len(shards))
        return jnp.repeat(jnp.exp(draws), extent[dim] // shards_of).reshape((-1,) + (1,) * (len(extent) - dim - 1))

    level = one(*shards[0])
    for cut in shards[1:]:
        level = level * one(*cut)
    return level


def centred(key, extent, deviation, bound, cuts=(), held_as=jnp.bfloat16):
    loudness = block_scale(key, extent, cuts, -0.22, 0.18) if cuts else 1.0
    drawn = jax.random.normal(key, extent, jnp.float32) * deviation * loudness
    return jnp.minimum(jnp.maximum(drawn, -bound), bound).astype(held_as)


def setup_inputs(seed: int = 0) -> dict:
    key_list = jax.random.split(jax.random.key(seed), 15)
    return {
        "fields": centred(key_list[0], (LEVELS, PATCHES, D), 1.0, 6.0, ((0, 4), (1, 32))),
        "patch_order": draw_patch_order(jax.random.fold_in(key_list[14], 71), 0),
        "shift_offsets": jax.random.randint(key_list[2], (2,), 1, WLON).astype(jnp.int32),
        "latent_query": draw_latent_query(jax.random.fold_in(key_list[14], 71), 0),
        "enc_kv": centred(key_list[4], (D, 2 * D), D ** -0.5, 0.25),
        "enc_out": centred(key_list[5], (D, D), D ** -0.5, 0.25),
        "qkv_a": draw_qkv_a(jax.random.fold_in(key_list[14], 71), 0),
        "proj_a": centred(key_list[7], (D, D), D ** -0.5, 0.25),
        "merge_w": centred(key_list[8], (4 * D, 2 * D), (4 * D) ** -0.5, 0.125),
        "qkv_b": draw_qkv_b(jax.random.fold_in(key_list[14], 71), 0),
        "proj_b": centred(key_list[10], (2 * D, 2 * D), (2 * D) ** -0.5, 0.1875),
        "expand_w": centred(key_list[11], (2 * D, 4 * D), (2 * D) ** -0.5, 0.1875),
        "qkv_c": draw_qkv_c(jax.random.fold_in(key_list[14], 71), 0),
        "proj_c": centred(key_list[13], (D, D), D ** -0.5, 0.25),
    }


epsilon = 1e-05

def rounded(values):
    return lax.optimization_barrier(values.astype(jnp.bfloat16)).astype(jnp.float32)

def normalize(values):
    values = values.astype(jnp.float32)
    centre = lax.optimization_barrier(jnp.mean(values, axis=-1, keepdims=True))
    offsets = values - centre
    spread = lax.optimization_barrier(jnp.mean(offsets * offsets, axis=-1, keepdims=True))
    return offsets * lax.rsqrt(spread + epsilon)

def level_partials(tokens, latent_query, enc_kv):
    groups, depth, count, width = tokens.shape
    head_size = width // HEADS
    projected = rounded(jnp.einsum('glrd,de->glre', tokens.astype(jnp.float32), enc_kv.astype(jnp.float32)))
    keyed = projected[..., :width].reshape(groups, depth, count, HEADS, head_size)
    valued = projected[..., width:].reshape(groups, depth, count, HEADS, head_size)
    queries = latent_query.astype(jnp.float32).reshape(LATENT, HEADS, head_size)
    scores = jnp.einsum('glrhe,ahe->grahl', keyed, queries) / math.sqrt(head_size)
    peaks = lax.optimization_barrier(jnp.max(scores, axis=-1))
    weights = jnp.exp(scores - peaks[..., None])
    totals = lax.optimization_barrier(jnp.sum(weights, axis=-1))
    blended = jnp.einsum('grahl,glrhe->grahe', rounded(weights), valued) / totals[..., None]
    return (blended.reshape(groups, count, LATENT * width), peaks.reshape(groups, count, LATENT * HEADS), totals.reshape(groups, count, LATENT * HEADS))

def combine(blended, peaks, totals):
    groups, count = (peaks.shape[0], peaks.shape[1])
    highest = lax.optimization_barrier(jnp.max(peaks, axis=0))
    scale = totals * jnp.exp(peaks - highest[None])
    denominator = lax.optimization_barrier(jnp.sum(scale, axis=0))
    pieces = blended.reshape(groups, count, LATENT * HEADS, -1)
    numerator = lax.optimization_barrier(jnp.sum(scale[..., None] * pieces, axis=0))
    return (numerator / denominator[..., None]).reshape(count, LATENT, -1).astype(jnp.bfloat16)

def latent_tokens(encoded, latent_query, enc_out):
    count, width = (encoded.shape[0], encoded.shape[-1])
    projected = jnp.dot(encoded.reshape(count * LATENT, width), enc_out, preferred_element_type=jnp.float32)
    return (projected.reshape(count, LATENT, width) + latent_query.astype(jnp.float32)[None]).astype(jnp.bfloat16)

def to_windows(grid, tall, broad):
    rows, cols, levels, width = grid.shape
    blocks = grid.reshape(rows // tall, tall, cols // broad, broad, levels, width)
    return blocks.transpose(0, 2, 1, 3, 4, 5).reshape(-1, tall * broad * levels, width)

def from_windows(windows, rows, cols, tall, broad):
    width = windows.shape[-1]
    levels = windows.shape[1] // (tall * broad)
    blocks = windows.reshape(rows // tall, cols // broad, tall, broad, levels, width)
    return blocks.transpose(0, 2, 1, 3, 4, 5).reshape(rows, cols, levels, width)

def attend(windows, w_qkv, w_proj, head_count):
    count, length, width = windows.shape
    head_size = width // head_count
    normed = rounded(normalize(windows))
    projected = rounded(jnp.einsum('wte,ef->wtf', normed, w_qkv.astype(jnp.float32)))
    queries = projected[..., :width].reshape(count, length, head_count, head_size)
    keyed = projected[..., width:2 * width].reshape(count, length, head_count, head_size)
    valued = projected[..., 2 * width:].reshape(count, length, head_count, head_size)
    scores = jnp.einsum('wqhe,wkhe->whqk', queries, keyed) / math.sqrt(head_size)
    weights = jnp.exp(scores - lax.optimization_barrier(jnp.max(scores, axis=-1, keepdims=True)))
    weights = weights / lax.optimization_barrier(jnp.sum(weights, axis=-1, keepdims=True))
    blended = rounded(jnp.einsum('whqk,wkhe->wqhe', rounded(weights), valued)).reshape(count, length, width)
    output = jnp.einsum('wte,ef->wtf', blended, w_proj.astype(jnp.float32))
    return (windows.astype(jnp.float32) + output).astype(jnp.bfloat16)

def window_block(grid, w_qkv, w_proj, head_count):
    rows, cols = (grid.shape[0], grid.shape[1])
    windows = to_windows(grid, WLAT, WLON)
    banded = windows.reshape(rows // WLAT, -1, windows.shape[1], windows.shape[2])

    def one_band(band):
        return attend(band, w_qkv, w_proj, head_count)
    done = lax.map(one_band, banded)
    return from_windows(done.reshape(windows.shape), rows, cols, WLAT, WLON)

def rolled_block(grid, offset, w_qkv, w_proj, head_count):
    moved = window_block(jnp.roll(grid, -offset, axis=1), w_qkv, w_proj, head_count)
    return jnp.roll(moved, offset, axis=1)

def merge_down(grid, merge_w):
    rows, cols, levels, width = grid.shape
    groups = grid.reshape(rows // 2, 2, cols // 2, 2, levels, width).transpose(0, 2, 4, 1, 3, 5)
    normed = normalize(groups.reshape(-1, 4 * width)).astype(jnp.bfloat16)
    down = jnp.dot(normed, merge_w, preferred_element_type=jnp.float32).astype(jnp.bfloat16)
    return down.reshape(rows // 2, cols // 2, levels, 2 * width)

def expand_up(grid, expand_w, skip):
    rows, cols, levels, width = grid.shape
    normed = normalize(grid.reshape(-1, width)).astype(jnp.bfloat16)
    grown = jnp.dot(normed, expand_w, preferred_element_type=jnp.float32)
    grown = grown.reshape(rows, cols, levels, 2, 2, width // 2).transpose(0, 3, 1, 4, 2, 5)
    grown = grown.reshape(2 * rows, 2 * cols, levels, width // 2)
    return (grown + skip.astype(jnp.float32)).astype(jnp.bfloat16)

def reference(fields, patch_order, shift_offsets, latent_query, enc_kv, enc_out, qkv_a, proj_a, merge_w, qkv_b, proj_b, expand_w, qkv_c, proj_c):
    blocks = fields.reshape(N_LEV, LEV_DEV, N_WIN, PSH, D).transpose(2, 0, 1, 3, 4)

    def encode(tokens):
        blended, peaks, totals = level_partials(tokens, latent_query, enc_kv)
        return latent_tokens(combine(blended, peaks, totals), latent_query, enc_out)
    latents = lax.map(encode, blocks).reshape(PATCHES, LATENT, D)
    grid = jnp.zeros((PATCHES, LATENT, D), jnp.bfloat16).at[patch_order].set(latents)
    grid = grid.reshape(GLAT, GLON, LATENT, D)
    first = rolled_block(grid, shift_offsets[0], qkv_a, proj_a, HEADS)
    coarse = window_block(merge_down(first, merge_w), qkv_b, proj_b, 2 * HEADS)
    joined = expand_up(coarse, expand_w, first)
    return rolled_block(joined, shift_offsets[1], qkv_c, proj_c, HEADS)
```

```python
import functools
import math

import jax
import jax.numpy as jnp
import numpy as np
from jax import lax
from jax.experimental import pallas as pl
from jax.experimental.pallas import tpu as pltpu
from jax.sharding import PartitionSpec as P

D = 512
HEADS = 16
LATENT = 3
PLAT = 12
PLON = 24
N_LEV = 4
N_WIN = 32
PSH = 1152
PER = 9
MSG = 32
CHUNK = 144
epsilon = 1e-05
BF = jnp.bfloat16
F32 = jnp.float32
MESH = pl.DeviceIdType.MESH
FAR = -1.0e6
VMEM = pl.BlockSpec(memory_space=pltpu.VMEM)
SMEM = pl.BlockSpec(memory_space=pltpu.SMEM)
ANY = pl.BlockSpec(memory_space=pl.ANY)


def params(mib=60, **more):
    return pltpu.CompilerParams(vmem_limit_bytes=mib << 20, **more)


def dot(a, b):
    return jnp.dot(a, b, preferred_element_type=F32)


def dot_nt(a, b):
    return lax.dot_general(a, b, (((1,), (1,)), ((), ())), preferred_element_type=F32)


def iota(shape, axis):
    return lax.broadcasted_iota(jnp.int32, shape, axis).astype(F32)


def div(values, by):
    return jnp.floor((values + 0.5) * (1.0 / by))


def hot(condition):
    return jnp.where(condition, 1.0, 0.0).astype(BF)


def group_ids(first_column):
    ids = np.full((4, 56), FAR, np.float32)
    for sub in range(4):
        for q in range(54):
            column = first_column + 2 * (q // 18) + (sub & 1)
            ids[sub, q] = column * 36 + (2 * (q % 6) + (sub >> 1)) * 3 + q % 18 // 6
    return ids


def half_ids(band, first_column):
    ids = np.full((112,), 2 * FAR, np.float32)
    for q in range(108):
        ids[q] = (first_column + q // 18) * 36 + (band * 6 + q % 6) * 3 + q % 18 // 6
    return ids


def tables():
    spread = np.concatenate([group_ids(6 * g).reshape(-1) for g in range(-1, 5)])
    windows = np.concatenate(
        [np.concatenate([half_ids(b, 0), half_ids(b, 6)]) for _ in range(2) for b in range(2)]
    )
    held = np.zeros((8, 1344), np.float32)
    held[0] = np.concatenate(
        [windows]
        + [half_ids(b, 6 - PLON) for b in range(2)]
        + [half_ids(b, PLON) for b in range(2)]
    )
    held[1, :448] = 1.0
    by_sub = np.stack([group_ids(6 * g) for g in range(4)], axis=1).reshape(-1)
    final = np.zeros((PLAT, LATENT, PLON), np.float32)
    for r in range(PLAT):
        for a in range(LATENT):
            for c in range(PLON):
                final[r, a, c] = c * 36 + r * 3 + a
    return (
        jnp.asarray(spread[None]),
        jnp.asarray(windows[:, None]),
        jnp.asarray(held),
        jnp.asarray(by_sub[:, None]),
        jnp.asarray(final.reshape(-1, 1)),
    )


def sort_kernel(core_ref, slots_ref, x_ref, keep_ref, send_ref, meta_ref, perm):
    @pl.when(pl.program_id(0) == 0)
    def _():
        core = core_ref[0].astype(F32)
        p = slots_ref[...].astype(F32)
        row = div(p, 768.0)
        column = p - row * 768.0
        band = div(row, 12.0)
        shard = div(column, 24.0)
        row = row - band * 12.0
        column = column - shard * 24.0
        half = div(band, 2.0)
        other = jnp.abs(band - 2.0 * half - core)
        key = other * 64.0 + half * 32.0 + shard
        member = hot(iota((128, PSH), 0) == key)
        upper = hot(iota((128, 128), 0) < iota((128, 128), 1))
        seen = jnp.zeros((128, 1), F32)
        ranks = []
        for b in range(PSH // 128):
            piece = member[:, b * 128 : (b + 1) * 128]
            wide = piece.astype(F32)
            ranks.append(jnp.sum(wide * (dot(piece, upper) + seen), axis=0, keepdims=True))
            seen = seen + jnp.sum(wide, axis=1, keepdims=True)
        target = key * PER + jnp.concatenate(ranks, axis=1)
        for b in range(PSH // 128):
            perm[b * 128 : (b + 1) * 128, :] = hot(iota((128, PSH), 0) + b * 128.0 == target)
        j = div(column, 2.0)
        group = div(j, 3.0)
        i = div(row, 2.0)
        sub = 2.0 * (row - 2.0 * i) + column - 2.0 * j
        base = group * 224.0 + sub * 56.0 + (j - 3.0 * group) * 18.0 + i
        high = div(base, 16.0)
        low = base - 16.0 * high
        at = iota((128, PSH), 0)
        meta = jnp.where(at == 48.0, high, jnp.where(at == 49.0, low, 0.0)).astype(BF)
        meta_ref[...] = dot_nt(perm[0:576, :], meta).astype(BF)

    done = dot(perm[...], x_ref[0])
    keep_ref[0] = done[:576].astype(BF)
    send_ref[0] = done[576:].astype(BF)


def sort_fields(core, slots, fields):
    levels = fields.shape[0]
    return pl.pallas_call(
        sort_kernel,
        grid=(levels,),
        in_specs=[
            SMEM,
            pl.BlockSpec((1, PSH), lambda l: (0, 0)),
            pl.BlockSpec((1, PSH, D), lambda l: (l, 0, 0)),
        ],
        out_specs=[
            pl.BlockSpec((1, 576, D), lambda l: (l, 0, 0)),
            pl.BlockSpec((1, 576, D), lambda l: (l, 0, 0)),
            pl.BlockSpec((576, 128), lambda l: (0, 0)),
        ],
        out_shape=[
            jax.ShapeDtypeStruct((levels, 576, D), BF),
            jax.ShapeDtypeStruct((levels, 576, D), BF),
            jax.ShapeDtypeStruct((576, 128), BF),
        ],
        scratch_shapes=[pltpu.VMEM((PSH, PSH), BF)],
        compiler_params=params(),
        name="sort_fields",
    )(core, slots, fields)


def encode_kernel(own_ref, got_ref, meta_ref, kv_ref, query_ref, out_ref, score_w, spread_w, stat_w, pick, stack):
    @pl.when(pl.program_id(0) == 0)
    def _():
        c = iota((128, D), 0)
        lane = iota((128, D), 1)
        a = div(c, 16.0)
        q = query_ref[...].astype(F32)
        chosen = jnp.where(a == 0.0, q[0:1], jnp.where(a == 1.0, q[1:2], q[2:3]))
        mine = (c - 16.0 * a == div(lane, 32.0)) & (c < 48.0)
        heads = jnp.where(mine, chosen, 0.0).astype(BF)
        folded = dot_nt(kv_ref[:, :D], heads) * (1.0 / math.sqrt(D // HEADS))
        high = folded.astype(BF)
        score_w[:, 0:128] = high
        score_w[:, 128:256] = (folded - high.astype(F32)).astype(BF)
        for a in range(LATENT):
            spread_w[:, a * D : (a + 1) * D] = hot(c == 16.0 * a + div(lane, 32.0))
            s = iota((128, 128), 0)
            t = iota((128, 128), 1)
            t = t - 64.0 * div(t, 64.0)
            for piece in range(3):
                here = (t >= 16.0 * piece) & (t < 16.0 * piece + 16.0)
                stat_w[piece * 128 : (piece + 1) * 128, a * 128 : (a + 1) * 128] = hot(
                    here & (s == 16.0 * a + t - 16.0 * piece)
                )
            stat_w[384:512, a * 128 : (a + 1) * 128] = hot((t >= 48.0) & (t < 50.0) & (s == t))
        lane = iota((1, 6 * CHUNK), 1)
        kind = div(lane, float(CHUNK))
        slot = lane - kind * CHUNK
        stats = kind >= 3.0
        a = jnp.where(stats, kind - 3.0, kind)
        dest = div(slot, float(PER))
        k = a * PER + slot - dest * PER
        row = dest * MSG + jnp.where(stats, 27.0 + div(k, 8.0), k)
        for b in range(4):
            pick[b * 128 : (b + 1) * 128, :] = hot(iota((128, 6 * CHUNK), 0) + b * 128.0 == row)

    xs = [own_ref[l] for l in range(3)] + [got_ref[l] for l in range(3)]
    scores = []
    for x in xs:
        both = dot(x, score_w[...])
        scores.append(both[:, :128] + both[:, 128:])
    peak = functools.reduce(jnp.maximum, scores)
    weights = [jnp.exp(s - peak) for s in scores]
    total = functools.reduce(jnp.add, weights)
    mixes = [jnp.zeros((CHUNK, D), F32)] * LATENT
    for x, w in zip(xs, weights):
        value = dot(x, kv_ref[:, D:]).astype(BF).astype(F32)
        wide = dot((w / total).astype(BF), spread_w[...])
        mixes = [m + wide[:, a * D : (a + 1) * D] * value for a, m in enumerate(mixes)]
    logsum = peak + jnp.log(total)
    high = logsum.astype(BF)
    rest = logsum - high.astype(F32)
    middle = rest.astype(BF)
    low = (rest - middle.astype(F32)).astype(BF)
    stats = dot(jnp.concatenate([high, middle, low, meta_ref[...]], axis=1), stat_w[...])
    slot = iota((CHUNK, D), 0)
    rank = slot - PER * div(slot, float(PER))
    block = div(iota((CHUNK, D), 1), 64.0)
    for a in range(LATENT):
        stack[a * CHUNK : (a + 1) * CHUNK, :] = mixes[a].astype(BF)
        k = rank + PER * a
        tiled = jnp.concatenate([stats[:, a * 128 : (a + 1) * 128]] * 4, axis=1)
        stack[(3 + a) * CHUNK : (4 + a) * CHUNK, :] = jnp.where(
            block == k - 8.0 * div(k, 8.0), tiled, 0.0
        ).astype(BF)
    out_ref[...] = dot(pick[...], stack[...]).astype(BF)


def encode(own, got, meta, enc_kv, latent_query):
    return pl.pallas_call(
        encode_kernel,
        grid=(576 // CHUNK,),
        in_specs=[
            pl.BlockSpec((3, CHUNK, D), lambda i: (0, i, 0)),
            pl.BlockSpec((3, CHUNK, D), lambda i: (0, i, 0)),
            pl.BlockSpec((CHUNK, 128), lambda i: (i, 0)),
            VMEM,
            VMEM,
        ],
        out_specs=pl.BlockSpec((16 * MSG, D), lambda i: (i, 0)),
        out_shape=jax.ShapeDtypeStruct((64 * MSG, D), BF),
        scratch_shapes=[
            pltpu.VMEM((D, 256), BF),
            pltpu.VMEM((128, LATENT * D), BF),
            pltpu.VMEM((512, LATENT * 128), BF),
            pltpu.VMEM((16 * MSG, 6 * CHUNK), BF),
            pltpu.VMEM((6 * CHUNK, D), BF),
        ],
        compiler_params=params(),
        name="encode",
    )(own, got, meta, enc_kv, latent_query)


def swap_kernel(msg_ref, out_ref, send_sem, recv_sem, own_sem):
    lev = lax.axis_index("lev")
    win = lax.axis_index("win")
    core = lax.rem(lev, 2)
    me = (lev // 2) * N_WIN + win
    count = 2 * N_WIN

    def device(index):
        return ((index // N_WIN) * 2 + core, lax.rem(index, N_WIN))

    own = pltpu.make_async_copy(msg_ref.at[me], out_ref.at[me], own_sem)
    own.start()
    barrier = pltpu.get_barrier_semaphore()

    @pl.loop(1, count)
    def _(k):
        pl.semaphore_signal(
            barrier, inc=1, device_id=device(lax.rem(me + k, count)), device_id_type=MESH
        )

    pl.semaphore_wait(barrier, count - 1)

    def copy(k):
        dest = lax.rem(me + k, count)
        return pltpu.make_async_remote_copy(
            src_ref=msg_ref.at[dest],
            dst_ref=out_ref.at[me],
            send_sem=send_sem.at[k],
            recv_sem=recv_sem.at[k],
            device_id=device(dest),
            device_id_type=MESH,
        )

    @pl.loop(1, count)
    def _(k):
        copy(k).start()

    @pl.loop(1, count)
    def _(k):
        copy(k).wait()

    own.wait()


def swap(messages):
    return pl.pallas_call(
        swap_kernel,
        out_shape=jax.ShapeDtypeStruct((64, MSG, D), BF),
        in_specs=[ANY],
        out_specs=ANY,
        scratch_shapes=[
            pltpu.SemaphoreType.DMA((64,)),
            pltpu.SemaphoreType.DMA((64,)),
            pltpu.SemaphoreType.DMA,
        ],
        compiler_params=pltpu.CompilerParams(collective_id=0, has_side_effects=True),
        name="swap",
    )(messages)


def settle_kernel(got_ref, query_ref, out_w_ref, grid_ref, latents, rows):
    m = iota((256, 256), 0)
    k = m - MSG * div(m, float(MSG))
    pick = hot((k < 27.0) & (iota((256, 256), 1) == m - k + 27.0 + div(k, 8.0)))
    k = iota((256, D), 0)
    k = k - MSG * div(k, float(MSG))
    mask = div(iota((256, D), 1), 64.0) == k - 8.0 * div(k, 8.0)
    lane = iota((D, D), 0)
    lane = lane - 64.0 * div(lane, 64.0)
    fold = hot((lane < 48.0) & (lane - 16.0 * div(lane, 16.0) == div(iota((D, D), 1), 32.0)))
    lane = iota((D, 128), 0)
    lane = lane - 64.0 * div(lane, 64.0)
    base_w = jnp.where(lane == 48.0, 16.0, jnp.where(lane == 49.0, 1.0, 0.0)).astype(BF)
    q = query_ref[...].astype(F32)
    bias = jnp.where(k < 9.0, q[0:1], jnp.where(k < 18.0, q[1:2], q[2:3]))
    k = iota((256, 128), 0)
    k = k - MSG * div(k, float(MSG))
    for c in range(4):
        values = [got_ref[g, c * 256 : (c + 1) * 256, :] for g in range(2)]
        stats = [jnp.where(mask, dot(pick, v), 0.0).astype(BF) for v in values]
        logs = [dot(s, fold) for s in stats]
        peak = jnp.maximum(logs[0], logs[1])
        weights = [jnp.exp(l - peak) for l in logs]
        mixed = weights[0] * values[0].astype(F32) + weights[1] * values[1].astype(F32)
        encoded = (mixed / (weights[0] + weights[1])).astype(BF)
        latents[c * 256 : (c + 1) * 256, :] = (dot(encoded, out_w_ref[...]) + bias).astype(BF)
        place = dot(stats[0], base_w) + 6.0 * div(k, 9.0)
        place = jnp.where(k < 27.0, place, FAR)
        rows[:, c * 256 : (c + 1) * 256] = jnp.transpose(place)[0:8, :]
    where = rows[0:1, :]
    for b in range(4):
        chosen = hot(iota((224, 1024), 0) + 224.0 * b == where)
        grid_ref[b] = dot(chosen, latents[...]).astype(BF)


def settle(got, latent_query, enc_out):
    return pl.pallas_call(
        settle_kernel,
        in_specs=[VMEM] * 3,
        out_specs=VMEM,
        out_shape=jax.ShapeDtypeStruct((4, 224, D), BF),
        scratch_shapes=[pltpu.VMEM((1024, D), BF), pltpu.VMEM((8, 1024), F32)],
        compiler_params=params(),
        name="settle",
    )(got, latent_query, enc_out)


def normalize(values):
    offsets = values - jnp.mean(values, axis=-1, keepdims=True)
    spread = jnp.mean(offsets * offsets, axis=-1, keepdims=True)
    return offsets * lax.rsqrt(spread + epsilon)


def heads_of_group(qkv, out, rows, g, width, bias):
    column = pl.multiple_of(g * 128, 128)
    q = qkv[rows, pl.ds(column, 128)]
    k = qkv[rows, pl.ds(width + column, 128)]
    v = qkv[rows, pl.ds(2 * width + column, 128)]
    v = jnp.concatenate([v, jnp.ones_like(v)], axis=1)
    head = div(iota((1, 128), 1), 32.0)
    scale = math.log2(math.e) / math.sqrt(32.0)
    total = jnp.zeros((224, 128), F32)
    for h in range(4):
        only = head == float(h)
        scores = dot_nt(q * hot(only), k) + bias
        peak = jnp.max(scores, axis=1, keepdims=True)
        weights = jnp.exp2((scores - peak) * scale).astype(BF)
        mixed = dot(weights, v)
        total = total + jnp.where(only, mixed[:, :128] / mixed[:, 128:], 0.0)
    out[rows, pl.ds(column, 128)] = total.astype(BF)


def key_bias(slots, valid):
    lane = iota((1, 224), 1)
    lane = lane - slots * div(lane, float(slots))
    return jnp.where(lane < valid, 0.0, -1.0e30)


def shift_starts(shift_ref):
    s = shift_ref[0]
    near = s.astype(F32)
    far = jnp.where(s <= 6, s + 12, s - 12).astype(F32)
    return near, far


def window_kernel(
    shift_ref, before_ref, own_ref, after_ref, spread_ref, windows_ref, w_ref, proj_ref, out_ref, cells, x, qkv, mixed
):
    near, far = shift_starts(shift_ref)
    cells[0:224, :] = before_ref[...]
    for g in range(4):
        cells[(g + 1) * 224 : (g + 2) * 224, :] = own_ref[g]
    cells[1120:1344, :] = after_ref[...]
    for n in range(4):
        rows = slice(n * 224, (n + 1) * 224)
        target = windows_ref[rows, :] + 36.0 * (near if n < 2 else far)
        x[rows, :] = dot(hot(target == spread_ref[...]), cells[...]).astype(BF)
    for n in range(4):
        rows = slice(n * 224, (n + 1) * 224)
        normed = normalize(x[rows, :].astype(F32)).astype(BF)
        qkv[rows, :] = dot(normed, w_ref[...]).astype(BF)
    bias = key_bias(112, 108)

    @pl.loop(0, 16)
    def _(step):
        rows = pl.ds(pl.multiple_of((step // 4) * 224, 224), 224)
        heads_of_group(qkv, mixed, rows, lax.rem(step, 4), D, bias)

    for n in range(4):
        rows = slice(n * 224, (n + 1) * 224)
        out_ref[n] = (x[rows, :].astype(F32) + dot(mixed[rows, :], proj_ref[...])).astype(BF)


def window_block(shift, before, own, after, spread, windows, w_qkv, w_proj):
    return pl.pallas_call(
        window_kernel,
        in_specs=[SMEM] + [VMEM] * 7,
        out_specs=VMEM,
        out_shape=jax.ShapeDtypeStruct((4, 224, D), BF),
        scratch_shapes=[
            pltpu.VMEM((1344, D), BF),
            pltpu.VMEM((896, D), BF),
            pltpu.VMEM((896, 3 * D), BF),
            pltpu.VMEM((896, D), BF),
        ],
        compiler_params=params(),
        name="window_block",
    )(shift, before, own, after, spread, windows, w_qkv, w_proj)


def held_ids(shift_ref, held_ref):
    near, far = shift_starts(shift_ref)
    local = held_ref[1:2, :]
    return held_ref[0:1, :] + 36.0 * jnp.where(local > 0.5, near, far)


def gather_cells(cells, own_ref, before_ref, after_ref):
    for n in range(4):
        cells[n * 224 : (n + 1) * 224, :] = own_ref[n]
    for b in range(2):
        cells[896 + b * 112 : 1008 + b * 112, :] = before_ref[b]
        cells[1120 + b * 112 : 1232 + b * 112, :] = after_ref[b]


def coarse_kernel(
    shift_ref,
    own_ref,
    before_ref,
    after_ref,
    held_ref,
    sub_ref,
    merge_ref,
    w_ref,
    proj_ref,
    expand_ref,
    out_ref,
    cells,
    first,
    qkv,
    mixed,
):
    gather_cells(cells, own_ref, before_ref, after_ref)
    ids = held_ids(shift_ref, held_ref)
    total = jnp.zeros((224, 1), F32)
    for sub in range(4):
        rows = slice(sub * 224, (sub + 1) * 224)
        piece = dot(hot(sub_ref[rows, :] == ids), cells[...])
        first[rows, :] = piece.astype(BF)
        total = total + jnp.sum(piece, axis=1, keepdims=True)
    centre = total * (1.0 / (4 * D))
    spread = jnp.zeros((224, 1), F32)
    for sub in range(4):
        offsets = first[sub * 224 : (sub + 1) * 224, :].astype(F32) - centre
        spread = spread + jnp.sum(offsets * offsets, axis=1, keepdims=True)
    scale = lax.rsqrt(spread * (1.0 / (4 * D)) + epsilon)
    down = jnp.zeros((224, 2 * D), F32)
    for sub in range(4):
        offsets = first[sub * 224 : (sub + 1) * 224, :].astype(F32) - centre
        down = down + dot((offsets * scale).astype(BF), merge_ref[sub * D : (sub + 1) * D, :])
    down = down.astype(BF).astype(F32)
    qkv[...] = dot(normalize(down).astype(BF), w_ref[...]).astype(BF)
    bias = key_bias(56, 54)

    @pl.loop(0, 8)
    def _(g):
        heads_of_group(qkv, mixed, pl.ds(0, 224), g, 2 * D, bias)

    coarse = (down + dot(mixed[...], proj_ref[...])).astype(BF).astype(F32)
    normed = normalize(coarse).astype(BF)
    for sub in range(4):
        grown = dot(normed, expand_ref[:, sub * D : (sub + 1) * D])
        joined = grown + first[sub * 224 : (sub + 1) * 224, :].astype(F32)
        for g in range(4):
            out_ref[g, sub] = joined[g * 56 : (g + 1) * 56, :].astype(BF)


def coarse_block(shift, own, before, after, held, by_sub, merge_w, w_qkv, w_proj, expand_w):
    return pl.pallas_call(
        coarse_kernel,
        in_specs=[SMEM] + [VMEM] * 9,
        out_specs=VMEM,
        out_shape=jax.ShapeDtypeStruct((4, 4, 56, D), BF),
        scratch_shapes=[
            pltpu.VMEM((1344, D), BF),
            pltpu.VMEM((896, D), BF),
            pltpu.VMEM((224, 6 * D), BF),
            pltpu.VMEM((224, 2 * D), BF),
        ],
        compiler_params=params(),
        name="coarse_block",
    )(shift, own, before, after, held, by_sub, merge_w, w_qkv, w_proj, expand_w)


def final_kernel(shift_ref, own_ref, before_ref, after_ref, held_ref, final_ref, out_ref, cells):
    gather_cells(cells, own_ref, before_ref, after_ref)
    ids = held_ids(shift_ref, held_ref)
    for b in range(4):
        rows = slice(b * 216, (b + 1) * 216)
        out_ref[rows, :] = dot(hot(final_ref[rows, :] == ids), cells[...]).astype(BF)


def final_order(shift, own, before, after, held, final):
    return pl.pallas_call(
        final_kernel,
        in_specs=[SMEM] + [VMEM] * 5,
        out_specs=VMEM,
        out_shape=jax.ShapeDtypeStruct((PLAT * LATENT * PLON, D), BF),
        scratch_shapes=[pltpu.VMEM((1344, D), BF)],
        compiler_params=params(),
        name="final_order",
    )(shift, own, before, after, held, final)


def passed_along(value, axis, steps):
    count = lax.axis_size(axis)
    pairs = [(source, (source + steps) % count) for source in range(count)]
    return lax.ppermute(value, axis, pairs)


def from_sides(to_previous, to_next):
    return passed_along(to_next, "win", 1), passed_along(to_previous, "win", -1)


def local(
    fields,
    patch_order,
    shift_offsets,
    latent_query,
    enc_kv,
    enc_out,
    qkv_a,
    proj_a,
    merge_w,
    qkv_b,
    proj_b,
    expand_w,
    qkv_c,
    proj_c,
):
    lev_at = lax.axis_index("lev")
    win_at = lax.axis_index("win")
    spread, windows, held, by_sub, final = tables()
    slots = lax.dynamic_slice_in_dim(patch_order, win_at * PSH, PSH, 0).reshape(1, PSH)
    core = lax.rem(lev_at, 2).astype(jnp.int32).reshape(1)
    keep, send, meta = sort_fields(core, slots, fields)
    got = lax.ppermute(send, "lev", [(0, 1), (1, 0), (2, 3), (3, 2)])
    messages = encode(keep, got, meta, enc_kv, latent_query)
    arrived = swap(messages.reshape(64, MSG, D)).reshape(2, 32 * MSG, D)
    grid = settle(arrived, latent_query, enc_out)

    def shifted(grid, shift, w_qkv, w_proj):
        before, after = from_sides(grid[0], grid[3])
        done = window_block(shift, before, grid, after, spread, windows, w_qkv, w_proj)
        return (done,) + from_sides(done[2:, :112], done[2:, 112:])

    shift = shift_offsets[0:1]
    done, before, after = shifted(grid, shift, qkv_a, proj_a)
    joined = coarse_block(
        shift, done, before, after, held, by_sub, merge_w, qkv_b, proj_b, expand_w
    ).reshape(4, 224, D)
    shift = shift_offsets[1:2]
    done, before, after = shifted(joined, shift, qkv_c, proj_c)
    result = final_order(shift, done, before, after, held, final)
    return result.reshape(PLAT, LATENT, PLON, D).transpose(0, 2, 1, 3)


def solution(mesh):
    placed = (P("lev", "win", None),) + (P(),) * 13
    return jax.shard_map(
        local, mesh=mesh, in_specs=placed, out_specs=P("lev", "win", None, None), check_vma=False
    )
```

```python
import functools
import math

import jax
import jax.numpy as jnp
import numpy as np
from jax import lax
from jax.experimental import pallas as pl
from jax.experimental.pallas import tpu as pltpu
from jax.sharding import PartitionSpec as P

D = 512
HEADS = 16
LATENT = 3
PLAT = 12
PLON = 24
N_LEV = 4
N_WIN = 32
PSH = 1152
PER = 9
MSG = 32
CHUNK = 144
epsilon = 1e-05
BF = jnp.bfloat16
F32 = jnp.float32
MESH = pl.DeviceIdType.MESH
FAR = -1.0e6
VMEM = pl.BlockSpec(memory_space=pltpu.VMEM)
SMEM = pl.BlockSpec(memory_space=pltpu.SMEM)
ANY = pl.BlockSpec(memory_space=pl.ANY)


def params(mib=60, **more):
    return pltpu.CompilerParams(vmem_limit_bytes=mib << 20, **more)


def dot(a, b):
    return jnp.dot(a, b, preferred_element_type=F32)


def dot_nt(a, b):
    return lax.dot_general(a, b, (((1,), (1,)), ((), ())), preferred_element_type=F32)


def iota(shape, axis):
    return lax.broadcasted_iota(jnp.int32, shape, axis).astype(F32)


def div(values, by):
    return jnp.floor((values + 0.5) * (1.0 / by))


def hot(condition):
    return jnp.where(condition, 1.0, 0.0).astype(BF)


def group_ids(first_column, spare=None):
    ids = np.zeros((4, 56), np.float32)
    for sub in range(4):
        for q in range(56):
            p = min(q, 53)
            column = first_column + 2 * (p // 18) + (sub & 1)
            ids[sub, q] = column * 36 + (2 * (p % 6) + (sub >> 1)) * 3 + p % 18 // 6
    if spare is not None:
        ids[:, 54:] = spare
    return ids


def half_ids(band, first_column, spare=None):
    ids = np.zeros((112,), np.float32)
    for q in range(112):
        p = min(q, 107)
        ids[q] = (first_column + p // 18) * 36 + (band * 6 + p % 6) * 3 + p % 18 // 6
    if spare is not None:
        ids[108:] = spare
    return ids


def tables():
    groups = [group_ids(6 * g, FAR).reshape(-1) for g in range(-1, 5)]
    spread = np.concatenate(groups[1:5] + [groups[0], groups[5]])
    windows = np.concatenate(
        [np.concatenate([half_ids(b, 0), half_ids(b, 6)]) for _ in range(2) for b in range(2)]
    )
    held = np.zeros((8, 1344), np.float32)
    held[0] = np.concatenate(
        [np.concatenate([half_ids(b, 0, FAR), half_ids(b, 6, FAR)]) for _ in range(2) for b in range(2)]
        + [half_ids(b, 6 - PLON, FAR) for b in range(2)]
        + [half_ids(b, PLON, FAR) for b in range(2)]
    )
    held[1, :448] = 1.0
    by_sub = np.stack([group_ids(6 * g) for g in range(4)], axis=1).reshape(-1)
    final = np.zeros((PLAT, LATENT, PLON), np.float32)
    for r in range(PLAT):
        for a in range(LATENT):
            for c in range(PLON):
                final[r, a, c] = c * 36 + r * 3 + a
    return (
        jnp.asarray(spread[None]),
        jnp.asarray(windows[:, None]),
        jnp.asarray(held),
        jnp.asarray(by_sub[:, None]),
        jnp.asarray(final.reshape(-1, 1)),
    )


def sort_kernel(core_ref, slots_ref, x_ref, keep_ref, send_ref, meta_ref, perm):
    @pl.when(pl.program_id(0) == 0)
    def _():
        core = core_ref[0].astype(F32)
        p = slots_ref[...].astype(F32)
        row = div(p, 768.0)
        column = p - row * 768.0
        band = div(row, 12.0)
        shard = div(column, 24.0)
        row = row - band * 12.0
        column = column - shard * 24.0
        half = div(band, 2.0)
        other = jnp.abs(band - 2.0 * half - core)
        key = other * 64.0 + half * 32.0 + shard
        member = hot(iota((128, PSH), 0) == key)
        upper = hot(iota((128, 128), 0) < iota((128, 128), 1))
        seen = jnp.zeros((128, 1), F32)
        ranks = []
        for b in range(PSH // 128):
            piece = member[:, b * 128 : (b + 1) * 128]
            wide = piece.astype(F32)
            ranks.append(jnp.sum(wide * (dot(piece, upper) + seen), axis=0, keepdims=True))
            seen = seen + jnp.sum(wide, axis=1, keepdims=True)
        target = key * PER + jnp.concatenate(ranks, axis=1)
        for b in range(PSH // 128):
            perm[b * 128 : (b + 1) * 128, :] = hot(iota((128, PSH), 0) + b * 128.0 == target)
        j = div(column, 2.0)
        group = div(j, 3.0)
        i = div(row, 2.0)
        sub = 2.0 * (row - 2.0 * i) + column - 2.0 * j
        base = group * 224.0 + sub * 56.0 + (j - 3.0 * group) * 18.0 + i
        high = div(base, 16.0)
        low = base - 16.0 * high
        at = iota((128, PSH), 0)
        meta = jnp.where(at == 48.0, high, jnp.where(at == 49.0, low, 0.0)).astype(BF)
        meta_ref[...] = dot_nt(perm[0:576, :], meta).astype(BF)

    done = dot(perm[...], x_ref[0])
    keep_ref[0] = done[:576].astype(BF)
    send_ref[0] = done[576:].astype(BF)


def sort_fields(core, slots, fields):
    levels = fields.shape[0]
    return pl.pallas_call(
        sort_kernel,
        grid=(levels,),
        in_specs=[
            SMEM,
            pl.BlockSpec((1, PSH), lambda l: (0, 0)),
            pl.BlockSpec((1, PSH, D), lambda l: (l, 0, 0)),
        ],
        out_specs=[
            pl.BlockSpec((1, 576, D), lambda l: (l, 0, 0)),
            pl.BlockSpec((1, 576, D), lambda l: (l, 0, 0)),
            pl.BlockSpec((576, 128), lambda l: (0, 0)),
        ],
        out_shape=[
            jax.ShapeDtypeStruct((levels, 576, D), BF),
            jax.ShapeDtypeStruct((levels, 576, D), BF),
            jax.ShapeDtypeStruct((576, 128), BF),
        ],
        scratch_shapes=[pltpu.VMEM((PSH, PSH), BF)],
        compiler_params=params(),
        name="sort_fields",
    )(core, slots, fields)


def encode_kernel(own_ref, got_ref, meta_ref, kv_ref, query_ref, out_ref, score_w, spread_w, stat_w, pick, stack):
    @pl.when(pl.program_id(0) == 0)
    def _():
        c = iota((128, D), 0)
        lane = iota((128, D), 1)
        a = div(c, 16.0)
        q = query_ref[...].astype(F32)
        chosen = jnp.where(a == 0.0, q[0:1], jnp.where(a == 1.0, q[1:2], q[2:3]))
        mine = (c - 16.0 * a == div(lane, 32.0)) & (c < 48.0)
        heads = jnp.where(mine, chosen, 0.0).astype(BF)
        folded = dot_nt(kv_ref[:, :D], heads) * (1.0 / math.sqrt(D // HEADS))
        high = folded.astype(BF)
        score_w[:, 0:128] = high
        score_w[:, 128:256] = (folded - high.astype(F32)).astype(BF)
        for a in range(LATENT):
            spread_w[:, a * D : (a + 1) * D] = hot(c == 16.0 * a + div(lane, 32.0))
            s = iota((128, 128), 0)
            t = iota((128, 128), 1)
            t = t - 64.0 * div(t, 64.0)
            for piece in range(3):
                here = (t >= 16.0 * piece) & (t < 16.0 * piece + 16.0)
                stat_w[piece * 128 : (piece + 1) * 128, a * 128 : (a + 1) * 128] = hot(
                    here & (s == 16.0 * a + t - 16.0 * piece)
                )
            stat_w[384:512, a * 128 : (a + 1) * 128] = hot((t >= 48.0) & (t < 50.0) & (s == t))
        lane = iota((1, 6 * CHUNK), 1)
        kind = div(lane, float(CHUNK))
        slot = lane - kind * CHUNK
        stats = kind >= 3.0
        a = jnp.where(stats, kind - 3.0, kind)
        dest = div(slot, float(PER))
        k = a * PER + slot - dest * PER
        row = dest * MSG + jnp.where(stats, 27.0 + div(k, 8.0), k)
        for b in range(4):
            pick[b * 128 : (b + 1) * 128, :] = hot(iota((128, 6 * CHUNK), 0) + b * 128.0 == row)

    xs = [own_ref[l] for l in range(3)] + [got_ref[l] for l in range(3)]
    scores = []
    for x in xs:
        both = dot(x, score_w[...])
        scores.append(both[:, :128] + both[:, 128:])
    peak = functools.reduce(jnp.maximum, scores)
    weights = [jnp.exp(s - peak) for s in scores]
    total = functools.reduce(jnp.add, weights)
    mixes = [jnp.zeros((CHUNK, D), F32)] * LATENT
    for x, w in zip(xs, weights):
        value = dot(x, kv_ref[:, D:]).astype(BF).astype(F32)
        wide = dot((w / total).astype(BF), spread_w[...])
        mixes = [m + wide[:, a * D : (a + 1) * D] * value for a, m in enumerate(mixes)]
    logsum = peak + jnp.log(total)
    high = logsum.astype(BF)
    rest = logsum - high.astype(F32)
    middle = rest.astype(BF)
    low = (rest - middle.astype(F32)).astype(BF)
    stats = dot(jnp.concatenate([high, middle, low, meta_ref[...]], axis=1), stat_w[...])
    slot = iota((CHUNK, D), 0)
    rank = slot - PER * div(slot, float(PER))
    block = div(iota((CHUNK, D), 1), 64.0)
    for a in range(LATENT):
        stack[a * CHUNK : (a + 1) * CHUNK, :] = mixes[a].astype(BF)
        k = rank + PER * a
        tiled = jnp.concatenate([stats[:, a * 128 : (a + 1) * 128]] * 4, axis=1)
        stack[(3 + a) * CHUNK : (4 + a) * CHUNK, :] = jnp.where(
            block == k - 8.0 * div(k, 8.0), tiled, 0.0
        ).astype(BF)
    out_ref[...] = dot(pick[...], stack[...]).astype(BF)


def encode(own, got, meta, enc_kv, latent_query):
    return pl.pallas_call(
        encode_kernel,
        grid=(576 // CHUNK,),
        in_specs=[
            pl.BlockSpec((3, CHUNK, D), lambda i: (0, i, 0)),
            pl.BlockSpec((3, CHUNK, D), lambda i: (0, i, 0)),
            pl.BlockSpec((CHUNK, 128), lambda i: (i, 0)),
            VMEM,
            VMEM,
        ],
        out_specs=pl.BlockSpec((16 * MSG, D), lambda i: (i, 0)),
        out_shape=jax.ShapeDtypeStruct((64 * MSG, D), BF),
        scratch_shapes=[
            pltpu.VMEM((D, 256), BF),
            pltpu.VMEM((128, LATENT * D), BF),
            pltpu.VMEM((512, LATENT * 128), BF),
            pltpu.VMEM((16 * MSG, 6 * CHUNK), BF),
            pltpu.VMEM((6 * CHUNK, D), BF),
        ],
        compiler_params=params(),
        name="encode",
    )(own, got, meta, enc_kv, latent_query)


def swap_kernel(msg_ref, out_ref, send_sem, recv_sem, own_sem):
    lev = lax.axis_index("lev")
    win = lax.axis_index("win")
    core = lax.rem(lev, 2)
    me = (lev // 2) * N_WIN + win
    count = 2 * N_WIN

    def device(index):
        return ((index // N_WIN) * 2 + core, lax.rem(index, N_WIN))

    own = pltpu.make_async_copy(msg_ref.at[me], out_ref.at[me], own_sem)
    own.start()
    barrier = pltpu.get_barrier_semaphore()

    @pl.loop(1, count)
    def _(k):
        pl.semaphore_signal(
            barrier, inc=1, device_id=device(lax.rem(me + k, count)), device_id_type=MESH
        )

    pl.semaphore_wait(barrier, count - 1)

    def copy(k):
        dest = lax.rem(me + k, count)
        return pltpu.make_async_remote_copy(
            src_ref=msg_ref.at[dest],
            dst_ref=out_ref.at[me],
            send_sem=send_sem.at[k],
            recv_sem=recv_sem.at[k],
            device_id=device(dest),
            device_id_type=MESH,
        )

    @pl.loop(1, count)
    def _(k):
        copy(k).start()

    @pl.loop(1, count)
    def _(k):
        copy(k).wait()

    own.wait()


def swap(messages):
    return pl.pallas_call(
        swap_kernel,
        out_shape=jax.ShapeDtypeStruct((64, MSG, D), BF),
        in_specs=[ANY],
        out_specs=ANY,
        scratch_shapes=[
            pltpu.SemaphoreType.DMA((64,)),
            pltpu.SemaphoreType.DMA((64,)),
            pltpu.SemaphoreType.DMA,
        ],
        compiler_params=pltpu.CompilerParams(collective_id=0, has_side_effects=True),
        name="swap",
    )(messages)


def settle_kernel(got_ref, query_ref, out_w_ref, grid_ref, latents, rows):
    m = iota((256, 256), 0)
    k = m - MSG * div(m, float(MSG))
    pick = hot((k < 27.0) & (iota((256, 256), 1) == m - k + 27.0 + div(k, 8.0)))
    k = iota((256, D), 0)
    k = k - MSG * div(k, float(MSG))
    mask = div(iota((256, D), 1), 64.0) == k - 8.0 * div(k, 8.0)
    lane = iota((D, D), 0)
    lane = lane - 64.0 * div(lane, 64.0)
    fold = hot((lane < 48.0) & (lane - 16.0 * div(lane, 16.0) == div(iota((D, D), 1), 32.0)))
    lane = iota((D, 128), 0)
    lane = lane - 64.0 * div(lane, 64.0)
    base_w = jnp.where(lane == 48.0, 16.0, jnp.where(lane == 49.0, 1.0, 0.0)).astype(BF)
    q = query_ref[...].astype(F32)
    bias = jnp.where(k < 9.0, q[0:1], jnp.where(k < 18.0, q[1:2], q[2:3]))
    k = iota((256, 128), 0)
    k = k - MSG * div(k, float(MSG))
    for c in range(4):
        values = [got_ref[g, c * 256 : (c + 1) * 256, :] for g in range(2)]
        stats = [jnp.where(mask, dot(pick, v), 0.0).astype(BF) for v in values]
        logs = [dot(s, fold) for s in stats]
        peak = jnp.maximum(logs[0], logs[1])
        weights = [jnp.exp(l - peak) for l in logs]
        mixed = weights[0] * values[0].astype(F32) + weights[1] * values[1].astype(F32)
        encoded = (mixed / (weights[0] + weights[1])).astype(BF)
        latents[c * 256 : (c + 1) * 256, :] = (dot(encoded, out_w_ref[...]) + bias).astype(BF)
        place = dot(stats[0], base_w) + 6.0 * div(k, 9.0)
        place = jnp.where(k < 27.0, place, FAR)
        rows[:, c * 256 : (c + 1) * 256] = jnp.transpose(place)[0:8, :]
    where = rows[0:1, :]
    for b in range(4):
        chosen = hot(iota((224, 1024), 0) + 224.0 * b == where)
        grid_ref[b] = dot(chosen, latents[...]).astype(BF)


def settle(got, latent_query, enc_out):
    return pl.pallas_call(
        settle_kernel,
        in_specs=[VMEM] * 3,
        out_specs=VMEM,
        out_shape=jax.ShapeDtypeStruct((4, 224, D), BF),
        scratch_shapes=[pltpu.VMEM((1024, D), BF), pltpu.VMEM((8, 1024), F32)],
        compiler_params=params(),
        name="settle",
    )(got, latent_query, enc_out)


def normalize(values):
    offsets = values - jnp.mean(values, axis=-1, keepdims=True)
    spread = jnp.mean(offsets * offsets, axis=-1, keepdims=True)
    return offsets * lax.rsqrt(spread + epsilon)


def heads_of_group(qkv, out, g, width, valid):
    column = g * 128
    if not isinstance(g, int):
        column = pl.multiple_of(column, 128)
    q = qkv[:, pl.ds(column, 128)]
    k = qkv[:, pl.ds(width + column, 128)]
    v = qkv[:, pl.ds(2 * width + column, 128)]
    v = jnp.concatenate([v * valid, valid], axis=1)
    head = div(iota((1, 128), 1), 32.0)
    queries = jnp.concatenate([q * hot(head == float(h)) for h in range(4)], axis=0)
    scores = dot_nt(queries, k)
    scores = (scores - jnp.max(scores, axis=1, keepdims=True)) * (math.log2(math.e) / math.sqrt(32.0))
    mixed = dot(jnp.exp2(scores).astype(BF), v)
    head = jnp.concatenate([head, head], axis=1)
    total = mixed[0:224]
    for h in range(1, 4):
        total = jnp.where(head == float(h), mixed[h * 224 : (h + 1) * 224], total)
    out[:, pl.ds(column, 128)] = (total[:, :128] / total[:, 128:]).astype(BF)


def valid_keys(slots, valid):
    row = iota((224, 128), 0)
    return hot(row - slots * div(row, float(slots)) < valid)


def shift_starts(s):
    near = s.astype(F32)
    far = jnp.where(s <= 6, s + 12, s - 12).astype(F32)
    return near, far


class Links:
    def __init__(self, send, recv):
        lev = lax.axis_index("lev")
        win = lax.axis_index("win")
        self.send, self.recv = send, recv
        self.sides = (
            (lev, lax.rem(win + N_WIN - 1, N_WIN)),
            (lev, lax.rem(win + 1, N_WIN)),
        )

    def greet(self):
        barrier = pltpu.get_barrier_semaphore()
        for side in self.sides:
            pl.semaphore_signal(barrier, inc=1, device_id=side, device_id_type=MESH)
        pl.semaphore_wait(barrier, 2)

    def copy(self, side, sem, source, target):
        return pltpu.make_async_remote_copy(
            src_ref=source,
            dst_ref=target,
            send_sem=self.send.at[sem],
            recv_sem=self.recv.at[sem],
            device_id=self.sides[side],
            device_id_type=MESH,
        )

    def cells(self, base, own, halo):
        return (
            self.copy(0, base, own.at[pl.ds(0, 224)], halo.at[pl.ds(224, 224)]),
            self.copy(1, base + 1, own.at[pl.ds(672, 224)], halo.at[pl.ds(0, 224)]),
        )

    def results(self, base, band, results, land):
        first = pl.multiple_of(448 + band * 224, 16)
        return (
            self.copy(
                0,
                base + 2 * band,
                results.at[pl.ds(first, 112)],
                land.at[pl.ds(pl.multiple_of(224 + band * 112, 16), 112)],
            ),
            self.copy(
                1,
                base + 2 * band + 1,
                results.at[pl.ds(pl.multiple_of(first + 112, 16), 112)],
                land.at[pl.ds(pl.multiple_of(band * 112, 16), 112)],
            ),
        )


def shifted_windows(links, base, shift, own, halo, results, land, spread_ref, windows_ref, w_ref, proj_ref, x, qkv, mixed):
    near, far = shift_starts(shift)
    valid = valid_keys(112, 108)

    @pl.loop(0, 4)
    def _(step):
        band = step // 2
        outer = lax.rem((step + 1) // 2, 2)
        rows = pl.ds(pl.multiple_of((outer * 2 + band) * 224, 224), 224)
        target = windows_ref[rows, :] + 36.0 * jnp.where(outer == 0, near, far)
        x[...] = dot(hot(target == spread_ref[:, 0:896]), own[...])

        @pl.when(step == 1)
        def _():
            for copy in links.cells(base, own, halo):
                copy.wait()

        @pl.when(outer == 1)
        def _():
            x[...] += dot(hot(target == spread_ref[:, 896:1344]), halo[...])

        qkv[...] = dot(normalize(x[...]).astype(BF), w_ref[...]).astype(BF)
        for g in range(4):
            heads_of_group(qkv, mixed, g, D, valid)
        results[rows, :] = (x[...] + dot(mixed[...], proj_ref[...])).astype(BF)

        @pl.when(outer == 1)
        def _():
            for copy in links.results(base + 2, band, results, land):
                copy.start()


def held_ids(shift, held_ref):
    near, far = shift_starts(shift)
    return held_ref[0:1, :] + 36.0 * jnp.where(held_ref[1:2, :] > 0.5, near, far)


def gathered(target, ids, results, land):
    return dot(hot(target == ids[:, 0:896]), results[...]) + dot(
        hot(target == ids[:, 896:1344]), land[...]
    )


def unet_kernel(
    shift_ref,
    own_ref,
    spread_ref,
    windows_ref,
    held_ref,
    sub_ref,
    final_ref,
    qkv_a,
    proj_a,
    merge_w,
    qkv_b,
    proj_b,
    expand_w,
    qkv_c,
    proj_c,
    out_ref,
    qkv_a_v,
    proj_a_v,
    merge_v,
    qkv_b_v,
    proj_b_v,
    expand_v,
    qkv_c_v,
    proj_c_v,
    halo_a,
    halo_c,
    land_a,
    land_c,
    results,
    joined,
    first,
    x,
    qkv,
    mixed,
    qkv_wide,
    mixed_wide,
    send,
    recv,
    weight_sem,
):
    links = Links(send, recv)
    links.greet()
    for copy in links.cells(0, own_ref, halo_a):
        copy.start()
    pairs = [
        (qkv_a, qkv_a_v),
        (proj_a, proj_a_v),
        (merge_w, merge_v),
        (qkv_b, qkv_b_v),
        (proj_b, proj_b_v),
        (expand_w, expand_v),
        (qkv_c, qkv_c_v),
        (proj_c, proj_c_v),
    ]
    loads = [pltpu.make_async_copy(a, b, weight_sem.at[n]) for n, (a, b) in enumerate(pairs)]
    for load in loads:
        load.start()
    loads[0].wait()
    loads[1].wait()
    shift = shift_ref[0]
    shifted_windows(
        links, 0, shift, own_ref, halo_a, results, land_a, spread_ref, windows_ref, qkv_a_v, proj_a_v, x, qkv, mixed
    )
    for load in loads[2:]:
        load.wait()
    for band in range(2):
        for copy in links.results(2, band, results, land_a):
            copy.wait()

    ids = held_ids(shift, held_ref)
    total = jnp.zeros((224, 1), F32)
    for sub in range(4):
        rows = slice(sub * 224, (sub + 1) * 224)
        piece = gathered(sub_ref[rows, :], ids, results, land_a)
        first[rows, :] = piece.astype(BF)
        total = total + jnp.sum(piece, axis=1, keepdims=True)
    centre = total * (1.0 / (4 * D))
    spread = jnp.zeros((224, 1), F32)
    for sub in range(4):
        offsets = first[sub * 224 : (sub + 1) * 224, :].astype(F32) - centre
        spread = spread + jnp.sum(offsets * offsets, axis=1, keepdims=True)
    scale = lax.rsqrt(spread * (1.0 / (4 * D)) + epsilon)
    down = jnp.zeros((224, 2 * D), F32)
    for sub in range(4):
        offsets = first[sub * 224 : (sub + 1) * 224, :].astype(F32) - centre
        down = down + dot((offsets * scale).astype(BF), merge_v[sub * D : (sub + 1) * D, :])
    down = down.astype(BF).astype(F32)
    qkv_wide[...] = dot(normalize(down).astype(BF), qkv_b_v[...]).astype(BF)
    valid = valid_keys(56, 54)

    @pl.loop(0, 2)
    def _(step):
        for g in range(4):
            heads_of_group(qkv_wide, mixed_wide, step * 4 + g, 2 * D, valid)

    coarse = (down + dot(mixed_wide[...], proj_b_v[...])).astype(BF).astype(F32)
    normed = normalize(coarse).astype(BF)
    for sub in range(4):
        grown = dot(normed, expand_v[:, sub * D : (sub + 1) * D])
        grown = grown + first[sub * 224 : (sub + 1) * 224, :].astype(F32)
        for g in range(4):
            joined[g * 224 + sub * 56 : g * 224 + (sub + 1) * 56, :] = grown[g * 56 : (g + 1) * 56, :].astype(BF)

    for copy in links.cells(6, joined, halo_c):
        copy.start()
    shift = shift_ref[1]
    shifted_windows(
        links, 6, shift, joined, halo_c, results, land_c, spread_ref, windows_ref, qkv_c_v, proj_c_v, x, qkv, mixed
    )
    for band in range(2):
        for copy in links.results(8, band, results, land_c):
            copy.wait()
    ids = held_ids(shift, held_ref)
    for b in range(4):
        rows = slice(b * 216, (b + 1) * 216)
        out_ref[rows, :] = gathered(final_ref[rows, :], ids, results, land_c).astype(BF)


def unet(shifts, grid, weights):
    rows = lambda count, width=D: pltpu.VMEM((count, width), BF)
    return pl.pallas_call(
        unet_kernel,
        in_specs=[SMEM] + [VMEM] * 6 + [ANY] * 8,
        out_specs=VMEM,
        out_shape=jax.ShapeDtypeStruct((PLAT * LATENT * PLON, D), BF),
        scratch_shapes=[pltpu.VMEM(w.shape, BF) for w in weights]
        + [rows(448)] * 4
        + [rows(896)] * 3
        + [pltpu.VMEM((224, D), F32), rows(224, 3 * D), rows(224), rows(224, 6 * D), rows(224, 2 * D)]
        + [pltpu.SemaphoreType.DMA((12,)), pltpu.SemaphoreType.DMA((12,)), pltpu.SemaphoreType.DMA((8,))],
        compiler_params=params(collective_id=1, has_side_effects=True),
        name="unet",
    )(shifts, grid, *tables(), *weights)


def local(
    fields,
    patch_order,
    shift_offsets,
    latent_query,
    enc_kv,
    enc_out,
    qkv_a,
    proj_a,
    merge_w,
    qkv_b,
    proj_b,
    expand_w,
    qkv_c,
    proj_c,
):
    lev_at = lax.axis_index("lev")
    win_at = lax.axis_index("win")
    slots = lax.dynamic_slice_in_dim(patch_order, win_at * PSH, PSH, 0).reshape(1, PSH)
    core = lax.rem(lev_at, 2).astype(jnp.int32).reshape(1)
    keep, send, meta = sort_fields(core, slots, fields)
    got = lax.ppermute(send, "lev", [(0, 1), (1, 0), (2, 3), (3, 2)])
    messages = encode(keep, got, meta, enc_kv, latent_query)
    arrived = swap(messages.reshape(64, MSG, D)).reshape(2, 32 * MSG, D)
    grid = settle(arrived, latent_query, enc_out)

    weights = (qkv_a, proj_a, merge_w, qkv_b, proj_b, expand_w, qkv_c, proj_c)
    result = unet(shift_offsets, grid.reshape(896, D), weights)
    return result.reshape(PLAT, LATENT, PLON, D).transpose(0, 2, 1, 3)


def solution(mesh):
    placed = (P("lev", "win", None),) + (P(),) * 13
    return jax.shard_map(
        local, mesh=mesh, in_specs=placed, out_specs=P("lev", "win", None, None), check_vma=False
    )
```

```python
import functools
import math

import jax
import jax.numpy as jnp
import numpy as np
from jax import lax
from jax.experimental import pallas as pl
from jax.experimental.pallas import tpu as pltpu
from jax.sharding import PartitionSpec as P

D = 512
HEADS = 16
LATENT = 3
PLAT = 12
PLON = 24
N_LEV = 4
N_WIN = 32
PSH = 1152
PER = 9
MSG = 32
CHUNK = 144
epsilon = 1e-05
BF = jnp.bfloat16
F32 = jnp.float32
MESH = pl.DeviceIdType.MESH
FAR = -1.0e6
VMEM = pl.BlockSpec(memory_space=pltpu.VMEM)
SMEM = pl.BlockSpec(memory_space=pltpu.SMEM)
ANY = pl.BlockSpec(memory_space=pl.ANY)
HBM = pl.BlockSpec(memory_space=pltpu.HBM)


def params(mib=60, **more):
    return pltpu.CompilerParams(vmem_limit_bytes=mib << 20, **more)


def dot(a, b):
    return jnp.dot(a, b, preferred_element_type=F32)


def dot_nt(a, b):
    return lax.dot_general(a, b, (((1,), (1,)), ((), ())), preferred_element_type=F32)


def iota(shape, axis):
    return lax.broadcasted_iota(jnp.int32, shape, axis).astype(F32)


def div(values, by):
    return jnp.floor((values + 0.5) * (1.0 / by))


def hot(condition):
    return jnp.where(condition, 1.0, 0.0).astype(BF)


def group_ids(first_column, spare=None):
    ids = np.zeros((4, 56), np.float32)
    for sub in range(4):
        for q in range(56):
            p = min(q, 53)
            column = first_column + 2 * (p // 18) + (sub & 1)
            ids[sub, q] = column * 36 + (2 * (p % 6) + (sub >> 1)) * 3 + p % 18 // 6
    if spare is not None:
        ids[:, 54:] = spare
    return ids


def half_ids(band, first_column, spare=None):
    ids = np.zeros((112,), np.float32)
    for q in range(112):
        p = min(q, 107)
        ids[q] = (first_column + p // 18) * 36 + (band * 6 + p % 6) * 3 + p % 18 // 6
    if spare is not None:
        ids[108:] = spare
    return ids


def tables():
    groups = [group_ids(6 * g, FAR).reshape(-1) for g in range(-1, 5)]
    spread = np.concatenate(groups[1:5] + [groups[0], groups[5]])
    windows = np.concatenate(
        [np.concatenate([half_ids(b, 0), half_ids(b, 6)]) for _ in range(2) for b in range(2)]
    )
    held = np.zeros((8, 1344), np.float32)
    held[0] = np.concatenate(
        [np.concatenate([half_ids(b, 0, FAR), half_ids(b, 6, FAR)]) for _ in range(2) for b in range(2)]
        + [half_ids(b, 6 - PLON, FAR) for b in range(2)]
        + [half_ids(b, PLON, FAR) for b in range(2)]
    )
    held[1, :448] = 1.0
    by_sub = np.stack([group_ids(6 * g) for g in range(4)], axis=1).reshape(-1)
    final = np.zeros((PLAT, LATENT, PLON), np.float32)
    for r in range(PLAT):
        for a in range(LATENT):
            for c in range(PLON):
                final[r, a, c] = c * 36 + r * 3 + a
    return (
        jnp.asarray(spread[None]),
        jnp.asarray(windows[:, None]),
        jnp.asarray(held),
        jnp.asarray(by_sub[:, None]),
        jnp.asarray(final.reshape(-1, 1)),
    )


def place_of_me():
    lev = lax.axis_index("lev")
    win = lax.axis_index("win")
    return lev // 2, win // 8, lax.rem(win // 4, 2), lax.rem(win, 4), lax.rem(lev, 2)


def receiver(j):
    half, x, low, y, core = place_of_me()
    k = lax.rem(((j // 16) * 8 + lax.rem(j, 8)) * 11, 32)
    half = lax.rem(half + lax.rem(j // 8, 2), 2)
    x = lax.rem(x + k // 8, 4)
    low = lax.rem(low + lax.rem(k // 4, 2), 2)
    y = lax.rem(y + lax.rem(k, 4), 4)
    return (half * 2 + core, x * 8 + low * 4 + y)


def message_of(half, shard):
    my_half, my_x, my_low, my_y, _ = (value.astype(F32) for value in place_of_me())
    x = div(shard, 8.0)
    y = shard - 8.0 * x
    low = div(y, 4.0)
    y = y - 4.0 * low
    x = x - my_x + 4.0
    x = x - 4.0 * div(x, 4.0)
    y = y - my_y + 4.0
    y = y - 4.0 * div(y, 4.0)
    pair = 3.0 * (8.0 * x + 4.0 * jnp.abs(low - my_low) + y)
    pair = pair - 32.0 * div(pair, 32.0)
    block = div(pair, 8.0)
    return block * 16.0 + 8.0 * jnp.abs(half - my_half) + pair - 8.0 * block


def sort_kernel(
    order_ref, fields_ref, keep_ref, got_ref, meta_ref, perm, fields, outgoing, load_sem, send_sem, recv_sem
):
    lev = lax.axis_index("lev")
    win = lax.axis_index("win")
    mate = (lev + 1 - 2 * lax.rem(lev, 2), win)
    loads = [
        pltpu.make_async_copy(fields_ref.at[l], fields.at[l], load_sem.at[l]) for l in range(3)
    ]
    for load in loads:
        load.start()
    barrier = pltpu.get_barrier_semaphore()
    pl.semaphore_signal(barrier, inc=1, device_id=mate, device_id_type=MESH)

    core = lax.rem(lev, 2).astype(F32)
    p = jnp.concatenate([order_ref[pl.ds(9 * win + r, 1), :] for r in range(9)], axis=1).astype(F32)
    row = div(p, 768.0)
    column = p - row * 768.0
    band = div(row, 12.0)
    shard = div(column, 24.0)
    row = row - band * 12.0
    column = column - shard * 24.0
    half = div(band, 2.0)
    key = jnp.abs(band - 2.0 * half - core) * 64.0 + message_of(half, shard)
    member = hot(iota((128, PSH), 0) == key)
    upper = hot(iota((128, 128), 0) < iota((128, 128), 1))
    seen = jnp.zeros((128, 1), F32)
    ranks = []
    for b in range(PSH // 128):
        piece = member[:, b * 128 : (b + 1) * 128]
        wide = piece.astype(F32)
        ranks.append(jnp.sum(wide * (dot(piece, upper) + seen), axis=0, keepdims=True))
        seen = seen + jnp.sum(wide, axis=1, keepdims=True)
    target = key * PER + jnp.concatenate(ranks, axis=1)
    for b in range(PSH // 128):
        perm[b * 128 : (b + 1) * 128, :] = hot(iota((128, PSH), 0) + b * 128.0 == target)
    pl.semaphore_wait(barrier, 1)
    copies = []
    for l in range(3):
        loads[l].wait()
        outgoing[l] = dot(perm[576:, :], fields[l]).astype(BF)
        copies.append(
            pltpu.make_async_remote_copy(
                src_ref=outgoing.at[l],
                dst_ref=got_ref.at[l],
                send_sem=send_sem.at[l],
                recv_sem=recv_sem.at[l],
                device_id=mate,
                device_id_type=MESH,
            )
        )
        copies[l].start()
    for l in range(3):
        keep_ref[l] = dot(perm[:576, :], fields[l]).astype(BF)
    j = div(column, 2.0)
    group = div(j, 3.0)
    i = div(row, 2.0)
    sub = 2.0 * (row - 2.0 * i) + column - 2.0 * j
    base = group * 224.0 + sub * 56.0 + (j - 3.0 * group) * 18.0 + i
    high = div(base, 16.0)
    low = base - 16.0 * high
    at = iota((128, PSH), 0)
    meta = jnp.where(at == 48.0, high, jnp.where(at == 49.0, low, 0.0)).astype(BF)
    meta_ref[...] = dot_nt(perm[0:576, :], meta).astype(BF)
    for copy in copies:
        copy.wait()


def sort_fields(order, fields):
    levels = pltpu.VMEM((3, 576, D), BF)
    return pl.pallas_call(
        sort_kernel,
        in_specs=[VMEM, ANY],
        out_specs=[VMEM, ANY, VMEM],
        out_shape=[
            jax.ShapeDtypeStruct((3, 576, D), BF),
            jax.ShapeDtypeStruct((3, 576, D), BF),
            jax.ShapeDtypeStruct((576, 128), BF),
        ],
        scratch_shapes=[
            pltpu.VMEM((PSH, PSH), BF),
            pltpu.VMEM((3, PSH, D), BF),
            levels,
            pltpu.SemaphoreType.DMA((3,)),
            pltpu.SemaphoreType.DMA((3,)),
            pltpu.SemaphoreType.DMA((3,)),
        ],
        compiler_params=params(60, collective_id=2, has_side_effects=True),
        name="sort_fields",
    )(order, fields)


def encode_tables(kv_ref, query_ref, score_w, spread_w, stat_w, pick):
    c = iota((128, D), 0)
    lane = iota((128, D), 1)
    a = div(c, 16.0)
    q = query_ref[...].astype(F32)
    chosen = jnp.where(a == 0.0, q[0:1], jnp.where(a == 1.0, q[1:2], q[2:3]))
    mine = (c - 16.0 * a == div(lane, 32.0)) & (c < 48.0)
    heads = jnp.where(mine, chosen, 0.0).astype(BF)
    folded = dot_nt(kv_ref[:, :D], heads) * (1.0 / math.sqrt(D // HEADS))
    high = folded.astype(BF)
    score_w[:, 0:128] = high
    score_w[:, 128:256] = (folded - high.astype(F32)).astype(BF)
    s = iota((128, 128), 0)
    t = iota((128, 128), 1)
    t = t - 64.0 * div(t, 64.0)
    for a in range(LATENT):
        spread_w[:, a * D : (a + 1) * D] = hot(c == 16.0 * a + div(lane, 32.0))
        for piece in range(3):
            here = (t >= 16.0 * piece) & (t < 16.0 * piece + 16.0)
            stat_w[piece * 128 : (piece + 1) * 128, a * 128 : (a + 1) * 128] = hot(
                here & (s == 16.0 * a + t - 16.0 * piece)
            )
        stat_w[384:512, a * 128 : (a + 1) * 128] = hot((t >= 48.0) & (t < 50.0) & (s == t))
    lane = iota((1, 6 * CHUNK), 1)
    kind = div(lane, float(CHUNK))
    slot = lane - kind * CHUNK
    stats = kind >= 3.0
    a = jnp.where(stats, kind - 3.0, kind)
    dest = div(slot, float(PER))
    k = a * PER + slot - dest * PER
    row = dest * MSG + jnp.where(stats, 27.0 + div(k, 8.0), k)
    for b in range(4):
        pick[b * 128 : (b + 1) * 128, :] = hot(iota((128, 6 * CHUNK), 0) + b * 128.0 == row)


def encode_chunk(xs, meta, kv_ref, score_w, spread_w, stat_w, pick, stack):
    scores = []
    for x in xs:
        both = dot(x, score_w[...])
        scores.append(both[:, :128] + both[:, 128:])
    peak = functools.reduce(jnp.maximum, scores)
    weights = [jnp.exp(s - peak) for s in scores]
    total = functools.reduce(jnp.add, weights)
    mixes = [jnp.zeros((CHUNK, D), F32)] * LATENT
    for x, w in zip(xs, weights):
        value = dot(x, kv_ref[:, D:]).astype(BF).astype(F32)
        wide = dot((w / total).astype(BF), spread_w[...])
        mixes = [m + wide[:, a * D : (a + 1) * D] * value for a, m in enumerate(mixes)]
    logsum = peak + jnp.log(total)
    high = logsum.astype(BF)
    rest = logsum - high.astype(F32)
    middle = rest.astype(BF)
    low = (rest - middle.astype(F32)).astype(BF)
    stats = dot(jnp.concatenate([high, middle, low, meta], axis=1), stat_w[...])
    slot = iota((CHUNK, D), 0)
    rank = slot - PER * div(slot, float(PER))
    block = div(iota((CHUNK, D), 1), 64.0)
    for a in range(LATENT):
        stack[a * CHUNK : (a + 1) * CHUNK, :] = mixes[a].astype(BF)
        k = rank + PER * a
        tiled = jnp.concatenate([stats[:, a * 128 : (a + 1) * 128]] * 4, axis=1)
        stack[(3 + a) * CHUNK : (4 + a) * CHUNK, :] = jnp.where(
            block == k - 8.0 * div(k, 8.0), tiled, 0.0
        ).astype(BF)
    return dot(pick[...], stack[...]).astype(BF)


def settle_tables(select, mask, fold):
    m = iota((256, 256), 0)
    k = m - MSG * div(m, float(MSG))
    select[...] = hot((k < 27.0) & (iota((256, 256), 1) == m - k + 27.0 + div(k, 8.0)))
    k = iota((256, D), 0)
    k = k - MSG * div(k, float(MSG))
    mask[...] = hot(div(iota((256, D), 1), 64.0) == k - 8.0 * div(k, 8.0))
    lane = iota((D, D), 0)
    lane = lane - 64.0 * div(lane, 64.0)
    fold[:, 0:D] = hot((lane < 48.0) & (lane - 16.0 * div(lane, 16.0) == div(iota((D, D), 1), 32.0)))
    lane = iota((D, 128), 0)
    lane = lane - 64.0 * div(lane, 64.0)
    fold[:, D : D + 128] = jnp.where(lane == 48.0, 16.0, jnp.where(lane == 49.0, 1.0, 0.0)).astype(BF)


def settle_chunk(values, query_ref, out_w_ref, select, mask, fold):
    stats = [(dot(select[...], v) * mask[...].astype(F32)).astype(BF) for v in values]
    logs = [dot(s, fold[:, 0:D]) for s in stats]
    peak = jnp.maximum(logs[0], logs[1])
    weights = [jnp.exp(l - peak) for l in logs]
    mixed = weights[0] * values[0].astype(F32) + weights[1] * values[1].astype(F32)
    encoded = (mixed / (weights[0] + weights[1])).astype(BF)
    q = query_ref[...].astype(F32)
    k = iota((256, D), 0)
    k = k - MSG * div(k, float(MSG))
    bias = jnp.where(k < 9.0, q[0:1], jnp.where(k < 18.0, q[1:2], q[2:3]))
    latents = (dot(encoded, out_w_ref[...]) + bias).astype(BF)
    k = k[:, 0:128]
    place = dot(stats[0], fold[:, D : D + 128]) + 6.0 * div(k, 9.0)
    place = jnp.where(k < 27.0, place, FAR)
    return latents, jnp.transpose(place)[0:8, :]


def encode_kernel(
    keep_ref,
    got_ref,
    meta_ref,
    kv_ref,
    query_ref,
    out_w_ref,
    grid_ref,
    own,
    mate,
    score_w,
    spread_w,
    stat_w,
    pick,
    stack,
    messages,
    landed,
    select,
    mask,
    fold,
    latents,
    rows,
    load_sem,
    send_sem,
    recv_sem,
):
    barrier = pltpu.get_barrier_semaphore()

    def load(i):
        part = pl.ds(pl.multiple_of(i * CHUNK, 16), CHUNK)
        return (
            pltpu.make_async_copy(keep_ref.at[:, part], own.at[:, part], load_sem.at[2 * i]),
            pltpu.make_async_copy(got_ref.at[:, part], mate.at[:, part], load_sem.at[2 * i + 1]),
        )

    for i in range(4):
        for part in load(i):
            part.start()

    @pl.loop(1, 64)
    def _(j):
        pl.semaphore_signal(barrier, inc=1, device_id=receiver(j), device_id_type=MESH)

    encode_tables(kv_ref, query_ref, score_w, spread_w, stat_w, pick)

    def copy(j):
        part = pl.ds(pl.multiple_of(j * MSG, MSG), MSG)
        return pltpu.make_async_remote_copy(
            src_ref=messages.at[part],
            dst_ref=landed.at[part],
            send_sem=send_sem.at[j],
            recv_sem=recv_sem.at[j],
            device_id=receiver(j),
            device_id_type=MESH,
        )

    def sixteen(i, act):
        @pl.loop(0, 16)
        def _(t):
            @pl.when(i * 16 + t > 0)
            def _():
                act(copy(i * 16 + t))

    @pl.loop(0, 4)
    def _(i):
        for part in load(i):
            part.wait()
        part = pl.ds(pl.multiple_of(i * CHUNK, 16), CHUNK)
        xs = [own[l, part, :] for l in range(3)] + [mate[l, part, :] for l in range(3)]
        messages[pl.ds(pl.multiple_of(i * 512, 512), 512), :] = encode_chunk(
            xs, meta_ref[part, :], kv_ref, score_w, spread_w, stat_w, pick, stack
        )

        @pl.when(i == 0)
        def _():
            landed[0:MSG, :] = messages[0:MSG, :]
            pl.semaphore_wait(barrier, 63)

        sixteen(i, lambda one: one.start())

    settle_tables(select, mask, fold)

    @pl.loop(0, 4)
    def _(i):
        sixteen(i, lambda one: one.wait())
        values = [
            landed[pl.ds(pl.multiple_of(i * 512 + g * 256, 256), 256), :] for g in range(2)
        ]
        done, place = settle_chunk(values, query_ref, out_w_ref, select, mask, fold)
        part = pl.ds(pl.multiple_of(i * 256, 256), 256)
        latents[part, :] = done
        rows[:, part] = place

    where = rows[0:1, :]
    for b in range(4):
        chosen = hot(iota((224, 1024), 0) + 224.0 * b == where)
        grid_ref[b * 224 : (b + 1) * 224, :] = dot(chosen, latents[...]).astype(BF)


def encode(keep, got, meta, enc_kv, latent_query, enc_out):
    levels = pltpu.VMEM((3, 576, D), BF)
    return pl.pallas_call(
        encode_kernel,
        in_specs=[HBM, HBM] + [VMEM] * 4,
        out_specs=VMEM,
        out_shape=jax.ShapeDtypeStruct((896, D), BF),
        scratch_shapes=[
            levels,
            levels,
            pltpu.VMEM((D, 256), BF),
            pltpu.VMEM((128, LATENT * D), BF),
            pltpu.VMEM((512, LATENT * 128), BF),
            pltpu.VMEM((16 * MSG, 6 * CHUNK), BF),
            pltpu.VMEM((6 * CHUNK, D), BF),
            pltpu.VMEM((64 * MSG, D), BF),
            pltpu.VMEM((64 * MSG, D), BF),
            pltpu.VMEM((256, 256), BF),
            pltpu.VMEM((256, D), BF),
            pltpu.VMEM((D, D + 128), BF),
            pltpu.VMEM((1024, D), BF),
            pltpu.VMEM((8, 1024), F32),
            pltpu.SemaphoreType.DMA((8,)),
            pltpu.SemaphoreType.DMA((64,)),
            pltpu.SemaphoreType.DMA((64,)),
        ],
        compiler_params=params(40, collective_id=0, has_side_effects=True),
        name="encode",
    )(keep, got, meta, enc_kv, latent_query, enc_out)


def normalize(values):
    offsets = values - jnp.mean(values, axis=-1, keepdims=True)
    spread = jnp.mean(offsets * offsets, axis=-1, keepdims=True)
    return offsets * lax.rsqrt(spread + epsilon)


def heads_of_group(qkv, out, g, width, valid):
    column = g * 128
    if not isinstance(g, int):
        column = pl.multiple_of(column, 128)
    q = qkv[:, pl.ds(column, 128)]
    k = qkv[:, pl.ds(width + column, 128)]
    v = qkv[:, pl.ds(2 * width + column, 128)]
    v = jnp.concatenate([v * valid, valid], axis=1)
    head = div(iota((1, 128), 1), 32.0)
    queries = jnp.concatenate([q * hot(head == float(h)) for h in range(4)], axis=0)
    scores = dot_nt(queries, k)
    scores = (scores - jnp.max(scores, axis=1, keepdims=True)) * (math.log2(math.e) / math.sqrt(32.0))
    mixed = dot(jnp.exp2(scores).astype(BF), v)
    head = jnp.concatenate([head, head], axis=1)
    total = mixed[0:224]
    for h in range(1, 4):
        total = jnp.where(head == float(h), mixed[h * 224 : (h + 1) * 224], total)
    out[:, pl.ds(column, 128)] = (total[:, :128] / total[:, 128:]).astype(BF)


def valid_keys(slots, valid):
    row = iota((224, 128), 0)
    return hot(row - slots * div(row, float(slots)) < valid)


def shift_starts(s):
    near = s.astype(F32)
    far = jnp.where(s <= 6, s + 12, s - 12).astype(F32)
    return near, far


class Links:
    def __init__(self, send, recv):
        lev = lax.axis_index("lev")
        win = lax.axis_index("win")
        self.send, self.recv = send, recv
        self.sides = (
            (lev, lax.rem(win + N_WIN - 1, N_WIN)),
            (lev, lax.rem(win + 1, N_WIN)),
        )

    def greet(self):
        barrier = pltpu.get_barrier_semaphore()
        for side in self.sides:
            pl.semaphore_signal(barrier, inc=1, device_id=side, device_id_type=MESH)
        pl.semaphore_wait(barrier, 2)

    def copy(self, side, sem, source, target):
        return pltpu.make_async_remote_copy(
            src_ref=source,
            dst_ref=target,
            send_sem=self.send.at[sem],
            recv_sem=self.recv.at[sem],
            device_id=self.sides[side],
            device_id_type=MESH,
        )

    def cells(self, base, own, halo):
        return (
            self.copy(0, base, own.at[pl.ds(0, 224)], halo.at[pl.ds(224, 224)]),
            self.copy(1, base + 1, own.at[pl.ds(672, 224)], halo.at[pl.ds(0, 224)]),
        )

    def results(self, base, band, results, land):
        first = pl.multiple_of(448 + band * 224, 16)
        return (
            self.copy(
                0,
                base + 2 * band,
                results.at[pl.ds(first, 112)],
                land.at[pl.ds(pl.multiple_of(224 + band * 112, 16), 112)],
            ),
            self.copy(
                1,
                base + 2 * band + 1,
                results.at[pl.ds(pl.multiple_of(first + 112, 16), 112)],
                land.at[pl.ds(pl.multiple_of(band * 112, 16), 112)],
            ),
        )


def shifted_windows(links, base, shift, own, halo, results, land, spread_ref, windows_ref, w_ref, proj_ref, x, qkv, mixed):
    near, far = shift_starts(shift)
    valid = valid_keys(112, 108)

    @pl.loop(0, 4)
    def _(step):
        band = step // 2
        outer = lax.rem((step + 1) // 2, 2)
        rows = pl.ds(pl.multiple_of((outer * 2 + band) * 224, 224), 224)
        target = windows_ref[rows, :] + 36.0 * jnp.where(outer == 0, near, far)
        x[...] = dot(hot(target == spread_ref[:, 0:896]), own[...])

        @pl.when(step == 1)
        def _():
            for copy in links.cells(base, own, halo):
                copy.wait()

        @pl.when(outer == 1)
        def _():
            x[...] += dot(hot(target == spread_ref[:, 896:1344]), halo[...])

        qkv[...] = dot(normalize(x[...]).astype(BF), w_ref[...]).astype(BF)
        for g in range(4):
            heads_of_group(qkv, mixed, g, D, valid)
        results[rows, :] = (x[...] + dot(mixed[...], proj_ref[...])).astype(BF)

        @pl.when(outer == 1)
        def _():
            for copy in links.results(base + 2, band, results, land):
                copy.start()


def held_ids(shift, held_ref):
    near, far = shift_starts(shift)
    return held_ref[0:1, :] + 36.0 * jnp.where(held_ref[1:2, :] > 0.5, near, far)


def gathered(target, ids, results, land):
    return dot(hot(target == ids[:, 0:896]), results[...]) + dot(
        hot(target == ids[:, 896:1344]), land[...]
    )


def unet_kernel(
    shift_ref,
    own_ref,
    spread_ref,
    windows_ref,
    held_ref,
    sub_ref,
    final_ref,
    qkv_a,
    proj_a,
    merge_w,
    qkv_b,
    proj_b,
    expand_w,
    qkv_c,
    proj_c,
    out_ref,
    qkv_a_v,
    proj_a_v,
    merge_v,
    qkv_b_v,
    proj_b_v,
    expand_v,
    qkv_c_v,
    proj_c_v,
    halo_a,
    halo_c,
    land_a,
    land_c,
    results,
    joined,
    first,
    x,
    qkv,
    mixed,
    qkv_wide,
    mixed_wide,
    send,
    recv,
    weight_sem,
):
    links = Links(send, recv)
    links.greet()
    for copy in links.cells(0, own_ref, halo_a):
        copy.start()
    pairs = [
        (qkv_a, qkv_a_v),
        (proj_a, proj_a_v),
        (merge_w, merge_v),
        (qkv_b, qkv_b_v),
        (proj_b, proj_b_v),
        (expand_w, expand_v),
        (qkv_c, qkv_c_v),
        (proj_c, proj_c_v),
    ]
    loads = [pltpu.make_async_copy(a, b, weight_sem.at[n]) for n, (a, b) in enumerate(pairs)]
    for load in loads:
        load.start()
    loads[0].wait()
    loads[1].wait()
    shift = shift_ref[0]
    shifted_windows(
        links, 0, shift, own_ref, halo_a, results, land_a, spread_ref, windows_ref, qkv_a_v, proj_a_v, x, qkv, mixed
    )
    for load in loads[2:]:
        load.wait()
    for band in range(2):
        for copy in links.results(2, band, results, land_a):
            copy.wait()

    ids = held_ids(shift, held_ref)
    total = jnp.zeros((224, 1), F32)
    for sub in range(4):
        rows = slice(sub * 224, (sub + 1) * 224)
        piece = gathered(sub_ref[rows, :], ids, results, land_a)
        first[rows, :] = piece.astype(BF)
        total = total + jnp.sum(piece, axis=1, keepdims=True)
    centre = total * (1.0 / (4 * D))
    spread = jnp.zeros((224, 1), F32)
    for sub in range(4):
        offsets = first[sub * 224 : (sub + 1) * 224, :].astype(F32) - centre
        spread = spread + jnp.sum(offsets * offsets, axis=1, keepdims=True)
    scale = lax.rsqrt(spread * (1.0 / (4 * D)) + epsilon)
    down = jnp.zeros((224, 2 * D), F32)
    for sub in range(4):
        offsets = first[sub * 224 : (sub + 1) * 224, :].astype(F32) - centre
        down = down + dot((offsets * scale).astype(BF), merge_v[sub * D : (sub + 1) * D, :])
    down = down.astype(BF).astype(F32)
    qkv_wide[...] = dot(normalize(down).astype(BF), qkv_b_v[...]).astype(BF)
    valid = valid_keys(56, 54)

    @pl.loop(0, 2)
    def _(step):
        for g in range(4):
            heads_of_group(qkv_wide, mixed_wide, step * 4 + g, 2 * D, valid)

    coarse = (down + dot(mixed_wide[...], proj_b_v[...])).astype(BF).astype(F32)
    normed = normalize(coarse).astype(BF)
    for sub in range(4):
        grown = dot(normed, expand_v[:, sub * D : (sub + 1) * D])
        grown = grown + first[sub * 224 : (sub + 1) * 224, :].astype(F32)
        for g in range(4):
            joined[g * 224 + sub * 56 : g * 224 + (sub + 1) * 56, :] = grown[g * 56 : (g + 1) * 56, :].astype(BF)

    for copy in links.cells(6, joined, halo_c):
        copy.start()
    shift = shift_ref[1]
    shifted_windows(
        links, 6, shift, joined, halo_c, results, land_c, spread_ref, windows_ref, qkv_c_v, proj_c_v, x, qkv, mixed
    )
    for band in range(2):
        for copy in links.results(8, band, results, land_c):
            copy.wait()
    ids = held_ids(shift, held_ref)
    for b in range(4):
        rows = slice(b * 216, (b + 1) * 216)
        out_ref[rows, :] = gathered(final_ref[rows, :], ids, results, land_c).astype(BF)


def unet(shifts, grid, weights):
    rows = lambda count, width=D: pltpu.VMEM((count, width), BF)
    return pl.pallas_call(
        unet_kernel,
        in_specs=[SMEM] + [VMEM] * 6 + [ANY] * 8,
        out_specs=VMEM,
        out_shape=jax.ShapeDtypeStruct((PLAT * LATENT * PLON, D), BF),
        scratch_shapes=[pltpu.VMEM(w.shape, BF) for w in weights]
        + [rows(448)] * 4
        + [rows(896)] * 3
        + [pltpu.VMEM((224, D), F32), rows(224, 3 * D), rows(224), rows(224, 6 * D), rows(224, 2 * D)]
        + [pltpu.SemaphoreType.DMA((12,)), pltpu.SemaphoreType.DMA((12,)), pltpu.SemaphoreType.DMA((8,))],
        compiler_params=params(44, collective_id=1, has_side_effects=True),
        name="unet",
    )(shifts, grid, *tables(), *weights)


def local(
    fields,
    patch_order,
    shift_offsets,
    latent_query,
    enc_kv,
    enc_out,
    qkv_a,
    proj_a,
    merge_w,
    qkv_b,
    proj_b,
    expand_w,
    qkv_c,
    proj_c,
):
    keep, got, meta = sort_fields(patch_order.reshape(288, 128), fields)
    grid = encode(keep, got, meta, enc_kv, latent_query, enc_out)
    weights = (qkv_a, proj_a, merge_w, qkv_b, proj_b, expand_w, qkv_c, proj_c)
    result = unet(shift_offsets, grid, weights)
    return result.reshape(PLAT, LATENT, PLON, D).transpose(0, 2, 1, 3)


def solution(mesh):
    placed = (P("lev", "win", None),) + (P(),) * 13
    return jax.shard_map(
        local, mesh=mesh, in_specs=placed, out_specs=P("lev", "win", None, None), check_vma=False
    )
```

```python
import functools
import math

import jax
import jax.numpy as jnp
import numpy as np
from jax import lax
from jax.experimental import pallas as pl
from jax.experimental.pallas import tpu as pltpu
from jax.sharding import PartitionSpec as P

D = 512
HEADS = 16
LATENT = 3
PLAT = 12
PLON = 24
N_LEV = 4
N_WIN = 32
PSH = 1152
PER = 9
MSG = 32
CHUNK = 144
epsilon = 1e-05
BF = jnp.bfloat16
F32 = jnp.float32
MESH = pl.DeviceIdType.MESH
FAR = -1.0e6
VMEM = pl.BlockSpec(memory_space=pltpu.VMEM)
SMEM = pl.BlockSpec(memory_space=pltpu.SMEM)
ANY = pl.BlockSpec(memory_space=pl.ANY)


def params(mib=60, **more):
    return pltpu.CompilerParams(vmem_limit_bytes=mib << 20, **more)


def dot(a, b):
    return jnp.dot(a, b, preferred_element_type=F32)


def dot_nt(a, b):
    return lax.dot_general(a, b, (((1,), (1,)), ((), ())), preferred_element_type=F32)


def iota(shape, axis):
    return lax.broadcasted_iota(jnp.int32, shape, axis).astype(F32)


def div(values, by):
    return jnp.floor((values + 0.5) * (1.0 / by))


def hot(condition):
    return jnp.where(condition, 1.0, 0.0).astype(BF)


def group_ids(first_column, spare=None):
    ids = np.zeros((4, 56), np.float32)
    for sub in range(4):
        for q in range(56):
            p = min(q, 53)
            column = first_column + 2 * (p // 18) + (sub & 1)
            ids[sub, q] = column * 36 + (2 * (p % 6) + (sub >> 1)) * 3 + p % 18 // 6
    if spare is not None:
        ids[:, 54:] = spare
    return ids


def half_ids(band, first_column, spare=None):
    ids = np.zeros((112,), np.float32)
    for q in range(112):
        p = min(q, 107)
        ids[q] = (first_column + p // 18) * 36 + (band * 6 + p % 6) * 3 + p % 18 // 6
    if spare is not None:
        ids[108:] = spare
    return ids


def tables():
    groups = [group_ids(6 * g, FAR).reshape(-1) for g in range(-1, 5)]
    spread = np.concatenate(groups[1:5] + [groups[0], groups[5]])
    windows = np.concatenate(
        [np.concatenate([half_ids(b, 0), half_ids(b, 6)]) for _ in range(2) for b in range(2)]
    )
    held = np.zeros((8, 1344), np.float32)
    held[0] = np.concatenate(
        [np.concatenate([half_ids(b, 0, FAR), half_ids(b, 6, FAR)]) for _ in range(2) for b in range(2)]
        + [half_ids(b, 6 - PLON, FAR) for b in range(2)]
        + [half_ids(b, PLON, FAR) for b in range(2)]
    )
    held[1, :448] = 1.0
    by_sub = np.stack([group_ids(6 * g) for g in range(4)], axis=1).reshape(-1)
    final = np.zeros((PLAT, LATENT, PLON), np.float32)
    for r in range(PLAT):
        for a in range(LATENT):
            for c in range(PLON):
                final[r, a, c] = c * 36 + r * 3 + a
    return (
        jnp.asarray(spread[None]),
        jnp.asarray(windows[:, None]),
        jnp.asarray(held),
        jnp.asarray(by_sub[:, None]),
        jnp.asarray(final.reshape(-1, 1)),
    )


def place_of_me():
    lev = lax.axis_index("lev")
    win = lax.axis_index("win")
    return lev // 2, win // 8, lax.rem(win // 4, 2), lax.rem(win, 4), lax.rem(lev, 2)


def receiver(j):
    half, x, low, y, core = place_of_me()
    k = lax.rem(((j // 16) * 8 + lax.rem(j, 8)) * 11, 32)
    half = lax.rem(half + lax.rem(j // 8, 2), 2)
    x = lax.rem(x + k // 8, 4)
    low = lax.rem(low + lax.rem(k // 4, 2), 2)
    y = lax.rem(y + lax.rem(k, 4), 4)
    return (half * 2 + core, x * 8 + low * 4 + y)


def message_of(half, shard):
    my_half, my_x, my_low, my_y, _ = (value.astype(F32) for value in place_of_me())
    x = div(shard, 8.0)
    y = shard - 8.0 * x
    low = div(y, 4.0)
    y = y - 4.0 * low
    x = x - my_x + 4.0
    x = x - 4.0 * div(x, 4.0)
    y = y - my_y + 4.0
    y = y - 4.0 * div(y, 4.0)
    pair = 3.0 * (8.0 * x + 4.0 * jnp.abs(low - my_low) + y)
    pair = pair - 32.0 * div(pair, 32.0)
    block = div(pair, 8.0)
    return block * 16.0 + 8.0 * jnp.abs(half - my_half) + pair - 8.0 * block


def sort_slots(order_ref, perm):
    win = lax.axis_index("win")
    core = lax.rem(lax.axis_index("lev"), 2).astype(F32)
    p = jnp.concatenate([order_ref[pl.ds(9 * win + r, 1), :] for r in range(9)], axis=1).astype(F32)
    row = div(p, 768.0)
    column = p - row * 768.0
    band = div(row, 12.0)
    shard = div(column, 24.0)
    row = row - band * 12.0
    column = column - shard * 24.0
    half = div(band, 2.0)
    key = jnp.abs(band - 2.0 * half - core) * 64.0 + message_of(half, shard)
    member = hot(iota((128, PSH), 0) == key)
    upper = hot(iota((128, 128), 0) < iota((128, 128), 1))
    seen = jnp.zeros((128, 1), F32)
    ranks = []
    for b in range(PSH // 128):
        piece = member[:, b * 128 : (b + 1) * 128]
        wide = piece.astype(F32)
        ranks.append(jnp.sum(wide * (dot(piece, upper) + seen), axis=0, keepdims=True))
        seen = seen + jnp.sum(wide, axis=1, keepdims=True)
    target = key * PER + jnp.concatenate(ranks, axis=1)
    for b in range(PSH // 128):
        perm[b * 128 : (b + 1) * 128, :] = hot(iota((128, PSH), 0) + b * 128.0 == target)
    j = div(column, 2.0)
    group = div(j, 3.0)
    i = div(row, 2.0)
    sub = 2.0 * (row - 2.0 * i) + column - 2.0 * j
    base = group * 224.0 + sub * 56.0 + (j - 3.0 * group) * 18.0 + i
    high = div(base, 16.0)
    low = base - 16.0 * high
    at = iota((128, PSH), 0)
    return jnp.where(at == 48.0, high, jnp.where(at == 49.0, low, 0.0)).astype(BF)


def encode_tables(kv_ref, query_ref, score_w, spread_w, stat_w, pick):
    c = iota((128, D), 0)
    lane = iota((128, D), 1)
    a = div(c, 16.0)
    q = query_ref[...].astype(F32)
    chosen = jnp.where(a == 0.0, q[0:1], jnp.where(a == 1.0, q[1:2], q[2:3]))
    mine = (c - 16.0 * a == div(lane, 32.0)) & (c < 48.0)
    heads = jnp.where(mine, chosen, 0.0).astype(BF)
    folded = dot_nt(kv_ref[:, :D], heads) * (1.0 / math.sqrt(D // HEADS))
    high = folded.astype(BF)
    score_w[:, 0:128] = high
    score_w[:, 128:256] = (folded - high.astype(F32)).astype(BF)
    s = iota((128, 128), 0)
    t = iota((128, 128), 1)
    t = t - 64.0 * div(t, 64.0)
    for a in range(LATENT):
        spread_w[:, a * D : (a + 1) * D] = hot(c == 16.0 * a + div(lane, 32.0))
        for piece in range(3):
            here = (t >= 16.0 * piece) & (t < 16.0 * piece + 16.0)
            stat_w[piece * 128 : (piece + 1) * 128, a * 128 : (a + 1) * 128] = hot(
                here & (s == 16.0 * a + t - 16.0 * piece)
            )
        stat_w[384:512, a * 128 : (a + 1) * 128] = hot((t >= 48.0) & (t < 50.0) & (s == t))
    lane = iota((1, 6 * CHUNK), 1)
    kind = div(lane, float(CHUNK))
    slot = lane - kind * CHUNK
    stats = kind >= 3.0
    a = jnp.where(stats, kind - 3.0, kind)
    dest = div(slot, float(PER))
    k = a * PER + slot - dest * PER
    row = dest * MSG + jnp.where(stats, 27.0 + div(k, 8.0), k)
    for b in range(4):
        pick[b * 128 : (b + 1) * 128, :] = hot(iota((128, 6 * CHUNK), 0) + b * 128.0 == row)


def encode_chunk(xs, meta, kv_ref, score_w, spread_w, stat_w, pick, stack):
    scores = []
    for x in xs:
        both = dot(x, score_w[...])
        scores.append(both[:, :128] + both[:, 128:])
    peak = functools.reduce(jnp.maximum, scores)
    weights = [jnp.exp(s - peak) for s in scores]
    total = functools.reduce(jnp.add, weights)
    mixes = [jnp.zeros((CHUNK, D), F32)] * LATENT
    for x, w in zip(xs, weights):
        value = dot(x, kv_ref[:, D:]).astype(BF).astype(F32)
        wide = dot((w / total).astype(BF), spread_w[...])
        mixes = [m + wide[:, a * D : (a + 1) * D] * value for a, m in enumerate(mixes)]
    logsum = peak + jnp.log(total)
    high = logsum.astype(BF)
    rest = logsum - high.astype(F32)
    middle = rest.astype(BF)
    low = (rest - middle.astype(F32)).astype(BF)
    stats = dot(jnp.concatenate([high, middle, low, meta], axis=1), stat_w[...])
    slot = iota((CHUNK, D), 0)
    rank = slot - PER * div(slot, float(PER))
    block = div(iota((CHUNK, D), 1), 64.0)
    for a in range(LATENT):
        stack[a * CHUNK : (a + 1) * CHUNK, :] = mixes[a].astype(BF)
        k = rank + PER * a
        tiled = jnp.concatenate([stats[:, a * 128 : (a + 1) * 128]] * 4, axis=1)
        stack[(3 + a) * CHUNK : (4 + a) * CHUNK, :] = jnp.where(
            block == k - 8.0 * div(k, 8.0), tiled, 0.0
        ).astype(BF)
    return dot(pick[...], stack[...]).astype(BF)


def settle_tables(select, mask, fold):
    m = iota((256, 256), 0)
    k = m - MSG * div(m, float(MSG))
    select[...] = hot((k < 27.0) & (iota((256, 256), 1) == m - k + 27.0 + div(k, 8.0)))
    k = iota((256, D), 0)
    k = k - MSG * div(k, float(MSG))
    mask[...] = hot(div(iota((256, D), 1), 64.0) == k - 8.0 * div(k, 8.0))
    lane = iota((D, D), 0)
    lane = lane - 64.0 * div(lane, 64.0)
    fold[:, 0:D] = hot((lane < 48.0) & (lane - 16.0 * div(lane, 16.0) == div(iota((D, D), 1), 32.0)))
    lane = iota((D, 128), 0)
    lane = lane - 64.0 * div(lane, 64.0)
    fold[:, D : D + 128] = jnp.where(lane == 48.0, 16.0, jnp.where(lane == 49.0, 1.0, 0.0)).astype(BF)


def settle_chunk(values, query_ref, out_w_ref, select, mask, fold):
    stats = [(dot(select[...], v) * mask[...].astype(F32)).astype(BF) for v in values]
    logs = [dot(s, fold[:, 0:D]) for s in stats]
    peak = jnp.maximum(logs[0], logs[1])
    weights = [jnp.exp(l - peak) for l in logs]
    mixed = weights[0] * values[0].astype(F32) + weights[1] * values[1].astype(F32)
    encoded = (mixed / (weights[0] + weights[1])).astype(BF)
    q = query_ref[...].astype(F32)
    k = iota((256, D), 0)
    k = k - MSG * div(k, float(MSG))
    bias = jnp.where(k < 9.0, q[0:1], jnp.where(k < 18.0, q[1:2], q[2:3]))
    latents = (dot(encoded, out_w_ref[...]) + bias).astype(BF)
    k = k[:, 0:128]
    place = dot(stats[0], fold[:, D : D + 128]) + 6.0 * div(k, 9.0)
    place = jnp.where(k < 27.0, place, FAR)
    return latents, jnp.transpose(place)[0:8, :]


def level_partials(
    order_ref,
    fields_ref,
    kv_ref,
    query_ref,
    out_w_ref,
    grid,
    links,
    halo,
    weight_loads,
    perm,
    fields,
    outgoing,
    own,
    mate,
    meta,
    score_w,
    spread_w,
    stat_w,
    pick,
    stack,
    messages,
    landed,
    select,
    mask,
    fold,
    latents,
    rows,
    level_load,
    level_send,
    level_recv,
    send_sem,
    recv_sem,
):
    lev = lax.axis_index("lev")
    other = (lev + 1 - 2 * lax.rem(lev, 2), lax.axis_index("win"))
    loads = [
        pltpu.make_async_copy(fields_ref.at[l], fields.at[l], level_load.at[l]) for l in range(3)
    ]
    for load in loads + weight_loads[:7]:
        load.start()
    barrier = pltpu.get_barrier_semaphore()
    pl.semaphore_signal(barrier, inc=1, device_id=other, device_id_type=MESH)

    @pl.loop(1, 64)
    def _(j):
        pl.semaphore_signal(barrier, inc=1, device_id=receiver(j), device_id_type=MESH)

    places = sort_slots(order_ref, perm)
    pl.semaphore_wait(barrier, 64)
    copies = []
    for l in range(3):
        loads[l].wait()
        outgoing[l] = dot(perm[576:, :], fields[l]).astype(BF)
        copies.append(
            pltpu.make_async_remote_copy(
                src_ref=outgoing.at[l],
                dst_ref=mate.at[l],
                send_sem=level_send.at[l],
                recv_sem=level_recv.at[l],
                device_id=other,
                device_id_type=MESH,
            )
        )
        copies[l].start()
    for l in range(3):
        own[l] = dot(perm[:576, :], fields[l]).astype(BF)
    for load in weight_loads[7:]:
        load.start()
    meta[...] = dot_nt(perm[0:576, :], places).astype(BF)
    for load in weight_loads[:2]:
        load.wait()
    encode_tables(kv_ref, query_ref, score_w, spread_w, stat_w, pick)
    for one in copies:
        one.wait()

    def copy(j):
        part = pl.ds(pl.multiple_of(j * MSG, MSG), MSG)
        return pltpu.make_async_remote_copy(
            src_ref=messages.at[part],
            dst_ref=landed.at[part],
            send_sem=send_sem.at[j],
            recv_sem=recv_sem.at[j],
            device_id=receiver(j),
            device_id_type=MESH,
        )

    def sixteen(i, act):
        @pl.loop(0, 16)
        def _(t):
            @pl.when(i * 16 + t > 0)
            def _():
                act(copy(i * 16 + t))

    @pl.loop(0, 4)
    def _(i):
        part = pl.ds(pl.multiple_of(i * CHUNK, 16), CHUNK)
        xs = [own[l, part, :] for l in range(3)] + [mate[l, part, :] for l in range(3)]
        messages[pl.ds(pl.multiple_of(i * 512, 512), 512), :] = encode_chunk(
            xs, meta[part, :], kv_ref, score_w, spread_w, stat_w, pick, stack
        )
        sixteen(i, lambda one: one.start())

    landed[0:MSG, :] = messages[0:MSG, :]
    settle_tables(select, mask, fold)

    @pl.loop(0, 4)
    def _(i):
        sixteen(i, lambda one: one.wait())
        values = [
            landed[pl.ds(pl.multiple_of(i * 512 + g * 256, 256), 256), :] for g in range(2)
        ]
        done, place = settle_chunk(values, query_ref, out_w_ref, select, mask, fold)
        part = pl.ds(pl.multiple_of(i * 256, 256), 256)
        latents[part, :] = done
        rows[:, part] = place

    where = rows[0:1, :]
    for n, b in enumerate((0, 3, 1, 2)):
        chosen = hot(iota((224, 1024), 0) + 224.0 * b == where)
        grid[b * 224 : (b + 1) * 224, :] = dot(chosen, latents[...]).astype(BF)
        if n == 1:
            for one in links.cells(0, grid, halo):
                one.start()


def partial_scratch():
    levels = pltpu.VMEM((3, 576, D), BF)
    return [
        pltpu.VMEM((PSH, PSH), BF),
        pltpu.VMEM((3, PSH, D), BF),
        levels,
        levels,
        levels,
        pltpu.VMEM((576, 128), BF),
        pltpu.VMEM((D, 256), BF),
        pltpu.VMEM((128, LATENT * D), BF),
        pltpu.VMEM((512, LATENT * 128), BF),
        pltpu.VMEM((16 * MSG, 6 * CHUNK), BF),
        pltpu.VMEM((6 * CHUNK, D), BF),
        pltpu.VMEM((64 * MSG, D), BF),
        pltpu.VMEM((64 * MSG, D), BF),
        pltpu.VMEM((256, 256), BF),
        pltpu.VMEM((256, D), BF),
        pltpu.VMEM((D, D + 128), BF),
        pltpu.VMEM((1024, D), BF),
        pltpu.VMEM((8, 1024), F32),
        pltpu.SemaphoreType.DMA((3,)),
        pltpu.SemaphoreType.DMA((3,)),
        pltpu.SemaphoreType.DMA((3,)),
        pltpu.SemaphoreType.DMA((64,)),
        pltpu.SemaphoreType.DMA((64,)),
    ]


def normalize(values):
    offsets = values - jnp.mean(values, axis=-1, keepdims=True)
    spread = jnp.mean(offsets * offsets, axis=-1, keepdims=True)
    return offsets * lax.rsqrt(spread + epsilon)


def heads_of_group(qkv, out, g, width, valid):
    column = g * 128
    if not isinstance(g, int):
        column = pl.multiple_of(column, 128)
    q = qkv[:, pl.ds(column, 128)]
    k = qkv[:, pl.ds(width + column, 128)]
    v = qkv[:, pl.ds(2 * width + column, 128)]
    v = jnp.concatenate([v * valid, valid], axis=1)
    head = div(iota((1, 128), 1), 32.0)
    queries = jnp.concatenate([q * hot(head == float(h)) for h in range(4)], axis=0)
    scores = dot_nt(queries, k)
    scores = (scores - jnp.max(scores, axis=1, keepdims=True)) * (math.log2(math.e) / math.sqrt(32.0))
    mixed = dot(jnp.exp2(scores).astype(BF), v)
    head = jnp.concatenate([head, head], axis=1)
    total = mixed[0:224]
    for h in range(1, 4):
        total = jnp.where(head == float(h), mixed[h * 224 : (h + 1) * 224], total)
    out[:, pl.ds(column, 128)] = (total[:, :128] / total[:, 128:]).astype(BF)


def valid_keys(slots, valid):
    row = iota((224, 128), 0)
    return hot(row - slots * div(row, float(slots)) < valid)


def shift_starts(s):
    near = s.astype(F32)
    far = jnp.where(s <= 6, s + 12, s - 12).astype(F32)
    return near, far


class Links:
    def __init__(self, send, recv):
        lev = lax.axis_index("lev")
        win = lax.axis_index("win")
        self.send, self.recv = send, recv
        self.sides = (
            (lev, lax.rem(win + N_WIN - 1, N_WIN)),
            (lev, lax.rem(win + 1, N_WIN)),
        )

    def copy(self, side, sem, source, target):
        return pltpu.make_async_remote_copy(
            src_ref=source,
            dst_ref=target,
            send_sem=self.send.at[sem],
            recv_sem=self.recv.at[sem],
            device_id=self.sides[side],
            device_id_type=MESH,
        )

    def cells(self, base, own, halo):
        return (
            self.copy(0, base, own.at[pl.ds(0, 224)], halo.at[pl.ds(224, 224)]),
            self.copy(1, base + 1, own.at[pl.ds(672, 224)], halo.at[pl.ds(0, 224)]),
        )

    def results(self, base, band, results, land):
        first = pl.multiple_of(448 + band * 224, 16)
        return (
            self.copy(
                0,
                base + 2 * band,
                results.at[pl.ds(first, 112)],
                land.at[pl.ds(pl.multiple_of(224 + band * 112, 16), 112)],
            ),
            self.copy(
                1,
                base + 2 * band + 1,
                results.at[pl.ds(pl.multiple_of(first + 112, 16), 112)],
                land.at[pl.ds(pl.multiple_of(band * 112, 16), 112)],
            ),
        )


def shifted_windows(links, base, shift, own, halo, results, land, spread_ref, windows_ref, w_ref, proj_ref, x, qkv, mixed):
    near, far = shift_starts(shift)
    valid = valid_keys(112, 108)

    @pl.loop(0, 4)
    def _(step):
        band = step // 2
        outer = lax.rem((step + 1) // 2, 2)
        rows = pl.ds(pl.multiple_of((outer * 2 + band) * 224, 224), 224)
        target = windows_ref[rows, :] + 36.0 * jnp.where(outer == 0, near, far)
        x[...] = dot(hot(target == spread_ref[:, 0:896]), own[...])

        @pl.when(step == 1)
        def _():
            for copy in links.cells(base, own, halo):
                copy.wait()

        @pl.when(outer == 1)
        def _():
            x[...] += dot(hot(target == spread_ref[:, 896:1344]), halo[...])

        qkv[...] = dot(normalize(x[...]).astype(BF), w_ref[...]).astype(BF)
        for g in range(4):
            heads_of_group(qkv, mixed, g, D, valid)
        results[rows, :] = (x[...] + dot(mixed[...], proj_ref[...])).astype(BF)

        @pl.when(outer == 1)
        def _():
            for copy in links.results(base + 2, band, results, land):
                copy.start()


def held_ids(shift, held_ref):
    near, far = shift_starts(shift)
    return held_ref[0:1, :] + 36.0 * jnp.where(held_ref[1:2, :] > 0.5, near, far)


def gathered(target, ids, results, land):
    return dot(hot(target == ids[:, 0:896]), results[...]) + dot(
        hot(target == ids[:, 896:1344]), land[...]
    )


def step_kernel(shift_ref, order_ref, query_ref, fields_ref, *refs):
    early, late = refs[:7], refs[7:15]
    out_ref = refs[15]
    kv, out_w, spread_ref, windows_ref, held_ref, sub_ref, final_ref = refs[16:23]
    qkv_a_v, proj_a_v, merge_v, qkv_b_v, proj_b_v, expand_v, qkv_c_v, proj_c_v = refs[23:31]
    halo_a, halo_c, land_a, land_c, x, qkv, mixed, qkv_wide, mixed_wide, send, recv, load_sem, grid = refs[31:44]
    encoder = refs[44:]
    fields = encoder[1]
    results, joined, first = (fields.at[l, pl.ds(0, 896)] for l in range(3))
    links = Links(send, recv)
    loads = [
        pltpu.make_async_copy(a, b, load_sem.at[n])
        for n, (a, b) in enumerate(zip(early + late, refs[16:31]))
    ]
    level_partials(
        order_ref, fields_ref, kv, query_ref, out_w, grid, links, halo_a, loads, *encoder
    )
    for load in loads[2:]:
        load.wait()
    shift = shift_ref[0]
    shifted_windows(
        links, 0, shift, grid, halo_a, results, land_a, spread_ref, windows_ref, qkv_a_v, proj_a_v, x, qkv, mixed
    )
    for band in range(2):
        for copy in links.results(2, band, results, land_a):
            copy.wait()

    ids = held_ids(shift, held_ref)
    total = jnp.zeros((224, 1), F32)
    for sub in range(4):
        rows = slice(sub * 224, (sub + 1) * 224)
        piece = gathered(sub_ref[rows, :], ids, results, land_a)
        first[rows, :] = piece.astype(BF)
        total = total + jnp.sum(piece, axis=1, keepdims=True)
    centre = total * (1.0 / (4 * D))
    spread = jnp.zeros((224, 1), F32)
    for sub in range(4):
        offsets = first[sub * 224 : (sub + 1) * 224, :].astype(F32) - centre
        spread = spread + jnp.sum(offsets * offsets, axis=1, keepdims=True)
    scale = lax.rsqrt(spread * (1.0 / (4 * D)) + epsilon)
    down = jnp.zeros((224, 2 * D), F32)
    for sub in range(4):
        offsets = first[sub * 224 : (sub + 1) * 224, :].astype(F32) - centre
        down = down + dot((offsets * scale).astype(BF), merge_v[sub * D : (sub + 1) * D, :])
    down = down.astype(BF).astype(F32)
    qkv_wide[...] = dot(normalize(down).astype(BF), qkv_b_v[...]).astype(BF)
    valid = valid_keys(56, 54)

    @pl.loop(0, 2)
    def _(step):
        for g in range(4):
            heads_of_group(qkv_wide, mixed_wide, step * 4 + g, 2 * D, valid)

    coarse = (down + dot(mixed_wide[...], proj_b_v[...])).astype(BF).astype(F32)
    normed = normalize(coarse).astype(BF)
    for sub in range(4):
        grown = dot(normed, expand_v[:, sub * D : (sub + 1) * D])
        grown = grown + first[sub * 224 : (sub + 1) * 224, :].astype(F32)
        for g in range(4):
            joined[g * 224 + sub * 56 : g * 224 + (sub + 1) * 56, :] = grown[g * 56 : (g + 1) * 56, :].astype(BF)

    for copy in links.cells(6, joined, halo_c):
        copy.start()
    shift = shift_ref[1]
    shifted_windows(
        links, 6, shift, joined, halo_c, results, land_c, spread_ref, windows_ref, qkv_c_v, proj_c_v, x, qkv, mixed
    )
    for band in range(2):
        for copy in links.results(8, band, results, land_c):
            copy.wait()
    ids = held_ids(shift, held_ref)
    for b in range(4):
        rows = slice(b * 216, (b + 1) * 216)
        out_ref[rows, :] = gathered(final_ref[rows, :], ids, results, land_c).astype(BF)


def step(shifts, order, latent_query, fields, held):
    rows = lambda count, width=D: pltpu.VMEM((count, width), BF)
    return pl.pallas_call(
        step_kernel,
        in_specs=[SMEM, VMEM, VMEM] + [ANY] * (1 + len(held)),
        out_specs=VMEM,
        out_shape=jax.ShapeDtypeStruct((PLAT * LATENT * PLON, D), BF),
        scratch_shapes=[pltpu.VMEM(w.shape, w.dtype) for w in held]
        + [rows(448)] * 4
        + [pltpu.VMEM((224, D), F32), rows(224, 3 * D), rows(224), rows(224, 6 * D), rows(224, 2 * D)]
        + [pltpu.SemaphoreType.DMA((12,)), pltpu.SemaphoreType.DMA((12,)), pltpu.SemaphoreType.DMA((15,))]
        + [rows(896)]
        + partial_scratch(),
        compiler_params=params(62, collective_id=0, has_side_effects=True),
        name="step",
    )(shifts, order, latent_query, fields, *held)


def local(
    fields,
    patch_order,
    shift_offsets,
    latent_query,
    enc_kv,
    enc_out,
    qkv_a,
    proj_a,
    merge_w,
    qkv_b,
    proj_b,
    expand_w,
    qkv_c,
    proj_c,
):
    held = (enc_kv, enc_out) + tables()
    held = held + (qkv_a, proj_a, merge_w, qkv_b, proj_b, expand_w, qkv_c, proj_c)
    result = step(shift_offsets, patch_order.reshape(288, 128), latent_query, fields, held)
    return result.reshape(PLAT, LATENT, PLON, D).transpose(0, 2, 1, 3)


def solution(mesh):
    placed = (P("lev", "win", None),) + (P(),) * 13
    return jax.shard_map(
        local, mesh=mesh, in_specs=placed, out_specs=P("lev", "win", None, None), check_vma=False
    )
```

```python
import functools
import math

import jax
import jax.numpy as jnp
import numpy as np
from jax import lax
from jax.experimental import pallas as pl
from jax.experimental.pallas import tpu as pltpu
from jax.sharding import PartitionSpec as P

D = 512
HEADS = 16
LATENT = 3
PLAT = 12
PLON = 24
N_LEV = 4
N_WIN = 32
PSH = 1152
PER = 9
MSG = 32
CHUNK = 144
epsilon = 1e-05
BF = jnp.bfloat16
F32 = jnp.float32
MESH = pl.DeviceIdType.MESH
FAR = -1.0e6
VMEM = pl.BlockSpec(memory_space=pltpu.VMEM)
SMEM = pl.BlockSpec(memory_space=pltpu.SMEM)
ANY = pl.BlockSpec(memory_space=pl.ANY)


def params(mib=60, **more):
    return pltpu.CompilerParams(vmem_limit_bytes=mib << 20, **more)


def dot(a, b):
    return jnp.dot(a, b, preferred_element_type=F32)


def dot_nt(a, b):
    return lax.dot_general(a, b, (((1,), (1,)), ((), ())), preferred_element_type=F32)


def iota(shape, axis):
    return lax.broadcasted_iota(jnp.int32, shape, axis).astype(F32)


def div(values, by):
    return jnp.floor((values + 0.5) * (1.0 / by))


def hot(condition):
    return jnp.where(condition, 1.0, 0.0).astype(BF)


def group_ids(first_column, spare=None):
    ids = np.zeros((4, 56), np.float32)
    for sub in range(4):
        for q in range(56):
            p = min(q, 53)
            column = first_column + 2 * (p // 18) + (sub & 1)
            ids[sub, q] = column * 36 + (2 * (p % 6) + (sub >> 1)) * 3 + p % 18 // 6
    if spare is not None:
        ids[:, 54:] = spare
    return ids


def half_ids(band, first_column, spare=None):
    ids = np.zeros((112,), np.float32)
    for q in range(112):
        p = min(q, 107)
        ids[q] = (first_column + p // 18) * 36 + (band * 6 + p % 6) * 3 + p % 18 // 6
    if spare is not None:
        ids[108:] = spare
    return ids


def tables():
    groups = [group_ids(6 * g, FAR).reshape(-1) for g in range(-1, 5)]
    spread = np.concatenate(groups[1:5] + [groups[0], groups[5]])
    windows = np.concatenate(
        [np.concatenate([half_ids(b, 0), half_ids(b, 6)]) for _ in range(2) for b in range(2)]
    )
    held = np.zeros((8, 1344), np.float32)
    held[0] = np.concatenate(
        [np.concatenate([half_ids(b, 0, FAR), half_ids(b, 6, FAR)]) for _ in range(2) for b in range(2)]
        + [half_ids(b, 6 - PLON, FAR) for b in range(2)]
        + [half_ids(b, PLON, FAR) for b in range(2)]
    )
    held[1, :448] = 1.0
    by_sub = np.stack([group_ids(6 * g) for g in range(4)], axis=1).reshape(-1)
    final = np.zeros((PLAT, LATENT, PLON), np.float32)
    for r in range(PLAT):
        for a in range(LATENT):
            for c in range(PLON):
                final[r, a, c] = c * 36 + r * 3 + a
    return (
        jnp.asarray(spread[None]),
        jnp.asarray(windows[:, None]),
        jnp.asarray(held),
        jnp.asarray(by_sub[:, None]),
        jnp.asarray(final.reshape(-1, 1)),
    )


def place_of_me():
    lev = lax.axis_index("lev")
    win = lax.axis_index("win")
    return lev // 2, win // 8, lax.rem(win // 4, 2), lax.rem(win, 4), lax.rem(lev, 2)


class Receivers:
    def __init__(self):
        half, x, low, self.y, core = place_of_me()
        self.levs = [lax.rem(half + z, 2) * 2 + core for z in range(2)]
        xs = [lax.rem(x + d, 4) * 8 for d in range(4)]
        lows = [lax.rem(low + d, 2) * 4 for d in range(2)]
        self.bases = [xs[p % 4] + lows[p // 4] for p in range(8)]

    def of(self, i, z, p):
        return (self.levs[z], self.bases[p] + lax.rem(self.y + i + p, 4))


def message_of(half, shard):
    my_half, my_x, my_low, my_y, _ = (value.astype(F32) for value in place_of_me())
    x = div(shard, 8.0)
    y = shard - 8.0 * x
    low = div(y, 4.0)
    y = y - 4.0 * low
    x = x - my_x + 4.0
    x = x - 4.0 * div(x, 4.0)
    i = y - my_y - x + 8.0
    i = i - 4.0 * div(i, 4.0)
    return 16.0 * i + 8.0 * jnp.abs(half - my_half) + x + 4.0 * jnp.abs(low - my_low)


def sort_slots(order_ref, perm, greetings):
    win = lax.axis_index("win")
    core = lax.rem(lax.axis_index("lev"), 2).astype(F32)
    p = jnp.concatenate([order_ref[pl.ds(9 * win + r, 1), :] for r in range(9)], axis=1).astype(F32)
    row = div(p, 768.0)
    column = p - row * 768.0
    band = div(row, 12.0)
    shard = div(column, 24.0)
    row = row - band * 12.0
    column = column - shard * 24.0
    half = div(band, 2.0)
    key = jnp.abs(band - 2.0 * half - core) * 64.0 + message_of(half, shard)
    member = hot(iota((128, PSH), 0) == key)
    upper = hot(iota((128, 128), 0) < iota((128, 128), 1))
    seen = jnp.zeros((128, 1), F32)
    ranks = []
    for b in range(PSH // 128):
        piece = member[:, b * 128 : (b + 1) * 128]
        wide = piece.astype(F32)
        ranks.append(jnp.sum(wide * (dot(piece, upper) + seen), axis=0, keepdims=True))
        seen = seen + jnp.sum(wide, axis=1, keepdims=True)
    target = key * PER + jnp.concatenate(ranks, axis=1)
    for b in range(PSH // 128):
        perm[b * 128 : (b + 1) * 128, :] = hot(iota((128, PSH), 0) + b * 128.0 == target)
        for greet in greetings[b * 7 : (b + 1) * 7]:
            greet()
    j = div(column, 2.0)
    group = div(j, 3.0)
    i = div(row, 2.0)
    sub = 2.0 * (row - 2.0 * i) + column - 2.0 * j
    base = group * 224.0 + sub * 56.0 + (j - 3.0 * group) * 18.0 + i
    high = div(base, 16.0)
    low = base - 16.0 * high
    at = iota((128, PSH), 0)
    return jnp.where(at == 48.0, high, jnp.where(at == 49.0, low, 0.0)).astype(BF)


def encode_tables(kv_ref, query_ref, score_w, spread_w, stat_w, pick):
    c = iota((128, D), 0)
    lane = iota((128, D), 1)
    a = div(c, 16.0)
    q = query_ref[...].astype(F32)
    chosen = jnp.where(a == 0.0, q[0:1], jnp.where(a == 1.0, q[1:2], q[2:3]))
    mine = (c - 16.0 * a == div(lane, 32.0)) & (c < 48.0)
    heads = jnp.where(mine, chosen, 0.0).astype(BF)
    folded = dot_nt(kv_ref[:, :D], heads) * (1.0 / math.sqrt(D // HEADS))
    high = folded.astype(BF)
    score_w[:, 0:128] = high
    score_w[:, 128:256] = (folded - high.astype(F32)).astype(BF)
    s = iota((128, 128), 0)
    t = iota((128, 128), 1)
    t = t - 64.0 * div(t, 64.0)
    for a in range(LATENT):
        spread_w[:, a * D : (a + 1) * D] = hot(c == 16.0 * a + div(lane, 32.0))
        for piece in range(3):
            here = (t >= 16.0 * piece) & (t < 16.0 * piece + 16.0)
            stat_w[piece * 128 : (piece + 1) * 128, a * 128 : (a + 1) * 128] = hot(
                here & (s == 16.0 * a + t - 16.0 * piece)
            )
        stat_w[384:512, a * 128 : (a + 1) * 128] = hot((t >= 48.0) & (t < 50.0) & (s == t))
    lane = iota((1, 6 * CHUNK), 1)
    kind = div(lane, float(CHUNK))
    slot = lane - kind * CHUNK
    stats = kind >= 3.0
    a = jnp.where(stats, kind - 3.0, kind)
    dest = div(slot, float(PER))
    k = a * PER + slot - dest * PER
    row = dest * MSG + jnp.where(stats, 27.0 + div(k, 8.0), k)
    for b in range(4):
        pick[b * 128 : (b + 1) * 128, :] = hot(iota((128, 6 * CHUNK), 0) + b * 128.0 == row)


def encode_chunk(xs, meta, kv_ref, score_w, spread_w, stat_w, pick, stack):
    scores = []
    for x in xs:
        both = dot(x, score_w[...])
        scores.append(both[:, :128] + both[:, 128:])
    peak = functools.reduce(jnp.maximum, scores)
    weights = [jnp.exp(s - peak) for s in scores]
    total = functools.reduce(jnp.add, weights)
    mixes = [jnp.zeros((CHUNK, D), F32)] * LATENT
    for x, w in zip(xs, weights):
        value = dot(x, kv_ref[:, D:]).astype(BF).astype(F32)
        wide = dot((w / total).astype(BF), spread_w[...])
        mixes = [m + wide[:, a * D : (a + 1) * D] * value for a, m in enumerate(mixes)]
    logsum = peak + jnp.log(total)
    high = logsum.astype(BF)
    rest = logsum - high.astype(F32)
    middle = rest.astype(BF)
    low = (rest - middle.astype(F32)).astype(BF)
    stats = dot(jnp.concatenate([high, middle, low, meta], axis=1), stat_w[...])
    slot = iota((CHUNK, D), 0)
    rank = slot - PER * div(slot, float(PER))
    block = div(iota((CHUNK, D), 1), 64.0)
    for a in range(LATENT):
        stack[a * CHUNK : (a + 1) * CHUNK, :] = mixes[a].astype(BF)
        k = rank + PER * a
        tiled = jnp.concatenate([stats[:, a * 128 : (a + 1) * 128]] * 4, axis=1)
        stack[(3 + a) * CHUNK : (4 + a) * CHUNK, :] = jnp.where(
            block == k - 8.0 * div(k, 8.0), tiled, 0.0
        ).astype(BF)
    return dot(pick[...], stack[...]).astype(BF)


def settle_tables(select, mask, fold):
    m = iota((256, 256), 0)
    k = m - MSG * div(m, float(MSG))
    select[...] = hot((k < 27.0) & (iota((256, 256), 1) == m - k + 27.0 + div(k, 8.0)))
    k = iota((256, D), 0)
    k = k - MSG * div(k, float(MSG))
    mask[...] = hot(div(iota((256, D), 1), 64.0) == k - 8.0 * div(k, 8.0))
    lane = iota((D, D), 0)
    lane = lane - 64.0 * div(lane, 64.0)
    fold[:, 0:D] = hot((lane < 48.0) & (lane - 16.0 * div(lane, 16.0) == div(iota((D, D), 1), 32.0)))
    lane = iota((D, 128), 0)
    lane = lane - 64.0 * div(lane, 64.0)
    fold[:, D : D + 128] = jnp.where(lane == 48.0, 16.0, jnp.where(lane == 49.0, 1.0, 0.0)).astype(BF)


def settle_chunk(values, query_ref, out_w_ref, select, mask, fold):
    stats = [(dot(select[...], v) * mask[...].astype(F32)).astype(BF) for v in values]
    logs = [dot(s, fold[:, 0:D]) for s in stats]
    peak = jnp.maximum(logs[0], logs[1])
    weights = [jnp.exp(l - peak) for l in logs]
    mixed = weights[0] * values[0].astype(F32) + weights[1] * values[1].astype(F32)
    encoded = (mixed / (weights[0] + weights[1])).astype(BF)
    q = query_ref[...].astype(F32)
    k = iota((256, D), 0)
    k = k - MSG * div(k, float(MSG))
    bias = jnp.where(k < 9.0, q[0:1], jnp.where(k < 18.0, q[1:2], q[2:3]))
    latents = (dot(encoded, out_w_ref[...]) + bias).astype(BF)
    k = k[:, 0:128]
    place = dot(stats[0], fold[:, D : D + 128]) + 6.0 * div(k, 9.0)
    place = jnp.where(k < 27.0, place, FAR)
    return latents, jnp.transpose(place)[0:8, :]


def level_partials(
    order_ref,
    fields_ref,
    kv_ref,
    query_ref,
    out_w_ref,
    grid,
    links,
    halo,
    weight_loads,
    perm,
    fields,
    outgoing,
    own,
    mate,
    meta,
    score_w,
    spread_w,
    stat_w,
    pick,
    stack,
    messages,
    landed,
    select,
    mask,
    fold,
    latents,
    rows,
    level_load,
    level_send,
    level_recv,
    send_sem,
    recv_sem,
):
    lev = lax.axis_index("lev")
    other = (lev + 1 - 2 * lax.rem(lev, 2), lax.axis_index("win"))
    loads = [
        pltpu.make_async_copy(fields_ref.at[l], fields.at[l], level_load.at[l]) for l in range(3)
    ]
    for load in loads + weight_loads[:7]:
        load.start()
    barrier = pltpu.get_barrier_semaphore()
    pl.semaphore_signal(barrier, inc=1, device_id=other, device_id_type=MESH)
    receivers = Receivers()

    def greeting(i, z, p):
        return lambda: pl.semaphore_signal(
            barrier, inc=1, device_id=receivers.of(i, z, p), device_id_type=MESH
        )

    peers = [(i, z, p) for i in range(4) for z in range(2) for p in range(8)][1:]
    places = sort_slots(order_ref, perm, [greeting(*peer) for peer in peers])
    pl.semaphore_wait(barrier, 64)
    copies = []
    for l in range(3):
        loads[l].wait()
        outgoing[l] = dot(perm[576:, :], fields[l]).astype(BF)
        copies.append(
            pltpu.make_async_remote_copy(
                src_ref=outgoing.at[l],
                dst_ref=mate.at[l],
                send_sem=level_send.at[l],
                recv_sem=level_recv.at[l],
                device_id=other,
                device_id_type=MESH,
            )
        )
        copies[l].start()
    for l in range(3):
        own[l] = dot(perm[:576, :], fields[l]).astype(BF)
    for load in weight_loads[7:]:
        load.start()
    meta[...] = dot_nt(perm[0:576, :], places).astype(BF)
    for load in weight_loads[:2]:
        load.wait()
    encode_tables(kv_ref, query_ref, score_w, spread_w, stat_w, pick)
    for one in copies:
        one.wait()

    def copy(i, z, p):
        j = i * 16 + z * 8 + p
        part = pl.ds(pl.multiple_of(j * MSG, MSG), MSG)
        return pltpu.make_async_remote_copy(
            src_ref=messages.at[part],
            dst_ref=landed.at[part],
            send_sem=send_sem.at[j],
            recv_sem=recv_sem.at[j],
            device_id=receivers.of(i, z, p),
            device_id_type=MESH,
        )

    def sixteen(i, act):
        @pl.when(i > 0)
        def _():
            act(copy(i, 0, 0))

        for t in range(1, 16):
            act(copy(i, t // 8, t % 8))

    @pl.loop(0, 4)
    def _(i):
        part = pl.ds(pl.multiple_of(i * CHUNK, 16), CHUNK)
        xs = [own[l, part, :] for l in range(3)] + [mate[l, part, :] for l in range(3)]
        messages[pl.ds(pl.multiple_of(i * 512, 512), 512), :] = encode_chunk(
            xs, meta[part, :], kv_ref, score_w, spread_w, stat_w, pick, stack
        )
        sixteen(i, lambda one: one.start())

    landed[0:MSG, :] = messages[0:MSG, :]
    settle_tables(select, mask, fold)

    @pl.loop(0, 4)
    def _(i):
        sixteen(i, lambda one: one.wait())
        values = [
            landed[pl.ds(pl.multiple_of(i * 512 + g * 256, 256), 256), :] for g in range(2)
        ]
        done, place = settle_chunk(values, query_ref, out_w_ref, select, mask, fold)
        part = pl.ds(pl.multiple_of(i * 256, 256), 256)
        latents[part, :] = done
        rows[:, part] = place

    where = rows[0:1, :]
    for n, b in enumerate((0, 3, 1, 2)):
        chosen = hot(iota((224, 1024), 0) + 224.0 * b == where)
        grid[b * 224 : (b + 1) * 224, :] = dot(chosen, latents[...]).astype(BF)
        if n == 1:
            for one in links.cells(0, grid, halo):
                one.start()


def partial_scratch():
    levels = pltpu.VMEM((3, 576, D), BF)
    return [
        pltpu.VMEM((PSH, PSH), BF),
        pltpu.VMEM((3, PSH, D), BF),
        levels,
        levels,
        levels,
        pltpu.VMEM((576, 128), BF),
        pltpu.VMEM((D, 256), BF),
        pltpu.VMEM((128, LATENT * D), BF),
        pltpu.VMEM((512, LATENT * 128), BF),
        pltpu.VMEM((16 * MSG, 6 * CHUNK), BF),
        pltpu.VMEM((6 * CHUNK, D), BF),
        pltpu.VMEM((64 * MSG, D), BF),
        pltpu.VMEM((64 * MSG, D), BF),
        pltpu.VMEM((256, 256), BF),
        pltpu.VMEM((256, D), BF),
        pltpu.VMEM((D, D + 128), BF),
        pltpu.VMEM((1024, D), BF),
        pltpu.VMEM((8, 1024), F32),
        pltpu.SemaphoreType.DMA((3,)),
        pltpu.SemaphoreType.DMA((3,)),
        pltpu.SemaphoreType.DMA((3,)),
        pltpu.SemaphoreType.DMA((64,)),
        pltpu.SemaphoreType.DMA((64,)),
    ]


def normalize(values):
    offsets = values - jnp.mean(values, axis=-1, keepdims=True)
    spread = jnp.mean(offsets * offsets, axis=-1, keepdims=True)
    return offsets * lax.rsqrt(spread + epsilon)


def heads_of_group(qkv, out, g, width, valid):
    column = g * 128
    if not isinstance(g, int):
        column = pl.multiple_of(column, 128)
    q = qkv[:, pl.ds(column, 128)]
    k = qkv[:, pl.ds(width + column, 128)]
    v = qkv[:, pl.ds(2 * width + column, 128)]
    v = jnp.concatenate([v * valid, valid], axis=1)
    head = div(iota((1, 128), 1), 32.0)
    queries = jnp.concatenate([q * hot(head == float(h)) for h in range(4)], axis=0)
    scores = dot_nt(queries, k)
    scores = (scores - jnp.max(scores, axis=1, keepdims=True)) * (math.log2(math.e) / math.sqrt(32.0))
    mixed = dot(jnp.exp2(scores).astype(BF), v)
    head = jnp.concatenate([head, head], axis=1)
    total = mixed[0:224]
    for h in range(1, 4):
        total = jnp.where(head == float(h), mixed[h * 224 : (h + 1) * 224], total)
    out[:, pl.ds(column, 128)] = (total[:, :128] / total[:, 128:]).astype(BF)


def valid_keys(slots, valid):
    row = iota((224, 128), 0)
    return hot(row - slots * div(row, float(slots)) < valid)


def shift_starts(s):
    near = s.astype(F32)
    far = jnp.where(s <= 6, s + 12, s - 12).astype(F32)
    return near, far


class Links:
    def __init__(self, send, recv):
        lev = lax.axis_index("lev")
        win = lax.axis_index("win")
        self.send, self.recv = send, recv
        self.sides = (
            (lev, lax.rem(win + N_WIN - 1, N_WIN)),
            (lev, lax.rem(win + 1, N_WIN)),
        )

    def copy(self, side, sem, source, target):
        return pltpu.make_async_remote_copy(
            src_ref=source,
            dst_ref=target,
            send_sem=self.send.at[sem],
            recv_sem=self.recv.at[sem],
            device_id=self.sides[side],
            device_id_type=MESH,
        )

    def cells(self, base, own, halo):
        return (
            self.copy(0, base, own.at[pl.ds(0, 224)], halo.at[pl.ds(224, 224)]),
            self.copy(1, base + 1, own.at[pl.ds(672, 224)], halo.at[pl.ds(0, 224)]),
        )

    def results(self, base, band, results, land):
        first = pl.multiple_of(448 + band * 224, 16)
        return (
            self.copy(
                0,
                base + 2 * band,
                results.at[pl.ds(first, 112)],
                land.at[pl.ds(pl.multiple_of(224 + band * 112, 16), 112)],
            ),
            self.copy(
                1,
                base + 2 * band + 1,
                results.at[pl.ds(pl.multiple_of(first + 112, 16), 112)],
                land.at[pl.ds(pl.multiple_of(band * 112, 16), 112)],
            ),
        )


def shifted_windows(links, base, shift, own, halo, results, land, spread_ref, windows_ref, w_ref, proj_ref, x, qkv, mixed):
    near, far = shift_starts(shift)
    valid = valid_keys(112, 108)

    @pl.loop(0, 4)
    def _(step):
        band = step // 2
        outer = lax.rem((step + 1) // 2, 2)
        rows = pl.ds(pl.multiple_of((outer * 2 + band) * 224, 224), 224)
        target = windows_ref[rows, :] + 36.0 * jnp.where(outer == 0, near, far)
        x[...] = dot(hot(target == spread_ref[:, 0:896]), own[...])

        @pl.when(step == 1)
        def _():
            for copy in links.cells(base, own, halo):
                copy.wait()

        @pl.when(outer == 1)
        def _():
            x[...] += dot(hot(target == spread_ref[:, 896:1344]), halo[...])

        qkv[...] = dot(normalize(x[...]).astype(BF), w_ref[...]).astype(BF)
        for g in range(4):
            heads_of_group(qkv, mixed, g, D, valid)
        results[rows, :] = (x[...] + dot(mixed[...], proj_ref[...])).astype(BF)

        @pl.when(outer == 1)
        def _():
            for copy in links.results(base + 2, band, results, land):
                copy.start()


def held_ids(shift, held_ref):
    near, far = shift_starts(shift)
    return held_ref[0:1, :] + 36.0 * jnp.where(held_ref[1:2, :] > 0.5, near, far)


def step_kernel(shift_ref, order_ref, query_ref, fields_ref, *refs):
    early, late = refs[:7], refs[7:15]
    out_ref = refs[15]
    kv, out_w, spread_ref, windows_ref, held_ref, sub_ref, final_ref = refs[16:23]
    qkv_a_v, proj_a_v, merge_v, qkv_b_v, proj_b_v, expand_v, qkv_c_v, proj_c_v = refs[23:31]
    halo_a, halo_c, land_a, land_c, x, qkv, mixed, qkv_wide, mixed_wide, send, recv, load_sem, grid = refs[31:44]
    encoder = refs[44:]
    fields = encoder[1]
    results, joined, first = (fields.at[l, pl.ds(0, 896)] for l in range(3))
    links = Links(send, recv)
    loads = [
        pltpu.make_async_copy(a, b, load_sem.at[n])
        for n, (a, b) in enumerate(zip(early + late, refs[16:31]))
    ]
    level_partials(
        order_ref, fields_ref, kv, query_ref, out_w, grid, links, halo_a, loads, *encoder
    )
    for load in loads[2:]:
        load.wait()
    shift = shift_ref[0]
    ids = held_ids(shift, held_ref)
    shifted_windows(
        links, 0, shift, grid, halo_a, results, land_a, spread_ref, windows_ref, qkv_a_v, proj_a_v, x, qkv, mixed
    )
    for sub in range(4):
        rows = slice(sub * 224, (sub + 1) * 224)
        first[rows, :] = dot(hot(sub_ref[rows, :] == ids[:, 0:896]), results[...]).astype(BF)
    for band in range(2):
        for copy in links.results(2, band, results, land_a):
            copy.wait()
    total = jnp.zeros((224, 1), F32)
    for sub in range(4):
        rows = slice(sub * 224, (sub + 1) * 224)
        piece = dot(hot(sub_ref[rows, :] == ids[:, 896:1344]), land_a[...])
        piece = piece + first[rows, :].astype(F32)
        first[rows, :] = piece.astype(BF)
        total = total + jnp.sum(piece, axis=1, keepdims=True)
    centre = total * (1.0 / (4 * D))
    spread = jnp.zeros((224, 1), F32)
    for sub in range(4):
        offsets = first[sub * 224 : (sub + 1) * 224, :].astype(F32) - centre
        spread = spread + jnp.sum(offsets * offsets, axis=1, keepdims=True)
    scale = lax.rsqrt(spread * (1.0 / (4 * D)) + epsilon)
    down = jnp.zeros((224, 2 * D), F32)
    for sub in range(4):
        offsets = first[sub * 224 : (sub + 1) * 224, :].astype(F32) - centre
        down = down + dot((offsets * scale).astype(BF), merge_v[sub * D : (sub + 1) * D, :])
    down = down.astype(BF).astype(F32)
    qkv_wide[...] = dot(normalize(down).astype(BF), qkv_b_v[...]).astype(BF)
    valid = valid_keys(56, 54)

    @pl.loop(0, 2)
    def _(step):
        for g in range(4):
            heads_of_group(qkv_wide, mixed_wide, step * 4 + g, 2 * D, valid)

    coarse = (down + dot(mixed_wide[...], proj_b_v[...])).astype(BF).astype(F32)
    normed = normalize(coarse).astype(BF)
    for sub in range(4):
        grown = dot(normed, expand_v[:, sub * D : (sub + 1) * D])
        grown = grown + first[sub * 224 : (sub + 1) * 224, :].astype(F32)
        for g in range(4):
            joined[g * 224 + sub * 56 : g * 224 + (sub + 1) * 56, :] = grown[g * 56 : (g + 1) * 56, :].astype(BF)

    for copy in links.cells(6, joined, halo_c):
        copy.start()
    shift = shift_ref[1]
    shifted_windows(
        links, 6, shift, joined, halo_c, results, land_c, spread_ref, windows_ref, qkv_c_v, proj_c_v, x, qkv, mixed
    )
    ids = held_ids(shift, held_ref)
    for b in range(4):
        rows = slice(b * 216, (b + 1) * 216)
        out_ref[rows, :] = dot(hot(final_ref[rows, :] == ids[:, 0:896]), results[...]).astype(BF)
    for band in range(2):
        for copy in links.results(8, band, results, land_c):
            copy.wait()
    for b in range(4):
        rows = slice(b * 216, (b + 1) * 216)
        piece = dot(hot(final_ref[rows, :] == ids[:, 896:1344]), land_c[...])
        out_ref[rows, :] = (piece + out_ref[rows, :].astype(F32)).astype(BF)


def step(shifts, order, latent_query, fields, held):
    rows = lambda count, width=D: pltpu.VMEM((count, width), BF)
    return pl.pallas_call(
        step_kernel,
        in_specs=[SMEM, VMEM, VMEM] + [ANY] * (1 + len(held)),
        out_specs=VMEM,
        out_shape=jax.ShapeDtypeStruct((PLAT * LATENT * PLON, D), BF),
        scratch_shapes=[pltpu.VMEM(w.shape, w.dtype) for w in held]
        + [rows(448)] * 4
        + [pltpu.VMEM((224, D), F32), rows(224, 3 * D), rows(224), rows(224, 6 * D), rows(224, 2 * D)]
        + [pltpu.SemaphoreType.DMA((12,)), pltpu.SemaphoreType.DMA((12,)), pltpu.SemaphoreType.DMA((15,))]
        + [rows(896)]
        + partial_scratch(),
        compiler_params=params(62, collective_id=0, has_side_effects=True),
        name="step",
    )(shifts, order, latent_query, fields, *held)


def local(
    fields,
    patch_order,
    shift_offsets,
    latent_query,
    enc_kv,
    enc_out,
    qkv_a,
    proj_a,
    merge_w,
    qkv_b,
    proj_b,
    expand_w,
    qkv_c,
    proj_c,
):
    held = (enc_kv, enc_out) + tables()
    held = held + (qkv_a, proj_a, merge_w, qkv_b, proj_b, expand_w, qkv_c, proj_c)
    result = step(shift_offsets, patch_order.reshape(288, 128), latent_query, fields, held)
    return result.reshape(PLAT, LATENT, PLON, D).transpose(0, 2, 1, 3)


def solution(mesh):
    placed = (P("lev", "win", None),) + (P(),) * 13
    return jax.shard_map(
        local, mesh=mesh, in_specs=placed, out_specs=P("lev", "win", None, None), check_vma=False
    )
```

```python
import functools
import math

import jax
import jax.numpy as jnp
import numpy as np
from jax import lax
from jax.experimental import pallas as pl
from jax.experimental.pallas import tpu as pltpu
from jax.sharding import PartitionSpec as P

D = 512
HEADS = 16
LATENT = 3
PLAT = 12
PLON = 24
N_LEV = 4
N_WIN = 32
PSH = 1152
PER = 9
MSG = 32
CHUNK = 144
epsilon = 1e-05
BF = jnp.bfloat16
F32 = jnp.float32
MESH = pl.DeviceIdType.MESH
FAR = -1.0e6
VMEM = pl.BlockSpec(memory_space=pltpu.VMEM)
SMEM = pl.BlockSpec(memory_space=pltpu.SMEM)
ANY = pl.BlockSpec(memory_space=pl.ANY)


def params(mib=60, **more):
    return pltpu.CompilerParams(vmem_limit_bytes=mib << 20, **more)


def dot(a, b):
    return jnp.dot(a, b, preferred_element_type=F32)


def dot_nt(a, b):
    return lax.dot_general(a, b, (((1,), (1,)), ((), ())), preferred_element_type=F32)


def iota(shape, axis):
    return lax.broadcasted_iota(jnp.int32, shape, axis).astype(F32)


def div(values, by):
    return jnp.floor((values + 0.5) * (1.0 / by))


def hot(condition):
    return jnp.where(condition, 1.0, 0.0).astype(BF)


def group_ids(first_column, spare=None):
    ids = np.zeros((4, 28), np.float32)
    for sub in range(4):
        for q in range(28):
            p = min(q, 26)
            column = first_column + 2 * (p // 9) + (sub & 1)
            ids[sub, q] = column * 36 + (2 * (p % 3) + (sub >> 1)) * 3 + p % 9 // 3
    if spare is not None:
        ids[:, 27:] = spare
    return ids


def half_ids(first_column, spare=None):
    ids = np.zeros((112,), np.float32)
    for q in range(112):
        p = min(q, 107)
        ids[q] = (first_column + p // 18) * 36 + p % 6 * 3 + p % 18 // 6
    if spare is not None:
        ids[108:] = spare
    return ids


def tables():
    groups = [group_ids(6 * g, FAR).reshape(-1) for g in range(-1, 5)]
    spread = np.concatenate(groups[1:5] + [groups[0], groups[5]])
    window = np.concatenate([half_ids(0), half_ids(6)])
    held = np.zeros((8, 672), np.float32)
    held[0] = np.concatenate(
        [half_ids(c, FAR) for c in (0, 6, 0, 6, 6 - PLON, PLON)]
    )
    held[1, :224] = 1.0
    by_sub = np.stack([group_ids(6 * g) for g in range(4)], axis=1).reshape(-1)
    final = np.zeros((6, LATENT, PLON), np.float32)
    for r in range(6):
        for a in range(LATENT):
            for c in range(PLON):
                final[r, a, c] = c * 36 + r * 3 + a
    return (
        jnp.asarray(spread[None]),
        jnp.asarray(window[:, None]),
        jnp.asarray(held),
        jnp.asarray(by_sub[:, None]),
        jnp.asarray(final.reshape(-1, 1)),
    )


def place_of_me():
    lev = lax.axis_index("lev")
    win = lax.axis_index("win")
    return lev // 2, win // 8, lax.rem(win // 4, 2), lax.rem(win, 4), lax.rem(lev, 2)


class Receivers:
    def __init__(self):
        half, x, low, self.y, core = place_of_me()
        self.levs = [lax.rem(half + z, 2) * 2 + core for z in range(2)]
        xs = [lax.rem(x + d, 4) * 8 for d in range(4)]
        lows = [lax.rem(low + d, 2) * 4 for d in range(2)]
        self.bases = [xs[p % 4] + lows[p // 4] for p in range(8)]

    def of(self, i, z, p):
        return (self.levs[z], self.bases[p] + lax.rem(self.y + i + p, 4))


def message_of(half, shard):
    my_half, my_x, my_low, my_y, _ = (value.astype(F32) for value in place_of_me())
    x = div(shard, 8.0)
    y = shard - 8.0 * x
    low = div(y, 4.0)
    y = y - 4.0 * low
    x = x - my_x + 4.0
    x = x - 4.0 * div(x, 4.0)
    i = y - my_y - x + 8.0
    i = i - 4.0 * div(i, 4.0)
    return 16.0 * i + 8.0 * jnp.abs(half - my_half) + x + 4.0 * jnp.abs(low - my_low)


def sort_slots(order_ref, perm, greetings):
    win = lax.axis_index("win")
    core = lax.rem(lax.axis_index("lev"), 2).astype(F32)
    p = jnp.concatenate([order_ref[pl.ds(9 * win + r, 1), :] for r in range(9)], axis=1).astype(F32)
    row = div(p, 768.0)
    column = p - row * 768.0
    band = div(row, 12.0)
    shard = div(column, 24.0)
    row = row - band * 12.0
    column = column - shard * 24.0
    half = div(band, 2.0)
    key = jnp.abs(band - 2.0 * half - core) * 64.0 + message_of(half, shard)
    member = hot(iota((128, PSH), 0) == key)
    upper = hot(iota((128, 128), 0) < iota((128, 128), 1))
    seen = jnp.zeros((128, 1), F32)
    ranks = []
    for b in range(PSH // 128):
        piece = member[:, b * 128 : (b + 1) * 128]
        wide = piece.astype(F32)
        ranks.append(jnp.sum(wide * (dot(piece, upper) + seen), axis=0, keepdims=True))
        seen = seen + jnp.sum(wide, axis=1, keepdims=True)
    target = key * PER + jnp.concatenate(ranks, axis=1)
    for b in range(PSH // 128):
        perm[b * 128 : (b + 1) * 128, :] = hot(iota((128, PSH), 0) + b * 128.0 == target)
        for greet in greetings[b * 7 : (b + 1) * 7]:
            greet()
    j = div(column, 2.0)
    group = div(j, 3.0)
    upper = div(row, 6.0)
    row = row - 6.0 * upper
    i = div(row, 2.0)
    sub = 2.0 * (row - 2.0 * i) + column - 2.0 * j
    base = upper * 448.0 + group * 112.0 + sub * 28.0 + (j - 3.0 * group) * 9.0 + i
    high = div(base, 16.0)
    low = base - 16.0 * high
    at = iota((128, PSH), 0)
    return jnp.where(at == 48.0, high, jnp.where(at == 49.0, low, 0.0)).astype(BF)


def encode_tables(kv_ref, query_ref, score_w, spread_w, stat_w, pick):
    c = iota((128, D), 0)
    lane = iota((128, D), 1)
    a = div(c, 16.0)
    q = query_ref[...].astype(F32)
    chosen = jnp.where(a == 0.0, q[0:1], jnp.where(a == 1.0, q[1:2], q[2:3]))
    mine = (c - 16.0 * a == div(lane, 32.0)) & (c < 48.0)
    heads = jnp.where(mine, chosen, 0.0).astype(BF)
    folded = dot_nt(kv_ref[:, :D], heads) * (1.0 / math.sqrt(D // HEADS))
    high = folded.astype(BF)
    score_w[:, 0:128] = high
    score_w[:, 128:256] = (folded - high.astype(F32)).astype(BF)
    s = iota((128, 128), 0)
    t = iota((128, 128), 1)
    t = t - 64.0 * div(t, 64.0)
    for a in range(LATENT):
        spread_w[:, a * D : (a + 1) * D] = hot(c == 16.0 * a + div(lane, 32.0))
        for piece in range(3):
            here = (t >= 16.0 * piece) & (t < 16.0 * piece + 16.0)
            stat_w[piece * 128 : (piece + 1) * 128, a * 128 : (a + 1) * 128] = hot(
                here & (s == 16.0 * a + t - 16.0 * piece)
            )
        stat_w[384:512, a * 128 : (a + 1) * 128] = hot((t >= 48.0) & (t < 50.0) & (s == t))
    lane = iota((1, 6 * CHUNK), 1)
    kind = div(lane, float(CHUNK))
    slot = lane - kind * CHUNK
    stats = kind >= 3.0
    a = jnp.where(stats, kind - 3.0, kind)
    dest = div(slot, float(PER))
    k = a * PER + slot - dest * PER
    row = dest * MSG + jnp.where(stats, 27.0 + div(k, 8.0), k)
    for b in range(4):
        pick[b * 128 : (b + 1) * 128, :] = hot(iota((128, 6 * CHUNK), 0) + b * 128.0 == row)


def encode_chunk(xs, meta, kv_ref, score_w, spread_w, stat_w, pick, stack):
    scores = []
    for x in xs:
        both = dot(x, score_w[...])
        scores.append(both[:, :128] + both[:, 128:])
    peak = functools.reduce(jnp.maximum, scores)
    weights = [jnp.exp(s - peak) for s in scores]
    total = functools.reduce(jnp.add, weights)
    mixes = [jnp.zeros((CHUNK, D), F32)] * LATENT
    for x, w in zip(xs, weights):
        value = dot(x, kv_ref[:, D:]).astype(BF).astype(F32)
        wide = dot((w / total).astype(BF), spread_w[...])
        mixes = [m + wide[:, a * D : (a + 1) * D] * value for a, m in enumerate(mixes)]
    logsum = peak + jnp.log(total)
    high = logsum.astype(BF)
    rest = logsum - high.astype(F32)
    middle = rest.astype(BF)
    low = (rest - middle.astype(F32)).astype(BF)
    stats = dot(jnp.concatenate([high, middle, low, meta], axis=1), stat_w[...])
    slot = iota((CHUNK, D), 0)
    rank = slot - PER * div(slot, float(PER))
    block = div(iota((CHUNK, D), 1), 64.0)
    for a in range(LATENT):
        stack[a * CHUNK : (a + 1) * CHUNK, :] = mixes[a].astype(BF)
        k = rank + PER * a
        tiled = jnp.concatenate([stats[:, a * 128 : (a + 1) * 128]] * 4, axis=1)
        stack[(3 + a) * CHUNK : (4 + a) * CHUNK, :] = jnp.where(
            block == k - 8.0 * div(k, 8.0), tiled, 0.0
        ).astype(BF)
    return dot(pick[...], stack[...]).astype(BF)


def settle_tables(select, mask, fold):
    m = iota((256, 256), 0)
    k = m - MSG * div(m, float(MSG))
    select[...] = hot((k < 27.0) & (iota((256, 256), 1) == m - k + 27.0 + div(k, 8.0)))
    k = iota((256, D), 0)
    k = k - MSG * div(k, float(MSG))
    mask[...] = hot(div(iota((256, D), 1), 64.0) == k - 8.0 * div(k, 8.0))
    lane = iota((D, D), 0)
    lane = lane - 64.0 * div(lane, 64.0)
    fold[:, 0:D] = hot((lane < 48.0) & (lane - 16.0 * div(lane, 16.0) == div(iota((D, D), 1), 32.0)))
    lane = iota((D, 128), 0)
    lane = lane - 64.0 * div(lane, 64.0)
    fold[:, D : D + 128] = jnp.where(lane == 48.0, 16.0, jnp.where(lane == 49.0, 1.0, 0.0)).astype(BF)


def settle_chunk(values, query_ref, out_w_ref, select, mask, fold):
    stats = [(dot(select[...], v) * mask[...].astype(F32)).astype(BF) for v in values]
    logs = [dot(s, fold[:, 0:D]) for s in stats]
    peak = jnp.maximum(logs[0], logs[1])
    weights = [jnp.exp(l - peak) for l in logs]
    mixed = weights[0] * values[0].astype(F32) + weights[1] * values[1].astype(F32)
    encoded = (mixed / (weights[0] + weights[1])).astype(BF)
    q = query_ref[...].astype(F32)
    k = iota((256, D), 0)
    k = k - MSG * div(k, float(MSG))
    bias = jnp.where(k < 9.0, q[0:1], jnp.where(k < 18.0, q[1:2], q[2:3]))
    latents = (dot(encoded, out_w_ref[...]) + bias).astype(BF)
    k = k[:, 0:128]
    place = dot(stats[0], fold[:, D : D + 128]) + 3.0 * div(k, 9.0)
    place = jnp.where(k < 27.0, place, FAR)
    return latents, jnp.transpose(place)[0:8, :]


def level_partials(
    order_ref,
    fields_ref,
    kv_ref,
    query_ref,
    out_w_ref,
    grid,
    links,
    halo,
    weight_loads,
    perm,
    fields,
    outgoing,
    own,
    mate,
    meta,
    score_w,
    spread_w,
    stat_w,
    pick,
    stack,
    messages,
    landed,
    select,
    mask,
    fold,
    latents,
    rows,
    level_load,
    level_send,
    level_recv,
    send_sem,
    recv_sem,
):
    lev = lax.axis_index("lev")
    other = (lev + 1 - 2 * lax.rem(lev, 2), lax.axis_index("win"))
    loads = [
        pltpu.make_async_copy(fields_ref.at[l], fields.at[l], level_load.at[l]) for l in range(3)
    ]
    for load in loads + weight_loads[:7]:
        load.start()
    barrier = pltpu.get_barrier_semaphore()
    pl.semaphore_signal(barrier, inc=1, device_id=other, device_id_type=MESH)
    receivers = Receivers()

    def greeting(i, z, p):
        return lambda: pl.semaphore_signal(
            barrier, inc=1, device_id=receivers.of(i, z, p), device_id_type=MESH
        )

    peers = [(i, z, p) for i in range(4) for z in range(2) for p in range(8)][1:]
    places = sort_slots(order_ref, perm, [greeting(*peer) for peer in peers])
    pl.semaphore_wait(barrier, 64)
    copies = []
    for l in range(3):
        loads[l].wait()
        outgoing[l] = dot(perm[576:, :], fields[l]).astype(BF)
        copies.append(
            pltpu.make_async_remote_copy(
                src_ref=outgoing.at[l],
                dst_ref=mate.at[l],
                send_sem=level_send.at[l],
                recv_sem=level_recv.at[l],
                device_id=other,
                device_id_type=MESH,
            )
        )
        copies[l].start()
    for l in range(3):
        own[l] = dot(perm[:576, :], fields[l]).astype(BF)
    for load in weight_loads[7:]:
        load.start()
    meta[...] = dot_nt(perm[0:576, :], places).astype(BF)
    for load in weight_loads[:2]:
        load.wait()
    encode_tables(kv_ref, query_ref, score_w, spread_w, stat_w, pick)
    for one in copies:
        one.wait()

    def copy(i, z, p):
        j = i * 16 + z * 8 + p
        part = pl.ds(pl.multiple_of(j * MSG, MSG), MSG)
        return pltpu.make_async_remote_copy(
            src_ref=messages.at[part],
            dst_ref=landed.at[part],
            send_sem=send_sem.at[j],
            recv_sem=recv_sem.at[j],
            device_id=receivers.of(i, z, p),
            device_id_type=MESH,
        )

    def sixteen(i, act):
        @pl.when(i > 0)
        def _():
            act(copy(i, 0, 0))

        for t in range(1, 16):
            act(copy(i, t // 8, t % 8))

    @pl.loop(0, 4)
    def _(i):
        part = pl.ds(pl.multiple_of(i * CHUNK, 16), CHUNK)
        xs = [own[l, part, :] for l in range(3)] + [mate[l, part, :] for l in range(3)]
        messages[pl.ds(pl.multiple_of(i * 512, 512), 512), :] = encode_chunk(
            xs, meta[part, :], kv_ref, score_w, spread_w, stat_w, pick, stack
        )
        sixteen(i, lambda one: one.start())

    landed[0:MSG, :] = messages[0:MSG, :]
    settle_tables(select, mask, fold)

    @pl.loop(0, 4)
    def _(i):
        sixteen(i, lambda one: one.wait())
        values = [
            landed[pl.ds(pl.multiple_of(i * 512 + g * 256, 256), 256), :] for g in range(2)
        ]
        done, place = settle_chunk(values, query_ref, out_w_ref, select, mask, fold)
        part = pl.ds(pl.multiple_of(i * 256, 256), 256)
        latents[part, :] = done
        rows[:, part] = place

    where = rows[0:1, :]
    for b in range(4):
        chosen = hot(iota((224, 1024), 0) + 224.0 * b == where)
        grid[b * 224 : (b + 1) * 224, :] = dot(chosen, latents[...]).astype(BF)
        if b % 2 == 1:
            for one in links.cells(0, b // 2, grid, halo):
                one.start()


def partial_scratch():
    levels = pltpu.VMEM((3, 576, D), BF)
    return [
        pltpu.VMEM((PSH, PSH), BF),
        pltpu.VMEM((3, PSH, D), BF),
        levels,
        levels,
        levels,
        pltpu.VMEM((576, 128), BF),
        pltpu.VMEM((D, 256), BF),
        pltpu.VMEM((128, LATENT * D), BF),
        pltpu.VMEM((512, LATENT * 128), BF),
        pltpu.VMEM((16 * MSG, 6 * CHUNK), BF),
        pltpu.VMEM((6 * CHUNK, D), BF),
        pltpu.VMEM((64 * MSG, D), BF),
        pltpu.VMEM((64 * MSG, D), BF),
        pltpu.VMEM((256, 256), BF),
        pltpu.VMEM((256, D), BF),
        pltpu.VMEM((D, D + 128), BF),
        pltpu.VMEM((1024, D), BF),
        pltpu.VMEM((8, 1024), F32),
        pltpu.SemaphoreType.DMA((3,)),
        pltpu.SemaphoreType.DMA((3,)),
        pltpu.SemaphoreType.DMA((3,)),
        pltpu.SemaphoreType.DMA((64,)),
        pltpu.SemaphoreType.DMA((64,)),
    ]


def normalize(values):
    offsets = values - jnp.mean(values, axis=-1, keepdims=True)
    spread = jnp.mean(offsets * offsets, axis=-1, keepdims=True)
    return offsets * lax.rsqrt(spread + epsilon)


def heads_of_group(qkv, out, g, width, valid):
    column = g * 128
    if not isinstance(g, int):
        column = pl.multiple_of(column, 128)
    q = qkv[:, pl.ds(column, 128)]
    k = qkv[:, pl.ds(width + column, 128)]
    v = qkv[:, pl.ds(2 * width + column, 128)]
    v = jnp.concatenate([v * valid, valid], axis=1)
    head = div(iota((1, 128), 1), 32.0)
    queries = jnp.concatenate([q * hot(head == float(h)) for h in range(4)], axis=0)
    scores = dot_nt(queries, k)
    scores = (scores - jnp.max(scores, axis=1, keepdims=True)) * (math.log2(math.e) / math.sqrt(32.0))
    mixed = dot(jnp.exp2(scores).astype(BF), v)
    head = jnp.concatenate([head, head], axis=1)
    total = mixed[0:224]
    for h in range(1, 4):
        total = jnp.where(head == float(h), mixed[h * 224 : (h + 1) * 224], total)
    out[:, pl.ds(column, 128)] = (total[:, :128] / total[:, 128:]).astype(BF)


def valid_keys(slots, valid):
    row = iota((224, 128), 0)
    return hot(row - slots * div(row, float(slots)) < valid)


def shift_starts(s):
    near = s.astype(F32)
    far = jnp.where(s <= 6, s + 12, s - 12).astype(F32)
    return near, far


class Links:
    def __init__(self, send, recv):
        lev = lax.axis_index("lev")
        win = lax.axis_index("win")
        self.send, self.recv = send, recv
        self.sides = (
            (lev, lax.rem(win + N_WIN - 1, N_WIN)),
            (lev, lax.rem(win + 1, N_WIN)),
        )

    def copy(self, side, sem, source, target):
        return pltpu.make_async_remote_copy(
            src_ref=source,
            dst_ref=target,
            send_sem=self.send.at[sem],
            recv_sem=self.recv.at[sem],
            device_id=self.sides[side],
            device_id_type=MESH,
        )

    def pair(self, sem, band, source, to_previous, to_next, target):
        rows = [pl.ds(pl.multiple_of(first, 16), 112) for first in (to_previous, to_next)]
        before = pl.ds(pl.multiple_of(band * 224, 16), 112)
        after = pl.ds(pl.multiple_of(band * 224 + 112, 16), 112)
        return (
            self.copy(0, sem + 2 * band, source.at[rows[0]], target.at[after]),
            self.copy(1, sem + 2 * band + 1, source.at[rows[1]], target.at[before]),
        )

    def cells(self, sem, band, own, halo):
        return self.pair(sem, band, own, band * 448, band * 448 + 336, halo)

    def results(self, sem, band, results, land):
        return self.pair(sem, band, results, band * 448 + 224, band * 448 + 336, land)


def shifted_windows(links, base, shift, own, halo, results, land, spread_ref, window_ref, w_ref, proj_ref, x, qkv, mixed):
    near, far = shift_starts(shift)
    valid = valid_keys(112, 108)

    @pl.loop(0, 4)
    def _(step):
        band = step // 2
        outer = lax.rem((step + 1) // 2, 2)
        cells = pl.ds(pl.multiple_of(band * 448, 448), 448)
        target = window_ref[...] + 36.0 * jnp.where(outer == 0, near, far)
        x[...] = dot(hot(target == spread_ref[:, 0:448]), own[cells, :])

        @pl.when(outer == 1)
        def _():
            for copy in links.cells(base, band, own, halo):
                copy.wait()
            part = pl.ds(pl.multiple_of(band * 224, 224), 224)
            x[...] += dot(hot(target == spread_ref[:, 448:672]), halo[part, :])

        qkv[...] = dot(normalize(x[...]).astype(BF), w_ref[...]).astype(BF)
        for g in range(4):
            heads_of_group(qkv, mixed, g, D, valid)
        rows = pl.ds(pl.multiple_of(band * 448 + outer * 224, 224), 224)
        results[rows, :] = (x[...] + dot(mixed[...], proj_ref[...])).astype(BF)

        @pl.when(outer == 1)
        def _():
            for copy in links.results(base + 4, band, results, land):
                copy.start()


def held_ids(shift, held_ref):
    near, far = shift_starts(shift)
    return held_ref[0:1, :] + 36.0 * jnp.where(held_ref[1:2, :] > 0.5, near, far)


def step_kernel(shift_ref, order_ref, query_ref, fields_ref, *refs):
    early, late = refs[:7], refs[7:15]
    out_ref = refs[15]
    kv, out_w, spread_ref, windows_ref, held_ref, sub_ref, final_ref = refs[16:23]
    qkv_a_v, proj_a_v, merge_v, qkv_b_v, proj_b_v, expand_v, qkv_c_v, proj_c_v = refs[23:31]
    halo_a, halo_c, land_a, land_c, x, qkv, mixed, qkv_wide, mixed_wide, wide, send, recv, load_sem, grid = refs[31:45]
    encoder = refs[45:]
    fields = encoder[1]
    results, joined, first = (fields.at[l, pl.ds(0, 896)] for l in range(3))
    links = Links(send, recv)
    loads = [
        pltpu.make_async_copy(a, b, load_sem.at[n])
        for n, (a, b) in enumerate(zip(early + late, refs[16:31]))
    ]
    level_partials(
        order_ref, fields_ref, kv, query_ref, out_w, grid, links, halo_a, loads, *encoder
    )
    for load in loads[2:]:
        load.wait()
    shift = shift_ref[0]
    ids = held_ids(shift, held_ref)
    shifted_windows(
        links, 0, shift, grid, halo_a, results, land_a, spread_ref, windows_ref, qkv_a_v, proj_a_v, x, qkv, mixed
    )
    for band in range(2):
        own = dot(hot(sub_ref[...] == ids[:, 0:448]), results[band * 448 : (band + 1) * 448, :])
        for sub in range(4):
            first[sub * 224 + band * 112 : sub * 224 + (band + 1) * 112, :] = own[
                sub * 112 : (sub + 1) * 112
            ].astype(BF)
    for band in range(2):
        for copy in links.results(4, band, results, land_a):
            copy.wait()
        got = dot(hot(sub_ref[...] == ids[:, 448:672]), land_a[band * 224 : (band + 1) * 224, :])
        for sub in range(4):
            rows = slice(sub * 224 + band * 112, sub * 224 + (band + 1) * 112)
            first[rows, :] = (got[sub * 112 : (sub + 1) * 112] + first[rows, :].astype(F32)).astype(BF)
    total = jnp.zeros((224, 1), F32)
    for sub in range(4):
        total = total + jnp.sum(
            first[sub * 224 : (sub + 1) * 224, :].astype(F32), axis=1, keepdims=True
        )
    centre = total * (1.0 / (4 * D))
    spread = jnp.zeros((224, 1), F32)
    for sub in range(4):
        offsets = first[sub * 224 : (sub + 1) * 224, :].astype(F32) - centre
        spread = spread + jnp.sum(offsets * offsets, axis=1, keepdims=True)
    scale = lax.rsqrt(spread * (1.0 / (4 * D)) + epsilon)
    down = jnp.zeros((224, 2 * D), F32)
    for sub in range(4):
        offsets = first[sub * 224 : (sub + 1) * 224, :].astype(F32) - centre
        down = down + dot((offsets * scale).astype(BF), merge_v[sub * D : (sub + 1) * D, :])
    down = down.astype(BF).astype(F32)
    qkv_wide[...] = dot(normalize(down).astype(BF), qkv_b_v[...]).astype(BF)
    valid = valid_keys(28, 27)

    @pl.loop(0, 2)
    def _(step):
        for g in range(4):
            heads_of_group(qkv_wide, mixed_wide, step * 4 + g, 2 * D, valid)

    coarse = (down + dot(mixed_wide[...], proj_b_v[...])).astype(BF).astype(F32)
    normed = normalize(coarse).astype(BF)
    for sub in range(4):
        grown = dot(normed, expand_v[:, sub * D : (sub + 1) * D])
        grown = grown + first[sub * 224 : (sub + 1) * 224, :].astype(F32)
        for g in range(8):
            wide[g * 112 + sub * 28 : g * 112 + (sub + 1) * 28, :] = grown[g * 28 : (g + 1) * 28, :]

    for band in range(2):
        rows = slice(band * 448, (band + 1) * 448)
        joined[rows, :] = wide[rows, :].astype(BF)
        for copy in links.cells(8, band, joined, halo_c):
            copy.start()
    shift = shift_ref[1]
    shifted_windows(
        links, 8, shift, joined, halo_c, results, land_c, spread_ref, windows_ref, qkv_c_v, proj_c_v, x, qkv, mixed
    )
    ids = held_ids(shift, held_ref)
    for band in range(2):
        rows = slice(band * 432, (band + 1) * 432)
        out_ref[rows, :] = dot(
            hot(final_ref[...] == ids[:, 0:448]), results[band * 448 : (band + 1) * 448, :]
        ).astype(BF)
    for band in range(2):
        for copy in links.results(12, band, results, land_c):
            copy.wait()
        rows = slice(band * 432, (band + 1) * 432)
        got = dot(hot(final_ref[...] == ids[:, 448:672]), land_c[band * 224 : (band + 1) * 224, :])
        out_ref[rows, :] = (got + out_ref[rows, :].astype(F32)).astype(BF)


def step(shifts, order, latent_query, fields, held):
    rows = lambda count, width=D: pltpu.VMEM((count, width), BF)
    return pl.pallas_call(
        step_kernel,
        in_specs=[SMEM, VMEM, VMEM] + [ANY] * (1 + len(held)),
        out_specs=VMEM,
        out_shape=jax.ShapeDtypeStruct((PLAT * LATENT * PLON, D), BF),
        scratch_shapes=[pltpu.VMEM(w.shape, w.dtype) for w in held]
        + [rows(448)] * 4
        + [pltpu.VMEM((224, D), F32), rows(224, 3 * D), rows(224), rows(224, 6 * D), rows(224, 2 * D)]
        + [pltpu.VMEM((896, D), F32)]
        + [pltpu.SemaphoreType.DMA((16,)), pltpu.SemaphoreType.DMA((16,)), pltpu.SemaphoreType.DMA((15,))]
        + [rows(896)]
        + partial_scratch(),
        compiler_params=params(62, collective_id=0, has_side_effects=True),
        name="step",
    )(shifts, order, latent_query, fields, *held)


def local(
    fields,
    patch_order,
    shift_offsets,
    latent_query,
    enc_kv,
    enc_out,
    qkv_a,
    proj_a,
    merge_w,
    qkv_b,
    proj_b,
    expand_w,
    qkv_c,
    proj_c,
):
    held = (enc_kv, enc_out) + tables()
    held = held + (qkv_a, proj_a, merge_w, qkv_b, proj_b, expand_w, qkv_c, proj_c)
    result = step(shift_offsets, patch_order.reshape(288, 128), latent_query, fields, held)
    return result.reshape(PLAT, LATENT, PLON, D).transpose(0, 2, 1, 3)


def solution(mesh):
    placed = (P("lev", "win", None),) + (P(),) * 13
    return jax.shard_map(
        local, mesh=mesh, in_specs=placed, out_specs=P("lev", "win", None, None), check_vma=False
    )
```

```python
import functools
import math

import jax
import jax.numpy as jnp
import numpy as np
from jax import lax
from jax.experimental import pallas as pl
from jax.experimental.pallas import tpu as pltpu
from jax.sharding import PartitionSpec as P

D = 512
HEADS = 16
LATENT = 3
PLAT = 12
PLON = 24
N_LEV = 4
N_WIN = 32
PSH = 1152
PER = 9
MSG = 32
CHUNK = 144
epsilon = 1e-05
BF = jnp.bfloat16
F32 = jnp.float32
MESH = pl.DeviceIdType.MESH
FAR = -1.0e6
VMEM = pl.BlockSpec(memory_space=pltpu.VMEM)
SMEM = pl.BlockSpec(memory_space=pltpu.SMEM)
ANY = pl.BlockSpec(memory_space=pl.ANY)


def params(mib=60, **more):
    return pltpu.CompilerParams(vmem_limit_bytes=mib << 20, **more)


def dot(a, b):
    return jnp.dot(a, b, preferred_element_type=F32)


def dot_nt(a, b):
    return lax.dot_general(a, b, (((1,), (1,)), ((), ())), preferred_element_type=F32)


def iota(shape, axis):
    return lax.broadcasted_iota(jnp.int32, shape, axis).astype(F32)


def div(values, by):
    return jnp.floor((values + 0.5) * (1.0 / by))


def hot(condition):
    return jnp.where(condition, 1.0, 0.0).astype(BF)


def group_ids(first_column, spare=None):
    ids = np.zeros((4, 28), np.float32)
    for sub in range(4):
        for q in range(28):
            p = min(q, 26)
            column = first_column + 2 * (p // 9) + (sub & 1)
            ids[sub, q] = column * 36 + (2 * (p % 3) + (sub >> 1)) * 3 + p % 9 // 3
    if spare is not None:
        ids[:, 27:] = spare
    return ids


def half_ids(first_column, spare=None):
    ids = np.zeros((112,), np.float32)
    for q in range(112):
        p = min(q, 107)
        ids[q] = (first_column + p // 18) * 36 + p % 6 * 3 + p % 18 // 6
    if spare is not None:
        ids[108:] = spare
    return ids


def tables():
    groups = [group_ids(6 * g, FAR).reshape(-1) for g in range(-1, 5)]
    spread = np.concatenate(groups[1:5] + [groups[0], groups[5]])
    window = np.concatenate([half_ids(0), half_ids(6)])
    held = np.zeros((8, 672), np.float32)
    held[0] = np.concatenate(
        [half_ids(c, FAR) for c in (0, 6, 0, 6, 6 - PLON, PLON)]
    )
    held[1, :224] = 1.0
    by_sub = np.stack([group_ids(6 * g) for g in range(4)], axis=1).reshape(-1)
    final = np.zeros((6, LATENT, PLON), np.float32)
    for r in range(6):
        for a in range(LATENT):
            for c in range(PLON):
                final[r, a, c] = c * 36 + r * 3 + a
    return (
        jnp.asarray(spread[None]),
        jnp.asarray(window[:, None]),
        jnp.asarray(held),
        jnp.asarray(by_sub[:, None]),
        jnp.asarray(final.reshape(-1, 1)),
    )


def place_of_me():
    lev = lax.axis_index("lev")
    win = lax.axis_index("win")
    return lev // 2, win // 8, lax.rem(win // 4, 2), lax.rem(win, 4), lax.rem(lev, 2)


class Receivers:
    def __init__(self):
        half, x, low, self.y, core = place_of_me()
        self.levs = [lax.rem(half + z, 2) * 2 + core for z in range(2)]
        xs = [lax.rem(x + d, 4) * 8 for d in range(4)]
        lows = [lax.rem(low + d, 2) * 4 for d in range(2)]
        self.bases = [xs[p % 4] + lows[p // 4] for p in range(8)]

    def of(self, i, z, p):
        return (self.levs[z], self.bases[p] + lax.rem(self.y + i + p, 4))


def message_of(half, shard):
    my_half, my_x, my_low, my_y, _ = (value.astype(F32) for value in place_of_me())
    x = div(shard, 8.0)
    y = shard - 8.0 * x
    low = div(y, 4.0)
    y = y - 4.0 * low
    x = x - my_x + 4.0
    x = x - 4.0 * div(x, 4.0)
    i = y - my_y - x + 8.0
    i = i - 4.0 * div(i, 4.0)
    return 16.0 * i + 8.0 * jnp.abs(half - my_half) + x + 4.0 * jnp.abs(low - my_low)


def sort_slots(order_ref, perm, greetings):
    win = lax.axis_index("win")
    core = lax.rem(lax.axis_index("lev"), 2).astype(F32)
    p = jnp.concatenate([order_ref[pl.ds(9 * win + r, 1), :] for r in range(9)], axis=1).astype(F32)
    row = div(p, 768.0)
    column = p - row * 768.0
    band = div(row, 12.0)
    shard = div(column, 24.0)
    row = row - band * 12.0
    column = column - shard * 24.0
    half = div(band, 2.0)
    key = jnp.abs(band - 2.0 * half - core) * 64.0 + message_of(half, shard)
    member = hot(iota((128, PSH), 0) == key)
    upper = hot(iota((128, 128), 0) < iota((128, 128), 1))
    seen = jnp.zeros((128, 1), F32)
    ranks = []
    for b in range(PSH // 128):
        piece = member[:, b * 128 : (b + 1) * 128]
        wide = piece.astype(F32)
        ranks.append(jnp.sum(wide * (dot(piece, upper) + seen), axis=0, keepdims=True))
        seen = seen + jnp.sum(wide, axis=1, keepdims=True)
    target = key * PER + jnp.concatenate(ranks, axis=1)
    for b in range(PSH // 128):
        perm[b * 128 : (b + 1) * 128, :] = hot(iota((128, PSH), 0) + b * 128.0 == target)
        for greet in greetings[b * 7 : (b + 1) * 7]:
            greet()
    j = div(column, 2.0)
    group = div(j, 3.0)
    upper = div(row, 6.0)
    row = row - 6.0 * upper
    i = div(row, 2.0)
    sub = 2.0 * (row - 2.0 * i) + column - 2.0 * j
    base = upper * 448.0 + group * 112.0 + sub * 28.0 + (j - 3.0 * group) * 9.0 + i
    high = div(base, 16.0)
    low = base - 16.0 * high
    at = iota((128, PSH), 0)
    return jnp.where(at == 48.0, high, jnp.where(at == 49.0, low, 0.0)).astype(BF)


def encode_tables(kv_ref, query_ref, score_w, spread_w, stat_w, pick):
    c = iota((128, D), 0)
    lane = iota((128, D), 1)
    a = div(c, 16.0)
    q = query_ref[...].astype(F32)
    chosen = jnp.where(a == 0.0, q[0:1], jnp.where(a == 1.0, q[1:2], q[2:3]))
    mine = (c - 16.0 * a == div(lane, 32.0)) & (c < 48.0)
    heads = jnp.where(mine, chosen, 0.0).astype(BF)
    folded = dot_nt(kv_ref[:, :D], heads) * (1.0 / math.sqrt(D // HEADS))
    high = folded.astype(BF)
    score_w[:, 0:128] = high
    score_w[:, 128:256] = (folded - high.astype(F32)).astype(BF)
    s = iota((128, 128), 0)
    t = iota((128, 128), 1)
    t = t - 64.0 * div(t, 64.0)
    for a in range(LATENT):
        spread_w[:, a * D : (a + 1) * D] = hot(c == 16.0 * a + div(lane, 32.0))
        for piece in range(3):
            here = (t >= 16.0 * piece) & (t < 16.0 * piece + 16.0)
            stat_w[piece * 128 : (piece + 1) * 128, a * 128 : (a + 1) * 128] = hot(
                here & (s == 16.0 * a + t - 16.0 * piece)
            )
        stat_w[384:512, a * 128 : (a + 1) * 128] = hot((t >= 48.0) & (t < 50.0) & (s == t))
    lane = iota((1, 6 * CHUNK), 1)
    kind = div(lane, float(CHUNK))
    slot = lane - kind * CHUNK
    stats = kind >= 3.0
    a = jnp.where(stats, kind - 3.0, kind)
    dest = div(slot, float(PER))
    k = a * PER + slot - dest * PER
    row = dest * MSG + jnp.where(stats, 27.0 + div(k, 8.0), k)
    for b in range(4):
        pick[b * 128 : (b + 1) * 128, :] = hot(iota((128, 6 * CHUNK), 0) + b * 128.0 == row)


def encode_chunk(xs, meta, kv_ref, score_w, spread_w, stat_w, pick, stack):
    scores = []
    for x in xs:
        both = dot(x, score_w[...])
        scores.append(both[:, :128] + both[:, 128:])
    peak = functools.reduce(jnp.maximum, scores)
    weights = [jnp.exp(s - peak) for s in scores]
    total = functools.reduce(jnp.add, weights)
    mixes = [jnp.zeros((CHUNK, D), F32)] * LATENT
    for x, w in zip(xs, weights):
        value = dot(x, kv_ref[:, D:]).astype(BF).astype(F32)
        wide = dot((w / total).astype(BF), spread_w[...])
        mixes = [m + wide[:, a * D : (a + 1) * D] * value for a, m in enumerate(mixes)]
    logsum = peak + jnp.log(total)
    high = logsum.astype(BF)
    rest = logsum - high.astype(F32)
    middle = rest.astype(BF)
    low = (rest - middle.astype(F32)).astype(BF)
    stats = dot(jnp.concatenate([high, middle, low, meta], axis=1), stat_w[...])
    slot = iota((CHUNK, D), 0)
    rank = slot - PER * div(slot, float(PER))
    block = div(iota((CHUNK, D), 1), 64.0)
    for a in range(LATENT):
        stack[a * CHUNK : (a + 1) * CHUNK, :] = mixes[a].astype(BF)
        k = rank + PER * a
        tiled = jnp.concatenate([stats[:, a * 128 : (a + 1) * 128]] * 4, axis=1)
        stack[(3 + a) * CHUNK : (4 + a) * CHUNK, :] = jnp.where(
            block == k - 8.0 * div(k, 8.0), tiled, 0.0
        ).astype(BF)
    return dot(pick[...], stack[...]).astype(BF)


def settle_tables(select, mask, fold):
    m = iota((256, 256), 0)
    k = m - MSG * div(m, float(MSG))
    select[...] = hot((k < 27.0) & (iota((256, 256), 1) == m - k + 27.0 + div(k, 8.0)))
    k = iota((256, D), 0)
    k = k - MSG * div(k, float(MSG))
    mask[...] = hot(div(iota((256, D), 1), 64.0) == k - 8.0 * div(k, 8.0))
    lane = iota((D, D), 0)
    lane = lane - 64.0 * div(lane, 64.0)
    fold[:, 0:D] = hot((lane < 48.0) & (lane - 16.0 * div(lane, 16.0) == div(iota((D, D), 1), 32.0)))
    lane = iota((D, 128), 0)
    lane = lane - 64.0 * div(lane, 64.0)
    fold[:, D : D + 128] = jnp.where(lane == 48.0, 16.0, jnp.where(lane == 49.0, 1.0, 0.0)).astype(BF)


def settle_chunk(values, query_ref, out_w_ref, select, mask, fold):
    stats = [(dot(select[...], v) * mask[...].astype(F32)).astype(BF) for v in values]
    logs = [dot(s, fold[:, 0:D]) for s in stats]
    peak = jnp.maximum(logs[0], logs[1])
    weights = [jnp.exp(l - peak) for l in logs]
    mixed = weights[0] * values[0].astype(F32) + weights[1] * values[1].astype(F32)
    encoded = (mixed / (weights[0] + weights[1])).astype(BF)
    q = query_ref[...].astype(F32)
    k = iota((256, D), 0)
    k = k - MSG * div(k, float(MSG))
    bias = jnp.where(k < 9.0, q[0:1], jnp.where(k < 18.0, q[1:2], q[2:3]))
    latents = (dot(encoded, out_w_ref[...]) + bias).astype(BF)
    k = k[:, 0:128]
    place = dot(stats[0], fold[:, D : D + 128]) + 3.0 * div(k, 9.0)
    place = jnp.where(k < 27.0, place, FAR)
    return latents, jnp.transpose(place)[0:8, :]


def level_partials(
    order_ref,
    fields_ref,
    kv_ref,
    query_ref,
    out_w_ref,
    grid,
    links,
    halo,
    weight_loads,
    perm,
    fields,
    outgoing,
    own,
    mate,
    meta,
    score_w,
    spread_w,
    stat_w,
    pick,
    stack,
    messages,
    landed,
    select,
    mask,
    fold,
    latents,
    rows,
    level_load,
    level_send,
    level_recv,
    send_sem,
    recv_sem,
):
    lev = lax.axis_index("lev")
    other = (lev + 1 - 2 * lax.rem(lev, 2), lax.axis_index("win"))
    loads = [
        pltpu.make_async_copy(fields_ref.at[l], fields.at[l], level_load.at[l]) for l in range(3)
    ]
    for load in loads + weight_loads[:7]:
        load.start()
    barrier = pltpu.get_barrier_semaphore()
    pl.semaphore_signal(barrier, inc=1, device_id=other, device_id_type=MESH)
    receivers = Receivers()

    def greeting(i, z, p):
        return lambda: pl.semaphore_signal(
            barrier, inc=1, device_id=receivers.of(i, z, p), device_id_type=MESH
        )

    peers = [(i, z, p) for i in range(4) for z in range(2) for p in range(8)][1:]
    places = sort_slots(order_ref, perm, [greeting(*peer) for peer in peers])
    pl.semaphore_wait(barrier, 64)
    copies = []
    for l in range(3):
        loads[l].wait()
        outgoing[l] = dot(perm[576:, :], fields[l]).astype(BF)
        copies.append(
            pltpu.make_async_remote_copy(
                src_ref=outgoing.at[l],
                dst_ref=mate.at[l],
                send_sem=level_send.at[l],
                recv_sem=level_recv.at[l],
                device_id=other,
                device_id_type=MESH,
            )
        )
        copies[l].start()
    for l in range(3):
        own[l] = dot(perm[:576, :], fields[l]).astype(BF)
    meta[...] = dot_nt(perm[0:576, :], places).astype(BF)
    for load in weight_loads[:2]:
        load.wait()
    encode_tables(kv_ref, query_ref, score_w, spread_w, stat_w, pick)
    for one in copies:
        one.wait()

    def copy(i, z, p):
        j = i * 16 + z * 8 + p
        part = pl.ds(pl.multiple_of(j * MSG, MSG), MSG)
        return pltpu.make_async_remote_copy(
            src_ref=messages.at[part],
            dst_ref=landed.at[part],
            send_sem=send_sem.at[j],
            recv_sem=recv_sem.at[j],
            device_id=receivers.of(i, z, p),
            device_id_type=MESH,
        )

    def sixteen(i, act):
        @pl.when(i > 0)
        def _():
            act(copy(i, 0, 0))

        for t in range(1, 16):
            act(copy(i, t % 2, t // 2))

    @pl.loop(0, 4)
    def _(i):
        part = pl.ds(pl.multiple_of(i * CHUNK, 16), CHUNK)
        xs = [own[l, part, :] for l in range(3)] + [mate[l, part, :] for l in range(3)]
        messages[pl.ds(pl.multiple_of(i * 512, 512), 512), :] = encode_chunk(
            xs, meta[part, :], kv_ref, score_w, spread_w, stat_w, pick, stack
        )
        sixteen(i, lambda one: one.start())

    for load in weight_loads[7:]:
        load.start()
    landed[0:MSG, :] = messages[0:MSG, :]
    settle_tables(select, mask, fold)

    @pl.loop(0, 4)
    def _(i):
        sixteen(i, lambda one: one.wait())
        values = [
            landed[pl.ds(pl.multiple_of(i * 512 + g * 256, 256), 256), :] for g in range(2)
        ]
        done, place = settle_chunk(values, query_ref, out_w_ref, select, mask, fold)
        part = pl.ds(pl.multiple_of(i * 256, 256), 256)
        latents[part, :] = done
        rows[:, part] = place

    where = rows[0:1, :]
    for b in range(4):
        chosen = hot(iota((224, 1024), 0) + 224.0 * b == where)
        grid[b * 224 : (b + 1) * 224, :] = dot(chosen, latents[...]).astype(BF)
        if b % 2 == 1:
            for one in links.cells(0, b // 2, grid, halo):
                one.start()


def partial_scratch():
    levels = pltpu.VMEM((3, 576, D), BF)
    return [
        pltpu.VMEM((PSH, PSH), BF),
        pltpu.VMEM((3, PSH, D), BF),
        levels,
        levels,
        levels,
        pltpu.VMEM((576, 128), BF),
        pltpu.VMEM((D, 256), BF),
        pltpu.VMEM((128, LATENT * D), BF),
        pltpu.VMEM((512, LATENT * 128), BF),
        pltpu.VMEM((16 * MSG, 6 * CHUNK), BF),
        pltpu.VMEM((6 * CHUNK, D), BF),
        pltpu.VMEM((64 * MSG, D), BF),
        pltpu.VMEM((64 * MSG, D), BF),
        pltpu.VMEM((256, 256), BF),
        pltpu.VMEM((256, D), BF),
        pltpu.VMEM((D, D + 128), BF),
        pltpu.VMEM((1024, D), BF),
        pltpu.VMEM((8, 1024), F32),
        pltpu.SemaphoreType.DMA((3,)),
        pltpu.SemaphoreType.DMA((3,)),
        pltpu.SemaphoreType.DMA((3,)),
        pltpu.SemaphoreType.DMA((64,)),
        pltpu.SemaphoreType.DMA((64,)),
    ]


def normalize(values):
    offsets = values - jnp.mean(values, axis=-1, keepdims=True)
    spread = jnp.mean(offsets * offsets, axis=-1, keepdims=True)
    return offsets * lax.rsqrt(spread + epsilon)


def heads_of_group(qkv, out, g, width, valid):
    column = g * 128
    if not isinstance(g, int):
        column = pl.multiple_of(column, 128)
    q = qkv[:, pl.ds(column, 128)]
    k = qkv[:, pl.ds(width + column, 128)]
    v = qkv[:, pl.ds(2 * width + column, 128)]
    v = jnp.concatenate([v * valid, valid], axis=1)
    head = div(iota((1, 128), 1), 32.0)
    queries = jnp.concatenate([q * hot(head == float(h)) for h in range(4)], axis=0)
    scores = dot_nt(queries, k)
    scores = (scores - jnp.max(scores, axis=1, keepdims=True)) * (math.log2(math.e) / math.sqrt(32.0))
    mixed = dot(jnp.exp2(scores).astype(BF), v)
    head = jnp.concatenate([head, head], axis=1)
    total = mixed[0:224]
    for h in range(1, 4):
        total = jnp.where(head == float(h), mixed[h * 224 : (h + 1) * 224], total)
    out[:, pl.ds(column, 128)] = (total[:, :128] / total[:, 128:]).astype(BF)


def valid_keys(slots, valid):
    row = iota((224, 128), 0)
    return hot(row - slots * div(row, float(slots)) < valid)


def shift_starts(s):
    near = s.astype(F32)
    far = jnp.where(s <= 6, s + 12, s - 12).astype(F32)
    return near, far


class Links:
    def __init__(self, send, recv):
        lev = lax.axis_index("lev")
        win = lax.axis_index("win")
        self.send, self.recv = send, recv
        self.sides = (
            (lev, lax.rem(win + N_WIN - 1, N_WIN)),
            (lev, lax.rem(win + 1, N_WIN)),
        )

    def copy(self, side, sem, source, target):
        return pltpu.make_async_remote_copy(
            src_ref=source,
            dst_ref=target,
            send_sem=self.send.at[sem],
            recv_sem=self.recv.at[sem],
            device_id=self.sides[side],
            device_id_type=MESH,
        )

    def pair(self, sem, band, source, to_previous, to_next, target):
        rows = [pl.ds(pl.multiple_of(first, 16), 112) for first in (to_previous, to_next)]
        before = pl.ds(pl.multiple_of(band * 224, 16), 112)
        after = pl.ds(pl.multiple_of(band * 224 + 112, 16), 112)
        return (
            self.copy(0, sem + 2 * band, source.at[rows[0]], target.at[after]),
            self.copy(1, sem + 2 * band + 1, source.at[rows[1]], target.at[before]),
        )

    def cells(self, sem, band, own, halo):
        return self.pair(sem, band, own, band * 448, band * 448 + 336, halo)

    def results(self, sem, band, results, land):
        return self.pair(sem, band, results, band * 448 + 224, band * 448 + 336, land)


def shifted_windows(links, base, shift, own, halo, results, land, spread_ref, window_ref, w_ref, proj_ref, x, qkv, mixed):
    near, far = shift_starts(shift)
    valid = valid_keys(112, 108)

    @pl.loop(0, 4)
    def _(step):
        band = step // 2
        outer = lax.rem((step + 1) // 2, 2)
        cells = pl.ds(pl.multiple_of(band * 448, 448), 448)
        target = window_ref[...] + 36.0 * jnp.where(outer == 0, near, far)
        x[...] = dot(hot(target == spread_ref[:, 0:448]), own[cells, :])

        @pl.when(outer == 1)
        def _():
            for copy in links.cells(base, band, own, halo):
                copy.wait()
            part = pl.ds(pl.multiple_of(band * 224, 224), 224)
            x[...] += dot(hot(target == spread_ref[:, 448:672]), halo[part, :])

        qkv[...] = dot(normalize(x[...]).astype(BF), w_ref[...]).astype(BF)
        for g in range(4):
            heads_of_group(qkv, mixed, g, D, valid)
        rows = pl.ds(pl.multiple_of(band * 448 + outer * 224, 224), 224)
        results[rows, :] = (x[...] + dot(mixed[...], proj_ref[...])).astype(BF)

        @pl.when(outer == 1)
        def _():
            for copy in links.results(base + 4, band, results, land):
                copy.start()


def held_ids(shift, held_ref):
    near, far = shift_starts(shift)
    return held_ref[0:1, :] + 36.0 * jnp.where(held_ref[1:2, :] > 0.5, near, far)


def step_kernel(shift_ref, order_ref, query_ref, fields_ref, *refs):
    early, late = refs[:7], refs[7:15]
    out_ref = refs[15]
    kv, out_w, spread_ref, windows_ref, held_ref, sub_ref, final_ref = refs[16:23]
    qkv_a_v, proj_a_v, merge_v, qkv_b_v, proj_b_v, expand_v, qkv_c_v, proj_c_v = refs[23:31]
    halo_a, halo_c, land_a, land_c, x, qkv, mixed, qkv_wide, mixed_wide, wide, send, recv, load_sem, grid = refs[31:45]
    encoder = refs[45:]
    fields = encoder[1]
    results, joined, first = (fields.at[l, pl.ds(0, 896)] for l in range(3))
    links = Links(send, recv)
    loads = [
        pltpu.make_async_copy(a, b, load_sem.at[n])
        for n, (a, b) in enumerate(zip(early + late, refs[16:31]))
    ]
    level_partials(
        order_ref, fields_ref, kv, query_ref, out_w, grid, links, halo_a, loads, *encoder
    )
    for load in loads[2:]:
        load.wait()
    shift = shift_ref[0]
    ids = held_ids(shift, held_ref)
    shifted_windows(
        links, 0, shift, grid, halo_a, results, land_a, spread_ref, windows_ref, qkv_a_v, proj_a_v, x, qkv, mixed
    )
    for band in range(2):
        own = dot(hot(sub_ref[...] == ids[:, 0:448]), results[band * 448 : (band + 1) * 448, :])
        for sub in range(4):
            first[sub * 224 + band * 112 : sub * 224 + (band + 1) * 112, :] = own[
                sub * 112 : (sub + 1) * 112
            ].astype(BF)
    for band in range(2):
        for copy in links.results(4, band, results, land_a):
            copy.wait()
        got = dot(hot(sub_ref[...] == ids[:, 448:672]), land_a[band * 224 : (band + 1) * 224, :])
        for sub in range(4):
            rows = slice(sub * 224 + band * 112, sub * 224 + (band + 1) * 112)
            first[rows, :] = (got[sub * 112 : (sub + 1) * 112] + first[rows, :].astype(F32)).astype(BF)
    total = jnp.zeros((224, 1), F32)
    for sub in range(4):
        total = total + jnp.sum(
            first[sub * 224 : (sub + 1) * 224, :].astype(F32), axis=1, keepdims=True
        )
    centre = total * (1.0 / (4 * D))
    spread = jnp.zeros((224, 1), F32)
    for sub in range(4):
        offsets = first[sub * 224 : (sub + 1) * 224, :].astype(F32) - centre
        spread = spread + jnp.sum(offsets * offsets, axis=1, keepdims=True)
    scale = lax.rsqrt(spread * (1.0 / (4 * D)) + epsilon)
    down = jnp.zeros((224, 2 * D), F32)
    for sub in range(4):
        offsets = first[sub * 224 : (sub + 1) * 224, :].astype(F32) - centre
        down = down + dot((offsets * scale).astype(BF), merge_v[sub * D : (sub + 1) * D, :])
    down = down.astype(BF).astype(F32)
    qkv_wide[...] = dot(normalize(down).astype(BF), qkv_b_v[...]).astype(BF)
    valid = valid_keys(28, 27)

    @pl.loop(0, 2)
    def _(step):
        for g in range(4):
            heads_of_group(qkv_wide, mixed_wide, step * 4 + g, 2 * D, valid)

    coarse = (down + dot(mixed_wide[...], proj_b_v[...])).astype(BF).astype(F32)
    normed = normalize(coarse).astype(BF)
    for sub in range(4):
        grown = dot(normed, expand_v[:, sub * D : (sub + 1) * D])
        grown = grown + first[sub * 224 : (sub + 1) * 224, :].astype(F32)
        for g in range(8):
            wide[g * 112 + sub * 28 : g * 112 + (sub + 1) * 28, :] = grown[g * 28 : (g + 1) * 28, :]

    for band in range(2):
        rows = slice(band * 448, (band + 1) * 448)
        joined[rows, :] = wide[rows, :].astype(BF)
        for copy in links.cells(8, band, joined, halo_c):
            copy.start()
    shift = shift_ref[1]
    shifted_windows(
        links, 8, shift, joined, halo_c, results, land_c, spread_ref, windows_ref, qkv_c_v, proj_c_v, x, qkv, mixed
    )
    ids = held_ids(shift, held_ref)
    for band in range(2):
        rows = slice(band * 432, (band + 1) * 432)
        out_ref[rows, :] = dot(
            hot(final_ref[...] == ids[:, 0:448]), results[band * 448 : (band + 1) * 448, :]
        ).astype(BF)
    for band in range(2):
        for copy in links.results(12, band, results, land_c):
            copy.wait()
        rows = slice(band * 432, (band + 1) * 432)
        got = dot(hot(final_ref[...] == ids[:, 448:672]), land_c[band * 224 : (band + 1) * 224, :])
        out_ref[rows, :] = (got + out_ref[rows, :].astype(F32)).astype(BF)


def step(shifts, order, latent_query, fields, held):
    rows = lambda count, width=D: pltpu.VMEM((count, width), BF)
    return pl.pallas_call(
        step_kernel,
        in_specs=[SMEM, VMEM, VMEM] + [ANY] * (1 + len(held)),
        out_specs=VMEM,
        out_shape=jax.ShapeDtypeStruct((PLAT * LATENT * PLON, D), BF),
        scratch_shapes=[pltpu.VMEM(w.shape, w.dtype) for w in held]
        + [rows(448)] * 4
        + [pltpu.VMEM((224, D), F32), rows(224, 3 * D), rows(224), rows(224, 6 * D), rows(224, 2 * D)]
        + [pltpu.VMEM((896, D), F32)]
        + [pltpu.SemaphoreType.DMA((16,)), pltpu.SemaphoreType.DMA((16,)), pltpu.SemaphoreType.DMA((15,))]
        + [rows(896)]
        + partial_scratch(),
        compiler_params=params(62, collective_id=0, has_side_effects=True),
        name="step",
    )(shifts, order, latent_query, fields, *held)


def local(
    fields,
    patch_order,
    shift_offsets,
    latent_query,
    enc_kv,
    enc_out,
    qkv_a,
    proj_a,
    merge_w,
    qkv_b,
    proj_b,
    expand_w,
    qkv_c,
    proj_c,
):
    held = (enc_kv, enc_out) + tables()
    held = held + (qkv_a, proj_a, merge_w, qkv_b, proj_b, expand_w, qkv_c, proj_c)
    result = step(shift_offsets, patch_order.reshape(288, 128), latent_query, fields, held)
    return result.reshape(PLAT, LATENT, PLON, D).transpose(0, 2, 1, 3)


def solution(mesh):
    placed = (P("lev", "win", None),) + (P(),) * 13
    return jax.shard_map(
        local, mesh=mesh, in_specs=placed, out_specs=P("lev", "win", None, None), check_vma=False
    )
```

```python
import functools
import math

import jax
import jax.numpy as jnp
import numpy as np
from jax import lax
from jax.experimental import pallas as pl
from jax.experimental.pallas import tpu as pltpu
from jax.sharding import PartitionSpec as P

D = 512
HEADS = 16
LATENT = 3
PLAT = 12
PLON = 24
N_LEV = 4
N_WIN = 32
PSH = 1152
PER = 9
MSG = 32
CHUNK = 144
epsilon = 1e-05
BF = jnp.bfloat16
F32 = jnp.float32
MESH = pl.DeviceIdType.MESH
FAR = -1.0e6
VMEM = pl.BlockSpec(memory_space=pltpu.VMEM)
SMEM = pl.BlockSpec(memory_space=pltpu.SMEM)
ANY = pl.BlockSpec(memory_space=pl.ANY)


def params(mib=60, **more):
    return pltpu.CompilerParams(vmem_limit_bytes=mib << 20, **more)


def dot(a, b):
    return jnp.dot(a, b, preferred_element_type=F32)


def dot_nt(a, b):
    return lax.dot_general(a, b, (((1,), (1,)), ((), ())), preferred_element_type=F32)


def iota(shape, axis):
    return lax.broadcasted_iota(jnp.int32, shape, axis).astype(F32)


def div(values, by):
    return jnp.floor((values + 0.5) * (1.0 / by))


def hot(condition):
    return jnp.where(condition, 1.0, 0.0).astype(BF)


def group_ids(first_column, spare=None):
    ids = np.zeros((4, 28), np.float32)
    for sub in range(4):
        for q in range(28):
            p = min(q, 26)
            column = first_column + 2 * (p // 9) + (sub & 1)
            ids[sub, q] = column * 36 + (2 * (p % 3) + (sub >> 1)) * 3 + p % 9 // 3
    if spare is not None:
        ids[:, 27:] = spare
    return ids


def half_ids(first_column, spare=None):
    ids = np.zeros((112,), np.float32)
    for q in range(112):
        p = min(q, 107)
        ids[q] = (first_column + p // 18) * 36 + p % 6 * 3 + p % 18 // 6
    if spare is not None:
        ids[108:] = spare
    return ids


def tables():
    groups = [group_ids(6 * g, FAR).reshape(-1) for g in range(-1, 5)]
    spread = np.concatenate(groups[1:5] + [groups[0], groups[5]])
    window = np.concatenate([half_ids(0), half_ids(6)])
    held = np.zeros((8, 672), np.float32)
    held[0] = np.concatenate(
        [half_ids(c, FAR) for c in (0, 6, 0, 6, 6 - PLON, PLON)]
    )
    held[1, :224] = 1.0
    by_sub = np.stack([group_ids(6 * g) for g in range(4)], axis=1).reshape(-1)
    final = np.zeros((6, LATENT, PLON), np.float32)
    for r in range(6):
        for a in range(LATENT):
            for c in range(PLON):
                final[r, a, c] = c * 36 + r * 3 + a
    return (
        jnp.asarray(spread[None]),
        jnp.asarray(window[:, None]),
        jnp.asarray(held),
        jnp.asarray(by_sub[:, None]),
        jnp.asarray(final.reshape(-1, 1)),
    )


def place_of_me():
    lev = lax.axis_index("lev")
    win = lax.axis_index("win")
    return lev // 2, win // 8, lax.rem(win // 4, 2), lax.rem(win, 4), lax.rem(lev, 2)


class Receivers:
    def __init__(self):
        half, x, low, self.y, core = place_of_me()
        self.levs = [lax.rem(half + z, 2) * 2 + core for z in range(2)]
        xs = [lax.rem(x + d, 4) * 8 for d in range(4)]
        lows = [lax.rem(low + d, 2) * 4 for d in range(2)]
        self.bases = [xs[p % 4] + lows[p // 4] for p in range(8)]

    def of(self, i, z, p):
        return (self.levs[z], self.bases[p] + lax.rem(self.y + i + p, 4))


def message_of(half, shard):
    my_half, my_x, my_low, my_y, _ = (value.astype(F32) for value in place_of_me())
    x = div(shard, 8.0)
    y = shard - 8.0 * x
    low = div(y, 4.0)
    y = y - 4.0 * low
    x = x - my_x + 4.0
    x = x - 4.0 * div(x, 4.0)
    i = y - my_y - x + 8.0
    i = i - 4.0 * div(i, 4.0)
    return 16.0 * i + 8.0 * jnp.abs(half - my_half) + x + 4.0 * jnp.abs(low - my_low)


def sort_slots(order_ref, perm, greetings):
    win = lax.axis_index("win")
    core = lax.rem(lax.axis_index("lev"), 2).astype(F32)
    p = jnp.concatenate([order_ref[pl.ds(9 * win + r, 1), :] for r in range(9)], axis=1).astype(F32)
    row = div(p, 768.0)
    column = p - row * 768.0
    band = div(row, 12.0)
    shard = div(column, 24.0)
    row = row - band * 12.0
    column = column - shard * 24.0
    half = div(band, 2.0)
    key = jnp.abs(band - 2.0 * half - core) * 64.0 + message_of(half, shard)
    member = hot(iota((128, PSH), 0) == key)
    upper = hot(iota((128, 128), 0) < iota((128, 128), 1))
    seen = jnp.zeros((128, 1), F32)
    ranks = []
    for b in range(PSH // 128):
        piece = member[:, b * 128 : (b + 1) * 128]
        wide = piece.astype(F32)
        ranks.append(jnp.sum(wide * (dot(piece, upper) + seen), axis=0, keepdims=True))
        seen = seen + jnp.sum(wide, axis=1, keepdims=True)
    target = key * PER + jnp.concatenate(ranks, axis=1)
    for b in range(PSH // 128):
        perm[b * 128 : (b + 1) * 128, :] = hot(iota((128, PSH), 0) + b * 128.0 == target)
        for greet in greetings[b * 7 : (b + 1) * 7]:
            greet()
    j = div(column, 2.0)
    group = div(j, 3.0)
    upper = div(row, 6.0)
    row = row - 6.0 * upper
    i = div(row, 2.0)
    sub = 2.0 * (row - 2.0 * i) + column - 2.0 * j
    base = upper * 448.0 + group * 112.0 + sub * 28.0 + (j - 3.0 * group) * 9.0 + i
    high = div(base, 16.0)
    low = base - 16.0 * high
    at = iota((128, PSH), 0)
    return jnp.where(at == 48.0, high, jnp.where(at == 49.0, low, 0.0)).astype(BF)


def encode_tables(kv_ref, query_ref, score_w, spread_w, stat_w, pick):
    c = iota((128, D), 0)
    lane = iota((128, D), 1)
    a = div(c, 16.0)
    q = query_ref[...].astype(F32)
    chosen = jnp.where(a == 0.0, q[0:1], jnp.where(a == 1.0, q[1:2], q[2:3]))
    mine = (c - 16.0 * a == div(lane, 32.0)) & (c < 48.0)
    heads = jnp.where(mine, chosen, 0.0).astype(BF)
    folded = dot_nt(kv_ref[:, :D], heads) * (1.0 / math.sqrt(D // HEADS))
    high = folded.astype(BF)
    score_w[:, 0:128] = high
    score_w[:, 128:256] = (folded - high.astype(F32)).astype(BF)
    s = iota((128, 128), 0)
    t = iota((128, 128), 1)
    t = t - 64.0 * div(t, 64.0)
    for a in range(LATENT):
        spread_w[:, a * D : (a + 1) * D] = hot(c == 16.0 * a + div(lane, 32.0))
        for piece in range(3):
            here = (t >= 16.0 * piece) & (t < 16.0 * piece + 16.0)
            stat_w[piece * 128 : (piece + 1) * 128, a * 128 : (a + 1) * 128] = hot(
                here & (s == 16.0 * a + t - 16.0 * piece)
            )
        stat_w[384:512, a * 128 : (a + 1) * 128] = hot((t >= 48.0) & (t < 50.0) & (s == t))
    lane = iota((1, 6 * CHUNK), 1)
    kind = div(lane, float(CHUNK))
    slot = lane - kind * CHUNK
    stats = kind >= 3.0
    a = jnp.where(stats, kind - 3.0, kind)
    dest = div(slot, float(PER))
    k = a * PER + slot - dest * PER
    row = dest * MSG + jnp.where(stats, 27.0 + div(k, 8.0), k)
    for b in range(4):
        pick[b * 128 : (b + 1) * 128, :] = hot(iota((128, 6 * CHUNK), 0) + b * 128.0 == row)


def encode_chunk(x, meta, kv_ref, score_w, spread_w, stat_w, pick, stack):
    parts = [slice(l * CHUNK, (l + 1) * CHUNK) for l in range(6)]
    both = dot(x, score_w[...])
    both = both[:, :128] + both[:, 128:]
    scores = [both[part] for part in parts]
    peak = functools.reduce(jnp.maximum, scores)
    weights = [jnp.exp(s - peak) for s in scores]
    total = functools.reduce(jnp.add, weights)
    share = jnp.concatenate([(w / total).astype(BF) for w in weights], axis=0)
    value = dot(x, kv_ref[:, D:]).astype(BF).astype(F32)
    mixes = []
    for a in range(LATENT):
        mixed = dot(share, spread_w[:, a * D : (a + 1) * D]) * value
        mixes.append(functools.reduce(jnp.add, [mixed[part] for part in parts]))
    logsum = peak + jnp.log(total)
    high = logsum.astype(BF)
    rest = logsum - high.astype(F32)
    middle = rest.astype(BF)
    low = (rest - middle.astype(F32)).astype(BF)
    stats = dot(jnp.concatenate([high, middle, low, meta], axis=1), stat_w[...])
    slot = iota((CHUNK, D), 0)
    rank = slot - PER * div(slot, float(PER))
    block = div(iota((CHUNK, D), 1), 64.0)
    for a in range(LATENT):
        stack[a * CHUNK : (a + 1) * CHUNK, :] = mixes[a].astype(BF)
        k = rank + PER * a
        tiled = jnp.concatenate([stats[:, a * 128 : (a + 1) * 128]] * 4, axis=1)
        stack[(3 + a) * CHUNK : (4 + a) * CHUNK, :] = jnp.where(
            block == k - 8.0 * div(k, 8.0), tiled, 0.0
        ).astype(BF)
    return dot(pick[...], stack[...]).astype(BF)


def settle_tables(select, mask, fold):
    m = iota((256, 256), 0)
    k = m - MSG * div(m, float(MSG))
    select[...] = hot((k < 27.0) & (iota((256, 256), 1) == m - k + 27.0 + div(k, 8.0)))
    k = iota((256, D), 0)
    k = k - MSG * div(k, float(MSG))
    mask[...] = hot(div(iota((256, D), 1), 64.0) == k - 8.0 * div(k, 8.0))
    lane = iota((D, D), 0)
    lane = lane - 64.0 * div(lane, 64.0)
    fold[:, 0:D] = hot((lane < 48.0) & (lane - 16.0 * div(lane, 16.0) == div(iota((D, D), 1), 32.0)))
    lane = iota((D, 128), 0)
    lane = lane - 64.0 * div(lane, 64.0)
    fold[:, D : D + 128] = jnp.where(lane == 48.0, 16.0, jnp.where(lane == 49.0, 1.0, 0.0)).astype(BF)


def settle_chunk(values, query_ref, out_w_ref, select, mask, fold):
    stats = [(dot(select[...], v) * mask[...].astype(F32)).astype(BF) for v in values]
    logs = [dot(s, fold[:, 0:D]) for s in stats]
    peak = jnp.maximum(logs[0], logs[1])
    weights = [jnp.exp(l - peak) for l in logs]
    mixed = weights[0] * values[0].astype(F32) + weights[1] * values[1].astype(F32)
    encoded = (mixed / (weights[0] + weights[1])).astype(BF)
    q = query_ref[...].astype(F32)
    k = iota((256, D), 0)
    k = k - MSG * div(k, float(MSG))
    bias = jnp.where(k < 9.0, q[0:1], jnp.where(k < 18.0, q[1:2], q[2:3]))
    latents = (dot(encoded, out_w_ref[...]) + bias).astype(BF)
    k = k[:, 0:128]
    place = dot(stats[0], fold[:, D : D + 128]) + 3.0 * div(k, 9.0)
    place = jnp.where(k < 27.0, place, FAR)
    return latents, jnp.transpose(place)[0:8, :]


def level_partials(
    order_ref,
    fields_ref,
    kv_ref,
    query_ref,
    out_w_ref,
    grid,
    links,
    halo,
    weight_loads,
    perm,
    fields,
    outgoing,
    own,
    mate,
    meta,
    score_w,
    spread_w,
    stat_w,
    pick,
    stack,
    messages,
    landed,
    select,
    mask,
    fold,
    latents,
    rows,
    level_load,
    level_send,
    level_recv,
    send_sem,
    recv_sem,
):
    lev = lax.axis_index("lev")
    other = (lev + 1 - 2 * lax.rem(lev, 2), lax.axis_index("win"))
    loads = [
        pltpu.make_async_copy(fields_ref.at[l], fields.at[l], level_load.at[l]) for l in range(3)
    ]
    for load in loads + weight_loads[:7]:
        load.start()
    barrier = pltpu.get_barrier_semaphore()
    pl.semaphore_signal(barrier, inc=1, device_id=other, device_id_type=MESH)
    receivers = Receivers()

    def greeting(i, z, p):
        return lambda: pl.semaphore_signal(
            barrier, inc=1, device_id=receivers.of(i, z, p), device_id_type=MESH
        )

    peers = [(i, z, p) for i in range(4) for z in range(2) for p in range(8)][1:]
    places = sort_slots(order_ref, perm, [greeting(*peer) for peer in peers])
    pl.semaphore_wait(barrier, 64)
    copies = []
    for l in range(3):
        loads[l].wait()
        outgoing[l] = dot(perm[576:, :], fields[l]).astype(BF)
        copies.append(
            pltpu.make_async_remote_copy(
                src_ref=outgoing.at[l],
                dst_ref=mate.at[l],
                send_sem=level_send.at[l],
                recv_sem=level_recv.at[l],
                device_id=other,
                device_id_type=MESH,
            )
        )
        copies[l].start()
    for l in range(3):
        own[l] = dot(perm[:576, :], fields[l]).astype(BF)
    meta[...] = dot_nt(perm[0:576, :], places).astype(BF)
    for load in weight_loads[:2]:
        load.wait()
    encode_tables(kv_ref, query_ref, score_w, spread_w, stat_w, pick)
    for one in copies:
        one.wait()

    def copy(i, z, p):
        j = i * 16 + z * 8 + p
        part = pl.ds(pl.multiple_of(j * MSG, MSG), MSG)
        return pltpu.make_async_remote_copy(
            src_ref=messages.at[part],
            dst_ref=landed.at[part],
            send_sem=send_sem.at[j],
            recv_sem=recv_sem.at[j],
            device_id=receivers.of(i, z, p),
            device_id_type=MESH,
        )

    def sixteen(i, act):
        @pl.when(i > 0)
        def _():
            act(copy(i, 0, 0))

        for t in range(1, 16):
            act(copy(i, t % 2, t // 2))

    @pl.loop(0, 4)
    def _(i):
        part = pl.ds(pl.multiple_of(i * CHUNK, 16), CHUNK)
        x = jnp.concatenate([ref[l, part, :] for ref in (own, mate) for l in range(3)], axis=0)
        messages[pl.ds(pl.multiple_of(i * 512, 512), 512), :] = encode_chunk(
            x, meta[part, :], kv_ref, score_w, spread_w, stat_w, pick, stack
        )
        sixteen(i, lambda one: one.start())

    for load in weight_loads[7:]:
        load.start()
    landed[0:MSG, :] = messages[0:MSG, :]
    settle_tables(select, mask, fold)

    @pl.loop(0, 4)
    def _(i):
        sixteen(i, lambda one: one.wait())
        values = [
            landed[pl.ds(pl.multiple_of(i * 512 + g * 256, 256), 256), :] for g in range(2)
        ]
        done, place = settle_chunk(values, query_ref, out_w_ref, select, mask, fold)
        part = pl.ds(pl.multiple_of(i * 256, 256), 256)
        latents[part, :] = done
        rows[:, part] = place

    where = rows[0:1, :]
    for b in range(4):
        chosen = hot(iota((224, 1024), 0) + 224.0 * b == where)
        grid[b * 224 : (b + 1) * 224, :] = dot(chosen, latents[...]).astype(BF)
        if b % 2 == 1:
            for one in links.cells(0, b // 2, grid, halo):
                one.start()


def partial_scratch():
    levels = pltpu.VMEM((3, 576, D), BF)
    return [
        pltpu.VMEM((PSH, PSH), BF),
        pltpu.VMEM((3, PSH, D), BF),
        levels,
        levels,
        levels,
        pltpu.VMEM((576, 128), BF),
        pltpu.VMEM((D, 256), BF),
        pltpu.VMEM((128, LATENT * D), BF),
        pltpu.VMEM((512, LATENT * 128), BF),
        pltpu.VMEM((16 * MSG, 6 * CHUNK), BF),
        pltpu.VMEM((6 * CHUNK, D), BF),
        pltpu.VMEM((64 * MSG, D), BF),
        pltpu.VMEM((64 * MSG, D), BF),
        pltpu.VMEM((256, 256), BF),
        pltpu.VMEM((256, D), BF),
        pltpu.VMEM((D, D + 128), BF),
        pltpu.VMEM((1024, D), BF),
        pltpu.VMEM((8, 1024), F32),
        pltpu.SemaphoreType.DMA((3,)),
        pltpu.SemaphoreType.DMA((3,)),
        pltpu.SemaphoreType.DMA((3,)),
        pltpu.SemaphoreType.DMA((64,)),
        pltpu.SemaphoreType.DMA((64,)),
    ]


def normalize(values):
    offsets = values - jnp.mean(values, axis=-1, keepdims=True)
    spread = jnp.mean(offsets * offsets, axis=-1, keepdims=True)
    return offsets * lax.rsqrt(spread + epsilon)


def heads_of_group(qkv, out, g, width, valid):
    column = g * 128
    if not isinstance(g, int):
        column = pl.multiple_of(column, 128)
    q = qkv[:, pl.ds(column, 128)]
    k = qkv[:, pl.ds(width + column, 128)]
    v = qkv[:, pl.ds(2 * width + column, 128)]
    v = jnp.concatenate([v * valid, valid], axis=1)
    head = div(iota((1, 128), 1), 32.0)
    queries = jnp.concatenate([q * hot(head == float(h)) for h in range(4)], axis=0)
    scores = dot_nt(queries, k)
    scores = (scores - jnp.max(scores, axis=1, keepdims=True)) * (math.log2(math.e) / math.sqrt(32.0))
    mixed = dot(jnp.exp2(scores).astype(BF), v)
    head = jnp.concatenate([head, head], axis=1)
    total = mixed[0:224]
    for h in range(1, 4):
        total = jnp.where(head == float(h), mixed[h * 224 : (h + 1) * 224], total)
    out[:, pl.ds(column, 128)] = (total[:, :128] / total[:, 128:]).astype(BF)


def valid_keys(slots, valid):
    row = iota((224, 128), 0)
    return hot(row - slots * div(row, float(slots)) < valid)


def shift_starts(s):
    near = s.astype(F32)
    far = jnp.where(s <= 6, s + 12, s - 12).astype(F32)
    return near, far


class Links:
    def __init__(self, send, recv):
        lev = lax.axis_index("lev")
        win = lax.axis_index("win")
        self.send, self.recv = send, recv
        self.sides = (
            (lev, lax.rem(win + N_WIN - 1, N_WIN)),
            (lev, lax.rem(win + 1, N_WIN)),
        )

    def copy(self, side, sem, source, target):
        return pltpu.make_async_remote_copy(
            src_ref=source,
            dst_ref=target,
            send_sem=self.send.at[sem],
            recv_sem=self.recv.at[sem],
            device_id=self.sides[side],
            device_id_type=MESH,
        )

    def pair(self, sem, band, source, to_previous, to_next, target):
        rows = [pl.ds(pl.multiple_of(first, 16), 112) for first in (to_previous, to_next)]
        before = pl.ds(pl.multiple_of(band * 224, 16), 112)
        after = pl.ds(pl.multiple_of(band * 224 + 112, 16), 112)
        return (
            self.copy(0, sem + 2 * band, source.at[rows[0]], target.at[after]),
            self.copy(1, sem + 2 * band + 1, source.at[rows[1]], target.at[before]),
        )

    def cells(self, sem, band, own, halo):
        return self.pair(sem, band, own, band * 448, band * 448 + 336, halo)

    def results(self, sem, band, results, land):
        return self.pair(sem, band, results, band * 448 + 224, band * 448 + 336, land)


def shifted_windows(links, base, shift, own, halo, results, land, spread_ref, window_ref, w_ref, proj_ref, x, qkv, mixed):
    near, far = shift_starts(shift)
    valid = valid_keys(112, 108)

    @pl.loop(0, 4)
    def _(step):
        band = step // 2
        outer = lax.rem((step + 1) // 2, 2)
        cells = pl.ds(pl.multiple_of(band * 448, 448), 448)
        target = window_ref[...] + 36.0 * jnp.where(outer == 0, near, far)
        x[...] = dot(hot(target == spread_ref[:, 0:448]), own[cells, :])

        @pl.when(outer == 1)
        def _():
            for copy in links.cells(base, band, own, halo):
                copy.wait()
            part = pl.ds(pl.multiple_of(band * 224, 224), 224)
            x[...] += dot(hot(target == spread_ref[:, 448:672]), halo[part, :])

        qkv[...] = dot(normalize(x[...]).astype(BF), w_ref[...]).astype(BF)
        for g in range(4):
            heads_of_group(qkv, mixed, g, D, valid)
        rows = pl.ds(pl.multiple_of(band * 448 + outer * 224, 224), 224)
        results[rows, :] = (x[...] + dot(mixed[...], proj_ref[...])).astype(BF)

        @pl.when(outer == 1)
        def _():
            for copy in links.results(base + 4, band, results, land):
                copy.start()


def held_ids(shift, held_ref):
    near, far = shift_starts(shift)
    return held_ref[0:1, :] + 36.0 * jnp.where(held_ref[1:2, :] > 0.5, near, far)


def step_kernel(shift_ref, order_ref, query_ref, fields_ref, *refs):
    early, late = refs[:7], refs[7:15]
    own_ref, got_ref = refs[15:17]
    refs = refs[1:]
    kv, out_w, spread_ref, windows_ref, held_ref, sub_ref, final_ref = refs[16:23]
    qkv_a_v, proj_a_v, merge_v, qkv_b_v, proj_b_v, expand_v, qkv_c_v, proj_c_v = refs[23:31]
    halo_a, halo_c, land_a, land_c, x, qkv, mixed, qkv_wide, mixed_wide, wide, send, recv, load_sem, grid = refs[31:45]
    encoder = refs[45:]
    fields = encoder[1]
    results, joined, first = (fields.at[l, pl.ds(0, 896)] for l in range(3))
    links = Links(send, recv)
    loads = [
        pltpu.make_async_copy(a, b, load_sem.at[n])
        for n, (a, b) in enumerate(zip(early + late, refs[16:31]))
    ]
    level_partials(
        order_ref, fields_ref, kv, query_ref, out_w, grid, links, halo_a, loads, *encoder
    )
    for load in loads[2:]:
        load.wait()
    shift = shift_ref[0]
    ids = held_ids(shift, held_ref)
    shifted_windows(
        links, 0, shift, grid, halo_a, results, land_a, spread_ref, windows_ref, qkv_a_v, proj_a_v, x, qkv, mixed
    )
    for band in range(2):
        own = dot(hot(sub_ref[...] == ids[:, 0:448]), results[band * 448 : (band + 1) * 448, :])
        for sub in range(4):
            first[sub * 224 + band * 112 : sub * 224 + (band + 1) * 112, :] = own[
                sub * 112 : (sub + 1) * 112
            ].astype(BF)
    for band in range(2):
        for copy in links.results(4, band, results, land_a):
            copy.wait()
        got = dot(hot(sub_ref[...] == ids[:, 448:672]), land_a[band * 224 : (band + 1) * 224, :])
        for sub in range(4):
            rows = slice(sub * 224 + band * 112, sub * 224 + (band + 1) * 112)
            first[rows, :] = (got[sub * 112 : (sub + 1) * 112] + first[rows, :].astype(F32)).astype(BF)
    total = jnp.zeros((224, 1), F32)
    for sub in range(4):
        total = total + jnp.sum(
            first[sub * 224 : (sub + 1) * 224, :].astype(F32), axis=1, keepdims=True
        )
    centre = total * (1.0 / (4 * D))
    spread = jnp.zeros((224, 1), F32)
    for sub in range(4):
        offsets = first[sub * 224 : (sub + 1) * 224, :].astype(F32) - centre
        spread = spread + jnp.sum(offsets * offsets, axis=1, keepdims=True)
    scale = lax.rsqrt(spread * (1.0 / (4 * D)) + epsilon)
    down = jnp.zeros((224, 2 * D), F32)
    for sub in range(4):
        offsets = first[sub * 224 : (sub + 1) * 224, :].astype(F32) - centre
        down = down + dot((offsets * scale).astype(BF), merge_v[sub * D : (sub + 1) * D, :])
    down = down.astype(BF).astype(F32)
    qkv_wide[...] = dot(normalize(down).astype(BF), qkv_b_v[...]).astype(BF)
    valid = valid_keys(28, 27)

    @pl.loop(0, 2)
    def _(step):
        for g in range(4):
            heads_of_group(qkv_wide, mixed_wide, step * 4 + g, 2 * D, valid)

    coarse = (down + dot(mixed_wide[...], proj_b_v[...])).astype(BF).astype(F32)
    normed = normalize(coarse).astype(BF)
    for sub in range(4):
        grown = dot(normed, expand_v[:, sub * D : (sub + 1) * D])
        grown = grown + first[sub * 224 : (sub + 1) * 224, :].astype(F32)
        for g in range(8):
            wide[g * 112 + sub * 28 : g * 112 + (sub + 1) * 28, :] = grown[g * 28 : (g + 1) * 28, :]

    for band in range(2):
        rows = slice(band * 448, (band + 1) * 448)
        joined[rows, :] = wide[rows, :].astype(BF)
        for copy in links.cells(8, band, joined, halo_c):
            copy.start()
    shift = shift_ref[1]
    shifted_windows(
        links, 8, shift, joined, halo_c, results, land_c, spread_ref, windows_ref, qkv_c_v, proj_c_v, x, qkv, mixed
    )
    ids = held_ids(shift, held_ref)
    for band in range(2):
        rows = slice(band * 432, (band + 1) * 432)
        own_ref[rows, :] = dot(
            hot(final_ref[...] == ids[:, 0:448]), results[band * 448 : (band + 1) * 448, :]
        ).astype(BF)
    for band in range(2):
        for copy in links.results(12, band, results, land_c):
            copy.wait()
        rows = slice(band * 432, (band + 1) * 432)
        got_ref[rows, :] = dot(
            hot(final_ref[...] == ids[:, 448:672]), land_c[band * 224 : (band + 1) * 224, :]
        ).astype(BF)


def step(shifts, order, latent_query, fields, held):
    rows = lambda count, width=D: pltpu.VMEM((count, width), BF)
    return pl.pallas_call(
        step_kernel,
        in_specs=[SMEM, VMEM, VMEM] + [ANY] * (1 + len(held)),
        out_specs=[VMEM, VMEM],
        out_shape=[jax.ShapeDtypeStruct((PLAT * LATENT * PLON, D), BF)] * 2,
        scratch_shapes=[pltpu.VMEM(w.shape, w.dtype) for w in held]
        + [rows(448)] * 4
        + [pltpu.VMEM((224, D), F32), rows(224, 3 * D), rows(224), rows(224, 6 * D), rows(224, 2 * D)]
        + [pltpu.VMEM((896, D), F32)]
        + [pltpu.SemaphoreType.DMA((16,)), pltpu.SemaphoreType.DMA((16,)), pltpu.SemaphoreType.DMA((15,))]
        + [rows(896)]
        + partial_scratch(),
        compiler_params=params(62, collective_id=0, has_side_effects=True),
        name="step",
    )(shifts, order, latent_query, fields, *held)


def local(
    fields,
    patch_order,
    shift_offsets,
    latent_query,
    enc_kv,
    enc_out,
    qkv_a,
    proj_a,
    merge_w,
    qkv_b,
    proj_b,
    expand_w,
    qkv_c,
    proj_c,
):
    held = (enc_kv, enc_out) + tables()
    held = held + (qkv_a, proj_a, merge_w, qkv_b, proj_b, expand_w, qkv_c, proj_c)
    own, got = step(shift_offsets, patch_order.reshape(288, 128), latent_query, fields, held)
    result = own + got
    return result.reshape(PLAT, LATENT, PLON, D).transpose(0, 2, 1, 3)


def solution(mesh):
    placed = (P("lev", "win", None),) + (P(),) * 13
    return jax.shard_map(
        local, mesh=mesh, in_specs=placed, out_specs=P("lev", "win", None, None), check_vma=False
    )
```

```python
import functools
import math

import jax
import jax.numpy as jnp
import numpy as np
from jax import lax
from jax.experimental import pallas as pl
from jax.experimental.pallas import tpu as pltpu
from jax.sharding import PartitionSpec as P

D = 512
HEADS = 16
LATENT = 3
PLAT = 12
PLON = 24
N_LEV = 4
N_WIN = 32
PSH = 1152
PER = 9
MSG = 32
CHUNK = 144
epsilon = 1e-05
BF = jnp.bfloat16
F32 = jnp.float32
MESH = pl.DeviceIdType.MESH
FAR = -1.0e6
VMEM = pl.BlockSpec(memory_space=pltpu.VMEM)
SMEM = pl.BlockSpec(memory_space=pltpu.SMEM)
ANY = pl.BlockSpec(memory_space=pl.ANY)


def params(mib=60, **more):
    return pltpu.CompilerParams(vmem_limit_bytes=mib << 20, **more)


def dot(a, b):
    return jnp.dot(a, b, preferred_element_type=F32)


def dot_nt(a, b):
    return lax.dot_general(a, b, (((1,), (1,)), ((), ())), preferred_element_type=F32)


def iota(shape, axis):
    return lax.broadcasted_iota(jnp.int32, shape, axis).astype(F32)


def div(values, by):
    return jnp.floor((values + 0.5) * (1.0 / by))


def hot(condition):
    return jnp.where(condition, 1.0, 0.0).astype(BF)


def group_ids(first_column, spare=None):
    ids = np.zeros((4, 28), np.float32)
    for sub in range(4):
        for q in range(28):
            p = min(q, 26)
            column = first_column + 2 * (p // 9) + (sub & 1)
            ids[sub, q] = column * 36 + (2 * (p % 3) + (sub >> 1)) * 3 + p % 9 // 3
    if spare is not None:
        ids[:, 27:] = spare
    return ids


def half_ids(first_column, spare=None):
    ids = np.zeros((112,), np.float32)
    for q in range(112):
        p = min(q, 107)
        ids[q] = (first_column + p // 18) * 36 + p % 6 * 3 + p % 18 // 6
    if spare is not None:
        ids[108:] = spare
    return ids


def tables():
    groups = [group_ids(6 * g, FAR).reshape(-1) for g in range(-1, 5)]
    spread = np.concatenate(groups[1:5] + [groups[0], groups[5]])
    window = np.concatenate([half_ids(0), half_ids(6)])
    held = np.zeros((8, 672), np.float32)
    held[0] = np.concatenate(
        [half_ids(c, FAR) for c in (0, 6, 0, 6, 6 - PLON, PLON)]
    )
    held[1, :224] = 1.0
    by_sub = np.stack([group_ids(6 * g) for g in range(4)], axis=1).reshape(-1)
    final = np.zeros((6, LATENT, PLON), np.float32)
    for r in range(6):
        for a in range(LATENT):
            for c in range(PLON):
                final[r, a, c] = c * 36 + r * 3 + a
    return (
        jnp.asarray(spread[None]),
        jnp.asarray(window[:, None]),
        jnp.asarray(held),
        jnp.asarray(by_sub[:, None]),
        jnp.asarray(final.reshape(-1, 1)),
    )


def place_of_me():
    lev = lax.axis_index("lev")
    win = lax.axis_index("win")
    return lev // 2, win // 8, lax.rem(win // 4, 2), lax.rem(win, 4), lax.rem(lev, 2)


class Receivers:
    def __init__(self):
        half, x, low, self.y, core = place_of_me()
        self.levs = [lax.rem(half + z, 2) * 2 + core for z in range(2)]
        xs = [lax.rem(x + d, 4) * 8 for d in range(4)]
        lows = [lax.rem(low + d, 2) * 4 for d in range(2)]
        self.bases = [xs[p % 4] + lows[p // 4] for p in range(8)]

    def of(self, i, z, p):
        return (self.levs[z], self.bases[p] + lax.rem(self.y + i + p, 4))


def message_of(half, shard):
    my_half, my_x, my_low, my_y, _ = (value.astype(F32) for value in place_of_me())
    x = div(shard, 8.0)
    y = shard - 8.0 * x
    low = div(y, 4.0)
    y = y - 4.0 * low
    x = x - my_x + 4.0
    x = x - 4.0 * div(x, 4.0)
    i = y - my_y - x + 8.0
    i = i - 4.0 * div(i, 4.0)
    return 16.0 * i + 8.0 * jnp.abs(half - my_half) + x + 4.0 * jnp.abs(low - my_low)


def sort_slots(order_ref, perm, greetings):
    win = lax.axis_index("win")
    core = lax.rem(lax.axis_index("lev"), 2).astype(F32)
    p = jnp.concatenate([order_ref[pl.ds(9 * win + r, 1), :] for r in range(9)], axis=1).astype(F32)
    row = div(p, 768.0)
    column = p - row * 768.0
    band = div(row, 12.0)
    shard = div(column, 24.0)
    row = row - band * 12.0
    column = column - shard * 24.0
    half = div(band, 2.0)
    key = jnp.abs(band - 2.0 * half - core) * 64.0 + message_of(half, shard)
    member = hot(iota((128, PSH), 0) == key)
    upper = hot(iota((128, 128), 0) < iota((128, 128), 1))
    seen = jnp.zeros((128, 1), F32)
    ranks = []
    for b in range(PSH // 128):
        piece = member[:, b * 128 : (b + 1) * 128]
        wide = piece.astype(F32)
        ranks.append(jnp.sum(wide * (dot(piece, upper) + seen), axis=0, keepdims=True))
        seen = seen + jnp.sum(wide, axis=1, keepdims=True)
    target = key * PER + jnp.concatenate(ranks, axis=1)
    for b in range(PSH // 128):
        perm[b * 128 : (b + 1) * 128, :] = hot(iota((128, PSH), 0) + b * 128.0 == target)
        for greet in greetings[b * 7 : (b + 1) * 7]:
            greet()
    j = div(column, 2.0)
    group = div(j, 3.0)
    upper = div(row, 6.0)
    row = row - 6.0 * upper
    i = div(row, 2.0)
    sub = 2.0 * (row - 2.0 * i) + column - 2.0 * j
    base = upper * 448.0 + group * 112.0 + sub * 28.0 + (j - 3.0 * group) * 9.0 + i
    high = div(base, 16.0)
    low = base - 16.0 * high
    at = iota((128, PSH), 0)
    return jnp.where(at == 48.0, high, jnp.where(at == 49.0, low, 0.0)).astype(BF)


def encode_tables(kv_ref, query_ref, score_w, spread_w, stat_w, pick):
    c = iota((128, D), 0)
    lane = iota((128, D), 1)
    a = div(c, 16.0)
    q = query_ref[...].astype(F32)
    chosen = jnp.where(a == 0.0, q[0:1], jnp.where(a == 1.0, q[1:2], q[2:3]))
    mine = (c - 16.0 * a == div(lane, 32.0)) & (c < 48.0)
    heads = jnp.where(mine, chosen, 0.0).astype(BF)
    folded = dot_nt(kv_ref[:, :D], heads) * (1.0 / math.sqrt(D // HEADS))
    high = folded.astype(BF)
    score_w[:, 0:128] = high
    score_w[:, 128:256] = (folded - high.astype(F32)).astype(BF)
    s = iota((128, 128), 0)
    t = iota((128, 128), 1)
    t = t - 64.0 * div(t, 64.0)
    for a in range(LATENT):
        spread_w[:, a * D : (a + 1) * D] = hot(c == 16.0 * a + div(lane, 32.0))
        for piece in range(3):
            here = (t >= 16.0 * piece) & (t < 16.0 * piece + 16.0)
            stat_w[piece * 128 : (piece + 1) * 128, a * 128 : (a + 1) * 128] = hot(
                here & (s == 16.0 * a + t - 16.0 * piece)
            )
        stat_w[384:512, a * 128 : (a + 1) * 128] = hot((t >= 48.0) & (t < 50.0) & (s == t))
    lane = iota((1, 6 * CHUNK), 1)
    kind = div(lane, float(CHUNK))
    slot = lane - kind * CHUNK
    stats = kind >= 3.0
    a = jnp.where(stats, kind - 3.0, kind)
    dest = div(slot, float(PER))
    k = a * PER + slot - dest * PER
    row = dest * MSG + jnp.where(stats, 27.0 + div(k, 8.0), k)
    for b in range(4):
        pick[b * 128 : (b + 1) * 128, :] = hot(iota((128, 6 * CHUNK), 0) + b * 128.0 == row)


def encode_chunk(x, meta, kv_ref, score_w, spread_w, stat_w, pick, stack):
    parts = [slice(l * CHUNK, (l + 1) * CHUNK) for l in range(6)]
    both = dot(x, score_w[...])
    both = both[:, :128] + both[:, 128:]
    scores = [both[part] for part in parts]
    peak = functools.reduce(jnp.maximum, scores)
    weights = [jnp.exp(s - peak) for s in scores]
    total = functools.reduce(jnp.add, weights)
    share = jnp.concatenate([(w / total).astype(BF) for w in weights], axis=0)
    value = dot(x, kv_ref[:, D:]).astype(BF).astype(F32)
    mixes = []
    for a in range(LATENT):
        mixed = dot(share, spread_w[:, a * D : (a + 1) * D]) * value
        mixes.append(functools.reduce(jnp.add, [mixed[part] for part in parts]))
    logsum = peak + jnp.log(total)
    high = logsum.astype(BF)
    rest = logsum - high.astype(F32)
    middle = rest.astype(BF)
    low = (rest - middle.astype(F32)).astype(BF)
    stats = dot(jnp.concatenate([high, middle, low, meta], axis=1), stat_w[...])
    slot = iota((CHUNK, D), 0)
    rank = slot - PER * div(slot, float(PER))
    block = div(iota((CHUNK, D), 1), 64.0)
    for a in range(LATENT):
        stack[a * CHUNK : (a + 1) * CHUNK, :] = mixes[a].astype(BF)
        k = rank + PER * a
        tiled = jnp.concatenate([stats[:, a * 128 : (a + 1) * 128]] * 4, axis=1)
        stack[(3 + a) * CHUNK : (4 + a) * CHUNK, :] = jnp.where(
            block == k - 8.0 * div(k, 8.0), tiled, 0.0
        ).astype(BF)
    return dot(pick[...], stack[...]).astype(BF)


def settle_tables(select, mask, fold):
    m = iota((256, 256), 0)
    k = m - MSG * div(m, float(MSG))
    select[...] = hot((k < 27.0) & (iota((256, 256), 1) == m - k + 27.0 + div(k, 8.0)))
    k = iota((256, D), 0)
    k = k - MSG * div(k, float(MSG))
    mask[...] = hot(div(iota((256, D), 1), 64.0) == k - 8.0 * div(k, 8.0))
    lane = iota((D, D), 0)
    lane = lane - 64.0 * div(lane, 64.0)
    fold[:, 0:D] = hot((lane < 48.0) & (lane - 16.0 * div(lane, 16.0) == div(iota((D, D), 1), 32.0)))
    lane = iota((D, 128), 0)
    lane = lane - 64.0 * div(lane, 64.0)
    fold[:, D : D + 128] = jnp.where(lane == 48.0, 16.0, jnp.where(lane == 49.0, 1.0, 0.0)).astype(BF)


def settle_chunk(values, query_ref, out_w_ref, select, mask, fold):
    stats = [(dot(select[...], v) * mask[...].astype(F32)).astype(BF) for v in values]
    logs = [dot(s, fold[:, 0:D]) for s in stats]
    peak = jnp.maximum(logs[0], logs[1])
    weights = [jnp.exp(l - peak) for l in logs]
    mixed = weights[0] * values[0].astype(F32) + weights[1] * values[1].astype(F32)
    encoded = (mixed / (weights[0] + weights[1])).astype(BF)
    q = query_ref[...].astype(F32)
    k = iota((256, D), 0)
    k = k - MSG * div(k, float(MSG))
    bias = jnp.where(k < 9.0, q[0:1], jnp.where(k < 18.0, q[1:2], q[2:3]))
    latents = (dot(encoded, out_w_ref[...]) + bias).astype(BF)
    k = k[:, 0:128]
    place = dot(stats[0], fold[:, D : D + 128]) + 3.0 * div(k, 9.0)
    place = jnp.where(k < 27.0, place, FAR)
    return latents, jnp.transpose(place)[0:8, :]


def level_partials(
    order_ref,
    fields_ref,
    kv_ref,
    query_ref,
    out_w_ref,
    grid,
    links,
    halo,
    weight_loads,
    perm,
    fields,
    outgoing,
    own,
    mate,
    meta,
    score_w,
    spread_w,
    stat_w,
    pick,
    stack,
    messages,
    landed,
    select,
    mask,
    fold,
    latents,
    rows,
    level_load,
    level_send,
    level_recv,
    send_sem,
    recv_sem,
):
    lev = lax.axis_index("lev")
    other = (lev + 1 - 2 * lax.rem(lev, 2), lax.axis_index("win"))
    loads = [
        pltpu.make_async_copy(fields_ref.at[l], fields.at[l], level_load.at[l]) for l in range(3)
    ]
    for load in loads + weight_loads[:7]:
        load.start()
    barrier = pltpu.get_barrier_semaphore()
    pl.semaphore_signal(barrier, inc=1, device_id=other, device_id_type=MESH)
    receivers = Receivers()

    def greeting(i, z, p):
        return lambda: pl.semaphore_signal(
            barrier, inc=1, device_id=receivers.of(i, z, p), device_id_type=MESH
        )

    peers = [(i, z, p) for i in range(4) for z in range(2) for p in range(8)][1:]
    places = sort_slots(order_ref, perm, [greeting(*peer) for peer in peers])
    for load in weight_loads[:2]:
        load.wait()
    encode_tables(kv_ref, query_ref, score_w, spread_w, stat_w, pick)
    settle_tables(select, mask, fold)
    pl.semaphore_wait(barrier, 64)
    copies = []
    for l in range(3):
        loads[l].wait()
        outgoing[l] = dot(perm[576:, :], fields[l]).astype(BF)
        copies.append(
            pltpu.make_async_remote_copy(
                src_ref=outgoing.at[l],
                dst_ref=mate.at[l],
                send_sem=level_send.at[l],
                recv_sem=level_recv.at[l],
                device_id=other,
                device_id_type=MESH,
            )
        )
        copies[l].start()
    for l in range(3):
        own[l] = dot(perm[:576, :], fields[l]).astype(BF)
    meta[...] = dot_nt(perm[0:576, :], places).astype(BF)
    for one in copies:
        one.wait()

    def copy(i, z, p):
        j = i * 16 + z * 8 + p
        part = pl.ds(pl.multiple_of(j * MSG, MSG), MSG)
        return pltpu.make_async_remote_copy(
            src_ref=messages.at[part],
            dst_ref=landed.at[part],
            send_sem=send_sem.at[j],
            recv_sem=recv_sem.at[j],
            device_id=receivers.of(i, z, p),
            device_id_type=MESH,
        )

    def sixteen(i, act):
        @pl.when(i > 0)
        def _():
            act(copy(i, 0, 0))

        for t in range(1, 16):
            act(copy(i, t % 2, t // 2))

    @pl.loop(0, 4)
    def _(i):
        part = pl.ds(pl.multiple_of(i * CHUNK, 16), CHUNK)
        x = jnp.concatenate([ref[l, part, :] for ref in (own, mate) for l in range(3)], axis=0)
        messages[pl.ds(pl.multiple_of(i * 512, 512), 512), :] = encode_chunk(
            x, meta[part, :], kv_ref, score_w, spread_w, stat_w, pick, stack
        )
        sixteen(i, lambda one: one.start())

    for load in weight_loads[7:]:
        load.start()
    landed[0:MSG, :] = messages[0:MSG, :]

    @pl.loop(0, 4)
    def _(i):
        sixteen(i, lambda one: one.wait())
        values = [
            landed[pl.ds(pl.multiple_of(i * 512 + g * 256, 256), 256), :] for g in range(2)
        ]
        done, place = settle_chunk(values, query_ref, out_w_ref, select, mask, fold)
        part = pl.ds(pl.multiple_of(i * 256, 256), 256)
        latents[part, :] = done
        rows[:, part] = place

    where = rows[0:1, :]
    for b in range(4):
        chosen = hot(iota((224, 1024), 0) + 224.0 * b == where)
        grid[b * 224 : (b + 1) * 224, :] = dot(chosen, latents[...]).astype(BF)
        if b % 2 == 1:
            for one in links.cells(0, b // 2, grid, halo):
                one.start()


def partial_scratch():
    levels = pltpu.VMEM((3, 576, D), BF)
    return [
        pltpu.VMEM((PSH, PSH), BF),
        pltpu.VMEM((3, PSH, D), BF),
        levels,
        levels,
        levels,
        pltpu.VMEM((576, 128), BF),
        pltpu.VMEM((D, 256), BF),
        pltpu.VMEM((128, LATENT * D), BF),
        pltpu.VMEM((512, LATENT * 128), BF),
        pltpu.VMEM((16 * MSG, 6 * CHUNK), BF),
        pltpu.VMEM((6 * CHUNK, D), BF),
        pltpu.VMEM((64 * MSG, D), BF),
        pltpu.VMEM((64 * MSG, D), BF),
        pltpu.VMEM((256, 256), BF),
        pltpu.VMEM((256, D), BF),
        pltpu.VMEM((D, D + 128), BF),
        pltpu.VMEM((1024, D), BF),
        pltpu.VMEM((8, 1024), F32),
        pltpu.SemaphoreType.DMA((3,)),
        pltpu.SemaphoreType.DMA((3,)),
        pltpu.SemaphoreType.DMA((3,)),
        pltpu.SemaphoreType.DMA((64,)),
        pltpu.SemaphoreType.DMA((64,)),
    ]


def normalize(values):
    offsets = values - jnp.mean(values, axis=-1, keepdims=True)
    spread = jnp.mean(offsets * offsets, axis=-1, keepdims=True)
    return offsets * lax.rsqrt(spread + epsilon)


def heads_of_group(qkv, out, g, width, valid):
    column = g * 128
    if not isinstance(g, int):
        column = pl.multiple_of(column, 128)
    q = qkv[:, pl.ds(column, 128)]
    k = qkv[:, pl.ds(width + column, 128)]
    v = qkv[:, pl.ds(2 * width + column, 128)]
    v = jnp.concatenate([v * valid, valid], axis=1)
    head = div(iota((1, 128), 1), 32.0)
    queries = jnp.concatenate([q * hot(head == float(h)) for h in range(4)], axis=0)
    scores = dot_nt(queries, k)
    scores = (scores - jnp.max(scores, axis=1, keepdims=True)) * (math.log2(math.e) / math.sqrt(32.0))
    mixed = dot(jnp.exp2(scores).astype(BF), v)
    head = jnp.concatenate([head, head], axis=1)
    total = mixed[0:224]
    for h in range(1, 4):
        total = jnp.where(head == float(h), mixed[h * 224 : (h + 1) * 224], total)
    out[:, pl.ds(column, 128)] = (total[:, :128] / total[:, 128:]).astype(BF)


def valid_keys(slots, valid):
    row = iota((224, 128), 0)
    return hot(row - slots * div(row, float(slots)) < valid)


def shift_starts(s):
    near = s.astype(F32)
    far = jnp.where(s <= 6, s + 12, s - 12).astype(F32)
    return near, far


class Links:
    def __init__(self, send, recv):
        lev = lax.axis_index("lev")
        win = lax.axis_index("win")
        self.send, self.recv = send, recv
        self.sides = (
            (lev, lax.rem(win + N_WIN - 1, N_WIN)),
            (lev, lax.rem(win + 1, N_WIN)),
        )

    def copy(self, side, sem, source, target):
        return pltpu.make_async_remote_copy(
            src_ref=source,
            dst_ref=target,
            send_sem=self.send.at[sem],
            recv_sem=self.recv.at[sem],
            device_id=self.sides[side],
            device_id_type=MESH,
        )

    def pair(self, sem, band, source, to_previous, to_next, target):
        rows = [pl.ds(pl.multiple_of(first, 16), 112) for first in (to_previous, to_next)]
        before = pl.ds(pl.multiple_of(band * 224, 16), 112)
        after = pl.ds(pl.multiple_of(band * 224 + 112, 16), 112)
        return (
            self.copy(0, sem + 2 * band, source.at[rows[0]], target.at[after]),
            self.copy(1, sem + 2 * band + 1, source.at[rows[1]], target.at[before]),
        )

    def cells(self, sem, band, own, halo):
        return self.pair(sem, band, own, band * 448, band * 448 + 336, halo)

    def results(self, sem, band, results, land):
        return self.pair(sem, band, results, band * 448 + 224, band * 448 + 336, land)


def shifted_windows(links, base, shift, own, halo, results, land, spread_ref, window_ref, w_ref, proj_ref, x, qkv, mixed):
    near, far = shift_starts(shift)
    valid = valid_keys(112, 108)

    @pl.loop(0, 4)
    def _(step):
        band = step // 2
        outer = lax.rem((step + 1) // 2, 2)
        cells = pl.ds(pl.multiple_of(band * 448, 448), 448)
        target = window_ref[...] + 36.0 * jnp.where(outer == 0, near, far)
        x[...] = dot(hot(target == spread_ref[:, 0:448]), own[cells, :])

        @pl.when(outer == 1)
        def _():
            for copy in links.cells(base, band, own, halo):
                copy.wait()
            part = pl.ds(pl.multiple_of(band * 224, 224), 224)
            x[...] += dot(hot(target == spread_ref[:, 448:672]), halo[part, :])

        qkv[...] = dot(normalize(x[...]).astype(BF), w_ref[...]).astype(BF)
        for g in range(4):
            heads_of_group(qkv, mixed, g, D, valid)
        rows = pl.ds(pl.multiple_of(band * 448 + outer * 224, 224), 224)
        results[rows, :] = (x[...] + dot(mixed[...], proj_ref[...])).astype(BF)

        @pl.when(outer == 1)
        def _():
            for copy in links.results(base + 4, band, results, land):
                copy.start()


def held_ids(shift, held_ref):
    near, far = shift_starts(shift)
    return held_ref[0:1, :] + 36.0 * jnp.where(held_ref[1:2, :] > 0.5, near, far)


def step_kernel(shift_ref, order_ref, query_ref, fields_ref, *refs):
    early, late = refs[:7], refs[7:15]
    out_ref = refs[15]
    kv, out_w, spread_ref, windows_ref, held_ref, sub_ref, final_ref = refs[16:23]
    qkv_a_v, proj_a_v, merge_v, qkv_b_v, proj_b_v, expand_v, qkv_c_v, proj_c_v = refs[23:31]
    halo_a, halo_c, land_a, land_c, x, qkv, mixed, qkv_wide, mixed_wide, wide, send, recv, load_sem, grid = refs[31:45]
    encoder = refs[45:]
    fields = encoder[1]
    results, joined, first = (fields.at[l, pl.ds(0, 896)] for l in range(3))
    links = Links(send, recv)
    loads = [
        pltpu.make_async_copy(a, b, load_sem.at[n])
        for n, (a, b) in enumerate(zip(early + late, refs[16:31]))
    ]
    level_partials(
        order_ref, fields_ref, kv, query_ref, out_w, grid, links, halo_a, loads, *encoder
    )
    for load in loads[2:]:
        load.wait()
    shift = shift_ref[0]
    ids = held_ids(shift, held_ref)
    shifted_windows(
        links, 0, shift, grid, halo_a, results, land_a, spread_ref, windows_ref, qkv_a_v, proj_a_v, x, qkv, mixed
    )
    for band in range(2):
        own = dot(hot(sub_ref[...] == ids[:, 0:448]), results[band * 448 : (band + 1) * 448, :])
        for sub in range(4):
            first[sub * 224 + band * 112 : sub * 224 + (band + 1) * 112, :] = own[
                sub * 112 : (sub + 1) * 112
            ].astype(BF)
    for band in range(2):
        for copy in links.results(4, band, results, land_a):
            copy.wait()
        got = dot(hot(sub_ref[...] == ids[:, 448:672]), land_a[band * 224 : (band + 1) * 224, :])
        for sub in range(4):
            rows = slice(sub * 224 + band * 112, sub * 224 + (band + 1) * 112)
            first[rows, :] = (got[sub * 112 : (sub + 1) * 112] + first[rows, :].astype(F32)).astype(BF)
    total = jnp.zeros((224, 1), F32)
    for sub in range(4):
        total = total + jnp.sum(
            first[sub * 224 : (sub + 1) * 224, :].astype(F32), axis=1, keepdims=True
        )
    centre = total * (1.0 / (4 * D))
    spread = jnp.zeros((224, 1), F32)
    for sub in range(4):
        offsets = first[sub * 224 : (sub + 1) * 224, :].astype(F32) - centre
        spread = spread + jnp.sum(offsets * offsets, axis=1, keepdims=True)
    scale = lax.rsqrt(spread * (1.0 / (4 * D)) + epsilon)
    down = jnp.zeros((224, 2 * D), F32)
    for sub in range(4):
        offsets = first[sub * 224 : (sub + 1) * 224, :].astype(F32) - centre
        down = down + dot((offsets * scale).astype(BF), merge_v[sub * D : (sub + 1) * D, :])
    down = down.astype(BF).astype(F32)
    qkv_wide[...] = dot(normalize(down).astype(BF), qkv_b_v[...]).astype(BF)
    valid = valid_keys(28, 27)

    @pl.loop(0, 2)
    def _(step):
        for g in range(4):
            heads_of_group(qkv_wide, mixed_wide, step * 4 + g, 2 * D, valid)

    coarse = (down + dot(mixed_wide[...], proj_b_v[...])).astype(BF).astype(F32)
    normed = normalize(coarse).astype(BF)
    for sub in range(4):
        grown = dot(normed, expand_v[:, sub * D : (sub + 1) * D])
        grown = grown + first[sub * 224 : (sub + 1) * 224, :].astype(F32)
        for g in range(8):
            wide[g * 112 + sub * 28 : g * 112 + (sub + 1) * 28, :] = grown[g * 28 : (g + 1) * 28, :]

    for band in range(2):
        rows = slice(band * 448, (band + 1) * 448)
        joined[rows, :] = wide[rows, :].astype(BF)
        for copy in links.cells(8, band, joined, halo_c):
            copy.start()
    shift = shift_ref[1]
    shifted_windows(
        links, 8, shift, joined, halo_c, results, land_c, spread_ref, windows_ref, qkv_c_v, proj_c_v, x, qkv, mixed
    )
    ids = held_ids(shift, held_ref)
    for band in range(2):
        rows = slice(band * 432, (band + 1) * 432)
        out_ref[rows, :] = dot(
            hot(final_ref[...] == ids[:, 0:448]), results[band * 448 : (band + 1) * 448, :]
        ).astype(BF)
    for band in range(2):
        for copy in links.results(12, band, results, land_c):
            copy.wait()
        rows = slice(band * 432, (band + 1) * 432)
        got = dot(hot(final_ref[...] == ids[:, 448:672]), land_c[band * 224 : (band + 1) * 224, :])
        out_ref[rows, :] = (got + out_ref[rows, :].astype(F32)).astype(BF)


def step(shifts, order, latent_query, fields, held):
    rows = lambda count, width=D: pltpu.VMEM((count, width), BF)
    return pl.pallas_call(
        step_kernel,
        in_specs=[SMEM, VMEM, VMEM] + [ANY] * (1 + len(held)),
        out_specs=VMEM,
        out_shape=jax.ShapeDtypeStruct((PLAT * LATENT * PLON, D), BF),
        scratch_shapes=[pltpu.VMEM(w.shape, w.dtype) for w in held]
        + [rows(448)] * 4
        + [pltpu.VMEM((224, D), F32), rows(224, 3 * D), rows(224), rows(224, 6 * D), rows(224, 2 * D)]
        + [pltpu.VMEM((896, D), F32)]
        + [pltpu.SemaphoreType.DMA((16,)), pltpu.SemaphoreType.DMA((16,)), pltpu.SemaphoreType.DMA((15,))]
        + [rows(896)]
        + partial_scratch(),
        compiler_params=params(62, collective_id=0, has_side_effects=True),
        name="step",
    )(shifts, order, latent_query, fields, *held)


def local(
    fields,
    patch_order,
    shift_offsets,
    latent_query,
    enc_kv,
    enc_out,
    qkv_a,
    proj_a,
    merge_w,
    qkv_b,
    proj_b,
    expand_w,
    qkv_c,
    proj_c,
):
    held = (enc_kv, enc_out) + tables()
    held = held + (qkv_a, proj_a, merge_w, qkv_b, proj_b, expand_w, qkv_c, proj_c)
    result = step(shift_offsets, patch_order.reshape(288, 128), latent_query, fields, held)
    return result.reshape(PLAT, LATENT, PLON, D).transpose(0, 2, 1, 3)


def solution(mesh):
    placed = (P("lev", "win", None),) + (P(),) * 13
    return jax.shard_map(
        local, mesh=mesh, in_specs=placed, out_specs=P("lev", "win", None, None), check_vma=False
    )
```
